128 devices in a mesh: req: 8 (over y, core), hid: 16 (over x, z).
Axes of the slice: x: 4, y: 4, z: 4, core: 2. Of those that a mesh axis runs over, the one named last changes fastest.
Arguments:
- merged: bfloat16 [8, 256, 12800], P(None, 'req', 'hid')
- ln_gain: bfloat16 [12800], replicated, may hold values from 0.25 to 1.75
- ln_bias: bfloat16 [12800], replicated, may hold values from -3 to 3
- proj_weight: bfloat16 [12800, 6144], P(None, 'hid'), may hold values from -0.0546875 to 0.0546875
- proj_bias: float32 [6144], P('hid'), may hold values from -3 to 3
- text_embed: bfloat16 [16, 480, 6144], P('req', None, 'hid')
- attn_gain: bfloat16 [6144], replicated, may hold values from 0.25 to 1.75
- query_weight: bfloat16 [6144, 6144], P(None, 'hid')
- key_weight: bfloat16 [6144, 1024], P(None, 'hid')
- value_weight: bfloat16 [6144, 1024], P(None, 'hid'), may hold values from -0.078125 to 0.078125
- out_weight: bfloat16 [6144, 6144], P('hid'), may hold values from -0.078125 to 0.078125
- final_gain: bfloat16 [6144], replicated, may hold values from 0.25 to 1.75
- head_weight: bfloat16 [49152, 6144], P(('req', 'hid')), may hold values from -0.23925781 to 0.23925781
- lengths: int32 [16], P('req'), may hold values from 160 to 480, as said below
- tile_request: int32 [8], replicated, may hold values from 0 to 15, as said below
- insert_pos: int32 [8], replicated, may hold values from 0 to 224, as said below
Outputs:
- hidden: bfloat16 [16, 480, 6144], P('req', None, 'hid')
- final_norm: float32 [16], replicated
- logit_max: float32 [16], replicated
The draws below stay inside these ranges and needn't reach their ends.
Inputs may be any that keep to these rules, and one draw needn't show every extreme that they name: For every g, the requests 2g and 2g + 1 have lengths that add up to exactly 640. `tile_request`: each pair of requests 2g, 2g + 1 holds exactly one tile, in the one of the two whose length is not smaller. insert_pos[t] + 256 is at most the length of request tile_request[t].
All inputs are finite; a program needn't handle non-finite values.
Results may differ from the reference program's by a relative error of at most 0.0095.
Values may be sent and summed in bfloat16 or wider, within the bound.
No kernel may reach another device: no remote copies, remote signals or barrier semaphores. Data moves between devices by JAX's collectives and lax.ppermute only.
A program may use at most 128 MiB of HBM per device.

```python
import math
import jax
import jax.numpy as jnp
from jax import lax

MERGED = 12800
HEADS = 48
KV_HEADS = 8
HEAD_DIM = 128
D = 6144
VOCAB = 49152
TILE_TOK = 256
REQ_GRP = 2
LEN_MAX = 480
LIVE_GRP = 640
REQS = 16
TILES = 8
N_HID = 16


def rough_field(key, array_shape, row_lo, row_hi, overall):
    key_base, key_rows, key_cols = jax.random.split(key, 3)
    columns = array_shape[-1]
    row_scale = jnp.exp(jax.random.uniform(key_rows, array_shape[:-1] + (1,), minval=math.log(row_lo), maxval=math.log(row_hi)))
    col_ramp = jnp.exp(jnp.linspace(0.0, math.log(3.0), columns))
    col_scale = col_ramp * jnp.exp(jax.random.uniform(key_cols, (columns,), minval=0.0, maxval=math.log(3.4)))
    base_vals = jax.random.normal(key_base, array_shape)
    return base_vals * row_scale * col_scale * overall


def draw_merged(key, part):
    return rough_field(key, (TILES, TILE_TOK, MERGED), 1.0, 10.0, 0.5).astype(jnp.bfloat16)


def draw_text_embed(key, part):
    return rough_field(key, (REQS, LEN_MAX, D), 0.4, 4.0, 0.3).astype(jnp.bfloat16)


def head_scaled(key, heads):
    key_base = jax.random.fold_in(key, 0)
    matrix = jax.random.normal(key_base, (D, heads * HEAD_DIM)) / math.sqrt(D)
    return matrix


def draw_query_weight(key, part):
    return head_scaled(key, HEADS).astype(jnp.bfloat16)


def draw_key_weight(key, part):
    return head_scaled(key, KV_HEADS).astype(jnp.bfloat16)


def layout_draw(key):
    base_key = jax.random.fold_in(key, 11)
    key_len, key_wide, key_perm, key_pos = jax.random.split(base_key, 4)
    groups = REQS // REQ_GRP
    group_ids = jnp.arange(groups, dtype=jnp.int32)
    first_len = jax.random.randint(key_len, (groups,), LIVE_GRP - LEN_MAX, LEN_MAX + 1, dtype=jnp.int32)
    first_len = jnp.where(group_ids == 0, jnp.maximum(first_len, LIVE_GRP - first_len), first_len)
    first_len = jnp.where(group_ids == groups - 1, jnp.minimum(first_len, LIVE_GRP // 2 - 1), first_len)
    widest = jax.random.randint(key_wide, (), 1, groups - 1, dtype=jnp.int32)
    first_len = jnp.where(group_ids == widest, LEN_MAX, first_len).astype(jnp.int32)
    second_len = (LIVE_GRP - first_len).astype(jnp.int32)
    lengths = jnp.stack([first_len, second_len], axis=1).reshape(REQS)
    owners = jax.random.permutation(key_perm, groups).astype(jnp.int32)
    longer = (second_len > first_len).astype(jnp.int32)
    requests = (REQ_GRP * owners + longer[owners]).astype(jnp.int32)
    room_left = lengths[requests] - TILE_TOK + 1
    positions = jax.random.randint(key_pos, (TILES,), 0, room_left, dtype=jnp.int32)
    positions = jnp.where(owners == widest, LEN_MAX - TILE_TOK, positions)
    positions = jnp.where(owners == 0, 0, positions).astype(jnp.int32)
    return (lengths, requests, positions)


def draw_lengths(key, part):
    return layout_draw(key)[0]


def draw_tile_request(key, part):
    return layout_draw(key)[1]


def draw_insert_pos(key, part):
    return layout_draw(key)[2]


def block_levels(own_key, extent, shards, smallest, top_value):
    loudness, own = 1.0, jax.random.fold_in(own_key, 6)
    for position, parts in shards:
        draws = jnp.exp(jax.random.uniform(jax.random.fold_in(own, position), (parts,), jnp.float32, smallest / len(shards), top_value / len(shards)))
        loudness = loudness * jnp.repeat(draws, extent[position] // parts).reshape([-1 if axis == position else 1 for axis in range(len(extent))])
    return loudness


def normal_values(key, extent, deviation, bound, pieces=(), held_as=jnp.bfloat16):
    result = deviation * jax.random.normal(key, extent, jnp.float32)
    if pieces:
        result = result * block_levels(key, extent, pieces, -0.22, 0.18)
    return jnp.clip(result, -bound, bound).astype(held_as)


def setup_inputs(seed: int = 0) -> dict:
    streams_of = jax.random.split(jax.random.key(seed), 17)
    merged = draw_merged(jax.random.fold_in(streams_of[16], 71), 0)
    ln_gain = jnp.clip(1.0 + 0.15 * jax.random.normal(streams_of[1], (MERGED,), jnp.float32), 0.25, 1.75).astype(jnp.bfloat16)
    ln_bias = normal_values(streams_of[2], (MERGED,), 0.5, 3.0)
    proj_weight = normal_values(streams_of[3], (MERGED, D), MERGED ** -0.5, 0.0546875, ((1, 16),))
    proj_bias = normal_values(streams_of[4], (D,), 0.5, 3.0, ((0, 16),), jnp.float32)
    text_embed = draw_text_embed(jax.random.fold_in(streams_of[16], 71), 0)
    attn_gain = jnp.clip(1.0 + 0.15 * jax.random.normal(streams_of[6], (D,), jnp.float32), 0.25, 1.75).astype(jnp.bfloat16)
    query_weight = draw_query_weight(jax.random.fold_in(streams_of[16], 71), 0)
    key_weight = draw_key_weight(jax.random.fold_in(streams_of[16], 71), 0)
    value_weight = normal_values(streams_of[9], (D, KV_HEADS * HEAD_DIM), D ** -0.5, 0.078125, ((1, 16),))
    out_weight = normal_values(streams_of[10], (D, D), D ** -0.5, 0.078125, ((0, 16),))
    final_gain = jnp.clip(1.0 + 0.15 * jax.random.normal(streams_of[11], (D,), jnp.float32), 0.25, 1.75).astype(jnp.bfloat16)
    head_weight = normal_values(streams_of[12], (VOCAB, D), 0.04, 0.23925781, ((0, 128),))
    lengths = draw_lengths(jax.random.fold_in(streams_of[16], 71), 0)
    tile_request = draw_tile_request(jax.random.fold_in(streams_of[16], 71), 0)
    insert_pos = draw_insert_pos(jax.random.fold_in(streams_of[16], 71), 0)
    return dict(merged=merged, ln_gain=ln_gain, ln_bias=ln_bias, proj_weight=proj_weight, proj_bias=proj_bias, text_embed=text_embed, attn_gain=attn_gain, query_weight=query_weight, key_weight=key_weight, value_weight=value_weight, out_weight=out_weight, final_gain=final_gain, head_weight=head_weight, lengths=lengths, tile_request=tile_request, insert_pos=insert_pos)


def rotary(values, positions):
    half_dim = values.shape[-1] // 2
    inv_freq = jnp.exp(jnp.arange(half_dim, dtype=jnp.float32) * (-2.0 * math.log(1000000.0) / values.shape[-1]))
    angles = positions.astype(jnp.float32)[:, None] * inv_freq[None, :]
    cosine = jnp.cos(angles)[:, None, :]
    sine_val = jnp.sin(angles)[:, None, :]
    first_half = values[..., :half_dim]
    second = values[..., half_dim:]
    return jnp.concatenate([first_half * cosine - second * sine_val, second * cosine + first_half * sine_val], axis=-1)

def attend(operands):
    queries, key_rows, value_rows, length = operands
    grouped = queries.reshape(LEN_MAX, KV_HEADS, HEADS // KV_HEADS, HEAD_DIM).astype(jnp.float32)
    scores = jnp.einsum('qkgd,skd->kgqs', grouped, key_rows.astype(jnp.float32)) / math.sqrt(HEAD_DIM)
    positions = jnp.arange(LEN_MAX)
    allowed = positions[None, :] <= positions[:, None]
    scores = jnp.where(allowed, scores, -jnp.inf)
    row_top = lax.optimization_barrier(jnp.max(scores, axis=-1, keepdims=True))
    weights = jnp.exp(scores - row_top)
    weights = (weights / lax.optimization_barrier(jnp.sum(weights, axis=-1, keepdims=True))).astype(jnp.bfloat16)
    mixed_out = jnp.einsum('kgqs,skd->qkgd', weights.astype(jnp.float32), value_rows.astype(jnp.float32))
    live_mask = (positions < length)[:, None, None, None]
    mixed_out = jnp.where(live_mask, mixed_out, 0.0)
    return mixed_out.reshape(LEN_MAX, D).astype(jnp.bfloat16)

def reference(merged, ln_gain, ln_bias, proj_weight, proj_bias, text_embed, attn_gain, query_weight, key_weight, value_weight, out_weight, final_gain, head_weight, lengths, tile_request, insert_pos):
    tile_rows = merged.reshape(TILES * TILE_TOK, MERGED).astype(jnp.float32)
    row_mean = lax.optimization_barrier(jnp.mean(tile_rows, axis=1, keepdims=True))
    row_var = lax.optimization_barrier(jnp.mean(tile_rows * tile_rows, axis=1, keepdims=True)) - row_mean * row_mean
    normed = ((tile_rows - row_mean) * lax.rsqrt(row_var + 1e-05) * ln_gain.astype(jnp.float32) + ln_bias.astype(jnp.float32)).astype(jnp.bfloat16)
    projected = jnp.dot(normed, proj_weight, preferred_element_type=jnp.float32) + proj_bias
    projected = jax.nn.gelu(projected, approximate=False).astype(jnp.bfloat16).reshape(TILES, TILE_TOK, D)
    embedded = text_embed
    zero_index = jnp.zeros((), jnp.int32)
    for tile_index in range(TILES):
        embedded = lax.dynamic_update_slice(embedded, projected[tile_index][None], (tile_request[tile_index].astype(jnp.int32), insert_pos[tile_index].astype(jnp.int32), zero_index))
    row_data = embedded.reshape(REQS * LEN_MAX, D).astype(jnp.float32)
    row_scale = lax.rsqrt(lax.optimization_barrier(jnp.sum(row_data * row_data, axis=1)) / D + 1e-05)[:, None]
    scaled = (row_data * attn_gain.astype(jnp.float32)).astype(jnp.bfloat16)
    queries = jnp.dot(scaled, query_weight, preferred_element_type=jnp.float32) * row_scale
    key_raw = (jnp.dot(scaled, key_weight, preferred_element_type=jnp.float32) * row_scale).astype(jnp.bfloat16)
    kv_values = (jnp.dot(scaled, value_weight, preferred_element_type=jnp.float32) * row_scale).astype(jnp.bfloat16)
    positions = jnp.arange(LEN_MAX)
    queries = queries.reshape(REQS, LEN_MAX, HEADS, HEAD_DIM)
    key_raw = key_raw.reshape(REQS, LEN_MAX, KV_HEADS, HEAD_DIM)
    kv_values = kv_values.reshape(REQS, LEN_MAX, KV_HEADS, HEAD_DIM)
    q_rotated = jax.vmap(lambda block: rotary(block, positions))(queries).astype(jnp.bfloat16)
    k_rotated = jax.vmap(lambda block: rotary(block.astype(jnp.float32), positions))(key_raw).astype(jnp.bfloat16)
    attended = lax.map(attend, (q_rotated, k_rotated, kv_values, lengths))
    flat_attended = attended.reshape(REQS * LEN_MAX, D)
    block_cols = D // N_HID
    partial_value = jnp.zeros((REQS * LEN_MAX, D), jnp.float32)
    for block_index in range(N_HID):
        lower = block_index * block_cols
        term = jnp.dot(flat_attended[:, lower:lower + block_cols], out_weight[lower:lower + block_cols], preferred_element_type=jnp.float32).astype(jnp.bfloat16)
        term = lax.optimization_barrier(term)
        partial_value = partial_value + term.astype(jnp.float32)
    hidden = (row_data + partial_value).astype(jnp.bfloat16).reshape(REQS, LEN_MAX, D)
    last_rows = hidden[jnp.arange(REQS), lengths - 1].astype(jnp.float32)
    squares = lax.optimization_barrier(jnp.sum(last_rows * last_rows, axis=1))
    final_norm = jnp.sqrt(squares)
    final_scaled = (last_rows * lax.rsqrt(squares / D + 1e-05)[:, None] * final_gain.astype(jnp.float32)).astype(jnp.bfloat16)
    logits = jnp.dot(final_scaled, head_weight.T, preferred_element_type=jnp.float32)
    return (hidden, final_norm, lax.optimization_barrier(jnp.max(logits, axis=1)))
```

```python
import math

import jax
import jax.numpy as jnp
from jax import lax
from jax.experimental import pallas as pl
from jax.experimental.pallas import tpu as pltpu
from jax.sharding import PartitionSpec as P

HEAD_DIM = 128
D = 6144
MERGED = 12800
REQ_GRP = 2
LEN_MAX = 480
LIVE = 640
TILE = 256
TEXT = LIVE - TILE
N_HID = 16
N_REQ = 8
RING = 4
FEAT = D // N_HID
MFEAT = MERGED // N_HID
MPAD = 896
BF = jnp.bfloat16
F32 = jnp.float32
VM = pltpu.VMEM


def vmem():
    return pl.BlockSpec(memory_space=pltpu.VMEM)


def params(mib):
    return pltpu.CompilerParams(vmem_limit_bytes=mib << 20)


def shift(block, dx, dz):
    route = []
    for i in range(N_HID):
        x, z = divmod(i, RING)
        route.append((((x + dx) % RING) * RING + (z + dz) % RING, i))
    return lax.ppermute(block, "hid", route)


def ring_gather(shard):
    half = shard.shape[0] // 2
    found = []
    for first in (0, 1):
        own = lax.slice_in_dim(shard, first * half, (first + 1) * half, axis=0)

        def inner(b, d):
            return shift(b, 0, d) if first == 0 else shift(b, d, 0)

        def outer(b, d):
            return shift(b, d, 0) if first == 0 else shift(b, 0, d)

        line = [(own, 0), (inner(own, -1), -1), (inner(own, 1), 1), (inner(own, 2), 2)]
        group = jnp.concatenate([b for b, _ in line], axis=0)
        minus = outer(group, -1)
        plus = outer(group, 1)
        far_a = outer(lax.slice_in_dim(minus, 0, 2 * half, axis=0), -1)
        far_b = outer(lax.slice_in_dim(plus, 2 * half, 4 * half, axis=0), 1)
        offs = [d for _, d in line]
        table = {}
        for array, out, part in (
            (group, 0, offs),
            (minus, -1, offs),
            (plus, 1, offs),
            (far_a, 2, offs[:2]),
            (far_b, 2, offs[2:]),
        ):
            found.append(array)
            for j, d in enumerate(part):
                rel = (out % RING, d % RING) if first == 0 else (d % RING, out % RING)
                table[rel] = (len(found) - 1, j * half)
        if first == 0:
            table_a = table
        else:
            table_b = table
    order = [(dx, dz) for dx in range(RING) for dz in range(RING)]
    return found, [(table_a[r], table_b[r]) for r in order]


def pack_kernel(order_ref, x_ref, o_ref):
    for g in range(N_REQ):
        rows = x_ref[order_ref[g]]
        v = rows.astype(F32)
        stats = []
        for s in (jnp.sum(v, axis=1, keepdims=True), jnp.sum(v * v, axis=1, keepdims=True)):
            for _ in range(3):
                part = s.astype(BF)
                stats.append(part)
                s = s - part.astype(F32)
        lo, hi = g * 32, (g + 1) * 32
        lane = lax.broadcasted_iota(jnp.int32, (32, MPAD - 768), 1)
        tail = jnp.zeros((32, MPAD - 768), F32)
        for j, part in enumerate(stats):
            tail = jnp.where(lane == 32 + j, part.astype(F32), tail)
        o_ref[lo:hi, 0:768] = rows[:, 0:768]
        o_ref[lo:hi, 768:MPAD] = tail.astype(BF)
        o_ref[lo:hi, 768:800] = rows[:, 768:800]


def pack(merged, tile_order):
    return pl.pallas_call(
        pack_kernel,
        out_shape=jax.ShapeDtypeStruct((TILE, MPAD), BF),
        in_specs=[pl.BlockSpec(memory_space=pltpu.SMEM), vmem()],
        out_specs=vmem(),
        compiler_params=params(16),
        name="pack",
    )(tile_order, merged)


def project_kernel(x_ref, st_ref, w_ref, g_ref, b_ref, pb_ref, o_ref, mean, rstd, acc):
    k = pl.program_id(0)

    @pl.when(k == 0)
    def _():
        total = jnp.zeros((TILE, 128), F32)
        for s in range(N_HID):
            total = total + st_ref[s * TILE : (s + 1) * TILE, :].astype(F32)
        m = jnp.sum(total[:, 32:35], axis=1, keepdims=True) * (1.0 / MERGED)
        q = jnp.sum(total[:, 35:38], axis=1, keepdims=True) * (1.0 / MERGED)
        mean[...] = jnp.broadcast_to(m, (TILE, 128))
        rstd[...] = jnp.broadcast_to(lax.rsqrt(q - m * m + 1e-05), (TILE, 128))
        acc[...] = jnp.zeros_like(acc)

    v = x_ref[:, 0:MFEAT].astype(F32)
    normed = (v - mean[:, 0:1]) * rstd[:, 0:1] * g_ref[0] + b_ref[0]
    acc[...] += jnp.dot(normed.astype(BF), w_ref[...], preferred_element_type=F32)

    @pl.when(k == N_HID - 1)
    def _():
        y = acc[...] + pb_ref[...]
        y = 0.5 * y * (1.0 + lax.erf(y * math.sqrt(0.5)))
        o_ref[...] = y.astype(BF)


def project(gathered, weight, gain, bias, out_bias):
    return pl.pallas_call(
        project_kernel,
        out_shape=jax.ShapeDtypeStruct((TILE, FEAT), BF),
        grid=(N_HID,),
        in_specs=[
            pl.BlockSpec((TILE, MPAD), lambda k: (k, 0)),
            pl.BlockSpec((N_HID * TILE, 128), lambda k: (0, 6)),
            pl.BlockSpec((MFEAT, FEAT), lambda k: (k, 0)),
            pl.BlockSpec((1, 1, MFEAT), lambda k: (k, 0, 0)),
            pl.BlockSpec((1, 1, MFEAT), lambda k: (k, 0, 0)),
            pl.BlockSpec((1, FEAT), lambda k: (0, 0)),
        ],
        out_specs=pl.BlockSpec((TILE, FEAT), lambda k: (0, 0)),
        scratch_shapes=[VM((TILE, 128), F32), VM((TILE, 128), F32), VM((TILE, FEAT), F32)],
        compiler_params=params(24),
        cost_estimate=pl.CostEstimate(
            flops=2 * TILE * MERGED * FEAT, bytes_accessed=17 << 20, transcendentals=0
        ),
        name="project",
    )(gathered, gathered, weight, gain, bias, out_bias)


def turn(v, cos, sin):
    return v * cos + pltpu.roll(v, HEAD_DIM // 2, 1) * sin


def qkv(shard, weight, gain, cos, sin, sources, name):
    rows = shard.shape[0]
    half = rows // 2
    arrays, where = ring_gather(shard)

    def kernel(src_ref, *refs):
        ins = refs[: len(arrays)]
        w_ref, g_ref, cos_ref, sin_ref, q_ref, kv_ref, xs, sq, acc = refs[len(arrays) :]
        k = pl.program_id(0)

        @pl.when(k == 0)
        def _():
            acc[...] = jnp.zeros_like(acc)
            sq[...] = jnp.zeros_like(sq)

        for i, places in enumerate(where):

            @pl.when(k == i)
            def _(places=places):
                for part, (a, row) in enumerate(places):
                    xs[part * half : (part + 1) * half, :] = ins[a][row : row + half, :]

        v = xs[...].astype(F32)
        w = v * v
        sq[...] += w[:, 0:128] + w[:, 128:256] + w[:, 256:384]
        scaled = (v * g_ref[0]).astype(BF)
        acc[...] += jnp.dot(scaled, w_ref[...], preferred_element_type=F32)

        @pl.when(k == N_HID - 1)
        def _():
            scale = lax.rsqrt(jnp.sum(sq[...], axis=1, keepdims=True) * (1.0 / D) + 1e-05)
            for h in range(FEAT // HEAD_DIM):
                part = acc[:, h * HEAD_DIM : (h + 1) * HEAD_DIM] * scale
                q_ref[:, h * HEAD_DIM : (h + 1) * HEAD_DIM] = turn(
                    part, cos_ref[...], sin_ref[...]
                ).astype(BF)
            kv_ref[...] = (acc[:, FEAT:] * scale).astype(BF)

    whole = lambda k, s: (0, 0)
    return pl.pallas_call(
        kernel,
        out_shape=(
            jax.ShapeDtypeStruct((rows, FEAT), BF),
            jax.ShapeDtypeStruct((rows, HEAD_DIM), BF),
        ),
        grid_spec=pltpu.PrefetchScalarGridSpec(
            num_scalar_prefetch=1,
            grid=(N_HID,),
            in_specs=[vmem() for _ in arrays]
            + [
                pl.BlockSpec((FEAT, FEAT + HEAD_DIM), lambda k, s: (s[k], 0)),
                pl.BlockSpec((1, 1, FEAT), lambda k, s: (s[k], 0, 0)),
                pl.BlockSpec((rows, HEAD_DIM), whole),
                pl.BlockSpec((rows, HEAD_DIM), whole),
            ],
            out_specs=(
                pl.BlockSpec((rows, FEAT), whole),
                pl.BlockSpec((rows, HEAD_DIM), whole),
            ),
            scratch_shapes=[
                VM((rows, FEAT), BF),
                VM((rows, HEAD_DIM), F32),
                VM((rows, FEAT + HEAD_DIM), F32),
            ],
        ),
        compiler_params=params(24),
        cost_estimate=pl.CostEstimate(
            flops=2 * rows * D * (FEAT + HEAD_DIM), bytes_accessed=12 << 20, transcendentals=0
        ),
        name=name,
    )(sources, *arrays, weight, gain, cos, sin)


def attend_kernel(
    low_ref, qt, qi, ot, pt, oi, pi, cos_ref, sin_ref, row_ref, col_ref, o_ref, keys, vals
):
    upper = low_ref[0] == 0
    lane = lax.broadcasted_iota(jnp.int32, (LIVE, HEAD_DIM), 1)
    own = jnp.concatenate([ot[...], oi[...]], axis=0).astype(F32)
    other = jnp.concatenate([pt[...], pi[...]], axis=0).astype(F32)
    low = jnp.where(upper, other, own)
    high = jnp.where(upper, own, other)
    key = jnp.where(lane < 64, low, pltpu.roll(high, 64, 1))
    val = jnp.where(lane < 64, pltpu.roll(low, 64, 1), high)
    keys[...] = turn(key, cos_ref[...], sin_ref[...]).astype(BF)
    vals[...] = val.astype(BF)
    code = col_ref[...]
    for blk in range(LIVE // 128):
        rows = slice(blk * 128, (blk + 1) * 128)
        mine = row_ref[rows, :]
        start = jnp.where(mine >= 1024, 1024, 0)
        live = jnp.logical_and(code <= mine, code >= start)
        for h in range(FEAT // HEAD_DIM):
            cols = slice(h * HEAD_DIM, (h + 1) * HEAD_DIM)
            if blk < TEXT // 128:
                q = qt[rows, cols]
            else:
                q = qi[blk * 128 - TEXT : blk * 128 - TEXT + 128, cols]
            s = lax.dot_general(
                q, keys[...], (((1,), (1,)), ((), ())), preferred_element_type=F32
            ) * (1.0 / math.sqrt(HEAD_DIM))
            s = jnp.where(live, s, -jnp.inf)
            w = jnp.exp(s - jnp.max(s, axis=1, keepdims=True))
            total = jnp.sum(w, axis=1, keepdims=True)
            mixed = jnp.dot(w.astype(BF), vals[...], preferred_element_type=F32)
            o_ref[rows, cols] = (mixed / total).astype(BF)


def attend(low, qt, qi, ot, pt, oi, pi, cos, sin, code):
    return pl.pallas_call(
        attend_kernel,
        out_shape=jax.ShapeDtypeStruct((LIVE, FEAT), BF),
        in_specs=[pl.BlockSpec(memory_space=pltpu.SMEM)] + [vmem()] * 10,
        out_specs=vmem(),
        scratch_shapes=[VM((LIVE, HEAD_DIM), BF), VM((LIVE, HEAD_DIM), BF)],
        compiler_params=params(24),
        cost_estimate=pl.CostEstimate(flops=1 << 30, bytes_accessed=2 << 20, transcendentals=0),
        name="attend",
    )(low, qt, qi, ot, pt, oi, pi, cos, sin, code[:, None], code[None, :])


def spread_kernel(a_ref, w_ref, o_ref):
    o_ref[0] = jnp.dot(a_ref[...], w_ref[...], preferred_element_type=F32).astype(BF)


def spread(attended, weight):
    return pl.pallas_call(
        spread_kernel,
        out_shape=jax.ShapeDtypeStruct((N_HID, LIVE, FEAT), BF),
        grid=(N_HID,),
        in_specs=[
            pl.BlockSpec((LIVE, FEAT), lambda k: (0, 0)),
            pl.BlockSpec((FEAT, FEAT), lambda k: (0, k)),
        ],
        out_specs=pl.BlockSpec((1, LIVE, FEAT), lambda k: (k, 0, 0)),
        compiler_params=params(24),
        cost_estimate=pl.CostEstimate(
            flops=2 * LIVE * FEAT * D, bytes_accessed=13 << 20, transcendentals=0
        ),
        name="spread",
    )(attended, weight)


def finish_kernel(text_ref, tile_ref, sum_ref, slot_ref, o_ref):
    for r in range(REQ_GRP):
        row = slot_ref[r]
        pick = (lax.broadcasted_iota(jnp.int32, (LEN_MAX, LIVE), 1) == row).astype(BF)
        moved = jnp.dot(pick, sum_ref[...], preferred_element_type=F32)
        image = jnp.dot(pick[:, TEXT:], tile_ref[...], preferred_element_type=F32)
        base = jnp.where(row >= TEXT, image, text_ref[r].astype(F32))
        o_ref[r] = (base + moved).astype(BF)


def finish(text, tile, sums, slots):
    return pl.pallas_call(
        finish_kernel,
        out_shape=jax.ShapeDtypeStruct((REQ_GRP, LEN_MAX, FEAT), BF),
        in_specs=[vmem()] * 4,
        out_specs=vmem(),
        compiler_params=params(24),
        name="finish",
    )(text, tile, sums, slots)


def shards(
    merged,
    ln_gain,
    ln_bias,
    proj_weight,
    proj_bias,
    text_embed,
    attn_gain,
    query_weight,
    key_weight,
    value_weight,
    out_weight,
    final_gain,
    head_weight,
    lengths,
    tile_request,
    insert_pos,
):
    hid = lax.axis_index("hid")
    me = lax.axis_index("req")
    owners = tile_request // REQ_GRP
    tiles = jnp.arange(N_REQ, dtype=jnp.int32)
    tile_order = jnp.sum(
        jnp.where(owners[None, :] == tiles[:, None], tiles[None, :], 0), axis=1
    ).astype(jnp.int32)
    mine = owners == me
    local_req = jnp.sum(jnp.where(mine, tile_request % REQ_GRP, 0))
    start = jnp.sum(jnp.where(mine, insert_pos, 0))
    len_a = lengths[0]
    first = local_req * len_a + start

    n = jnp.arange(LIVE, dtype=jnp.int32)
    packed = jnp.where(n < TEXT, jnp.where(n < first, n, n + TILE), n - TEXT + first)
    second = packed >= len_a
    pos = packed - jnp.where(second, len_a, 0)
    code = pos + jnp.where(second, 1024, 0)
    flat = pos + jnp.where(second, LEN_MAX, 0)
    slot = jnp.arange(LEN_MAX, dtype=jnp.int32)
    at = jnp.stack([slot, slot + len_a])
    in_tile = jnp.logical_and(at >= first, at < first + TILE)
    row_of = jnp.where(in_tile, at - first + TEXT, jnp.where(at < first, at, at - TILE))
    row_of = jnp.where(slot[None, :] < lengths[:, None], row_of, -1)

    half_dim = HEAD_DIM // 2
    inv_freq = jnp.exp(
        jnp.arange(half_dim, dtype=F32) * (-2.0 * math.log(1000000.0) / HEAD_DIM)
    )
    angles = pos.astype(F32)[:, None] * inv_freq[None, :]
    cosine, sine = jnp.cos(angles), jnp.sin(angles)
    cos = jnp.concatenate([cosine, cosine], axis=1)
    sin = jnp.concatenate([-sine, sine], axis=1)

    gathered = lax.all_gather(pack(merged, tile_order), "hid", axis=0, tiled=True)

    pick = (flat[:TEXT, None] == jnp.arange(REQ_GRP * LEN_MAX)[None, :]).astype(BF)
    text_rows = jnp.dot(
        pick, text_embed.reshape(REQ_GRP * LEN_MAX, FEAT), preferred_element_type=F32
    ).astype(BF)
    x, z = hid // RING, hid % RING
    rel = jnp.arange(N_HID, dtype=jnp.int32)
    sources = ((x + rel // RING) % RING) * RING + (z + rel % RING) % RING
    weight = jnp.concatenate([query_weight, key_weight, value_weight], axis=1)
    gain = attn_gain.astype(F32).reshape(N_HID, 1, FEAT)
    partner = [(i, i ^ 1) for i in range(N_HID)]

    q_text, kv_text = qkv(text_rows, weight, gain, cos[:TEXT], sin[:TEXT], sources, "qkv_text")
    other_text = lax.ppermute(kv_text, "hid", partner)

    projected = project(
        gathered,
        proj_weight,
        ln_gain.astype(F32).reshape(N_HID, 1, MFEAT),
        ln_bias.astype(F32).reshape(N_HID, 1, MFEAT),
        proj_bias[None, :],
    )
    tile = lax.all_to_all(
        projected.reshape(N_REQ, TILE // N_REQ, FEAT), "req", split_axis=0, concat_axis=0, tiled=True
    ).reshape(TILE, FEAT)
    q_tile, kv_tile = qkv(tile, weight, gain, cos[TEXT:], sin[TEXT:], sources, "qkv_tile")
    other_tile = lax.ppermute(kv_tile, "hid", partner)

    low = (hid % 2 == 0).astype(jnp.int32)[None]
    attended = attend(
        low, q_text, q_tile, kv_text, other_text, kv_tile, other_tile, cos, sin, code
    )
    partial = spread(attended, out_weight)
    sums = lax.psum_scatter(
        partial.reshape(N_HID * LIVE, FEAT), "hid", scatter_dimension=0, tiled=True
    )
    hidden = finish(text_embed, tile, sums, row_of[:, :, None])

    last = jnp.sum(jnp.where(slot[None, :] == lengths[:, None] - 1, row_of, 0), axis=1)
    pick_last = (last[:, None] == n[None, :]).astype(BF)
    rows_last = jnp.dot(pick_last, attended, preferred_element_type=F32).astype(BF)
    term = jnp.dot(rows_last, out_weight, preferred_element_type=F32).astype(BF)
    term = term.reshape(REQ_GRP, N_HID, FEAT).transpose(1, 0, 2)
    terms = lax.all_to_all(term, "hid", split_axis=0, concat_axis=0, tiled=True)
    base = jnp.dot(pick_last[:, :TEXT], text_rows, preferred_element_type=F32) + jnp.dot(
        pick_last[:, TEXT:], tile, preferred_element_type=F32
    )
    last_own = (base + jnp.sum(terms.astype(F32), axis=0)).astype(BF)
    full_width = lax.all_gather(last_own, "hid", axis=1, tiled=True)
    all_last = lax.all_gather(full_width, "req", axis=0, tiled=True)
    last_values = all_last.astype(F32)
    last_squares = jnp.sum(last_values * last_values, axis=1)
    final_norm = jnp.sqrt(last_squares)
    final_scaled = (
        last_values * lax.rsqrt(last_squares / D + 1e-05)[:, None] * final_gain.astype(F32)
    ).astype(BF)
    logits = lax.dot_general(
        final_scaled, head_weight, (((1,), (1,)), ((), ())), preferred_element_type=F32
    )
    top = jnp.max(logits, axis=1)
    top = jnp.max(lax.all_gather(top, "hid", axis=0), axis=0)
    logit_max = jnp.max(lax.all_gather(top, "req", axis=0), axis=0)
    return (hidden, final_norm, logit_max)


def solution(mesh):
    return jax.shard_map(
        shards,
        mesh=mesh,
        in_specs=(
            P(None, "req", "hid"),
            P(),
            P(),
            P(None, "hid"),
            P("hid"),
            P("req", None, "hid"),
            P(),
            P(None, "hid"),
            P(None, "hid"),
            P(None, "hid"),
            P("hid", None),
            P(),
            P(("req", "hid"), None),
            P("req"),
            P(),
            P(),
        ),
        out_specs=(P("req", None, "hid"), P(), P()),
        check_vma=False,
    )
```

```python
import math

import jax
import jax.numpy as jnp
from jax import lax
from jax.experimental import pallas as pl
from jax.experimental.pallas import tpu as pltpu
from jax.sharding import PartitionSpec as P

HEAD_DIM = 128
D = 6144
MERGED = 12800
REQ_GRP = 2
LEN_MAX = 480
LIVE = 640
TILE = 256
TEXT = LIVE - TILE
N_HID = 16
N_REQ = 8
RING = 4
FEAT = D // N_HID
MFEAT = MERGED // N_HID
MPAD = 896
BF = jnp.bfloat16
F32 = jnp.float32
VM = pltpu.VMEM


def vmem():
    return pl.BlockSpec(memory_space=pltpu.VMEM)


def params(mib):
    return pltpu.CompilerParams(vmem_limit_bytes=mib << 20)


def shift(block, dx, dz):
    route = []
    for i in range(N_HID):
        x, z = divmod(i, RING)
        route.append((((x + dx) % RING) * RING + (z + dz) % RING, i))
    return lax.ppermute(block, "hid", route)


def shift_req(block, dy, dc):
    route = []
    for i in range(N_REQ):
        y, c = divmod(i, 2)
        route.append((((y + dy) % RING) * 2 + (c + dc) % 2, i))
    return lax.ppermute(block, "req", route)


def line_of(block, move):
    return [block, move(block, -1), move(block, 1), move(block, 2)]


def along_x(b, d):
    return shift(b, d, 0)


def along_z(b, d):
    return shift(b, 0, d)


def along_y(b, d):
    return shift_req(b, d, 0)


def join(*blocks):
    total = blocks[0].astype(F32)
    for b in blocks[1:]:
        total = total + b.astype(F32)
    return total


def over_line(block, move):
    own, below, above, far = line_of(block, move)
    return (own + far) + (below + above)


def axes_of(first):
    return (along_z, along_x) if first == 0 else (along_x, along_z)


def gather_near(shard):
    half = shard.shape[0] // 2
    near = []
    for first in (0, 1):
        inner, outer = axes_of(first)
        own = lax.slice_in_dim(shard, first * half, (first + 1) * half, axis=0)
        group = jnp.concatenate(line_of(own, inner), axis=0)
        near.append((group, outer(group, -1), outer(group, 1)))
    return near


def gather_far(near):
    arrays, tables = [], []
    for first in (0, 1):
        _, outer = axes_of(first)
        group, minus, plus = near[first]
        half = group.shape[0] // RING
        far_a = outer(lax.slice_in_dim(minus, 0, 2 * half, axis=0), -1)
        far_b = outer(lax.slice_in_dim(plus, 2 * half, 4 * half, axis=0), 1)
        offs = [0, -1, 1, 2]
        table = {}
        for array, out, part in (
            (group, 0, offs),
            (minus, -1, offs),
            (plus, 1, offs),
            (far_a, 2, offs[:2]),
            (far_b, 2, offs[2:]),
        ):
            arrays.append(array)
            for j, d in enumerate(part):
                rel = (out % RING, d % RING) if first == 0 else (d % RING, out % RING)
                table[rel] = (len(arrays) - 1, j * half)
        tables.append(table)
    order = [(dx, dz) for dx in range(RING) for dz in range(RING)]
    return arrays, [(tables[0][r], tables[1][r]) for r in order]


def in_hbm(x):
    return pltpu.with_memory_space_constraint(x, pltpu.HBM)


def pack_kernel(order_ref, x_ref, o_ref):
    for g in range(N_REQ):
        rows = x_ref[order_ref[g]]
        v = rows.astype(F32)
        stats = []
        for s in (jnp.sum(v, axis=1, keepdims=True), jnp.sum(v * v, axis=1, keepdims=True)):
            for _ in range(3):
                part = s.astype(BF)
                stats.append(part)
                s = s - part.astype(F32)
        lo, hi = g * 32, (g + 1) * 32
        lane = lax.broadcasted_iota(jnp.int32, (32, MPAD - 768), 1)
        tail = jnp.zeros((32, MPAD - 768), F32)
        for j, part in enumerate(stats):
            tail = jnp.where(lane == 32 + j, part.astype(F32), tail)
        o_ref[lo:hi, 0:768] = rows[:, 0:768]
        o_ref[lo:hi, 768:MPAD] = tail.astype(BF)
        o_ref[lo:hi, 768:800] = rows[:, 768:800]


def pack(merged, tile_order):
    return pl.pallas_call(
        pack_kernel,
        out_shape=jax.ShapeDtypeStruct((TILE, MPAD), BF),
        in_specs=[pl.BlockSpec(memory_space=pltpu.SMEM), vmem()],
        out_specs=vmem(),
        compiler_params=params(16),
        name="pack",
    )(tile_order, merged)


def project(arrays, where, weight, gain, bias, out_bias, sources):
    half = TILE // 2
    n = len(arrays)

    def kernel(src_ref, *refs):
        ins = refs[:n]
        wa_ref, wb_ref, ga_ref, gb_ref, ba_ref, bb_ref, pb_ref, o_ref, mean, rstd, xs, acc = refs[n:]
        k = pl.program_id(0)

        @pl.when(k == 0)
        def _():
            parts = []
            for h in (0, 1):
                total = jnp.zeros((half, 128), F32)
                for places in where:
                    a, row = places[h]
                    total = total + ins[a][row : row + half, 768:MPAD].astype(F32)
                parts.append(total)
            total = jnp.concatenate(parts, axis=0)
            m = jnp.sum(total[:, 32:35], axis=1, keepdims=True) * (1.0 / MERGED)
            q = jnp.sum(total[:, 35:38], axis=1, keepdims=True) * (1.0 / MERGED)
            mean[...] = jnp.broadcast_to(m, (TILE, 128))
            rstd[...] = jnp.broadcast_to(lax.rsqrt(q - m * m + 1e-05), (TILE, 128))
            acc[...] = jnp.zeros_like(acc)

        for i in range(N_HID // 2):

            @pl.when(k == i)
            def _(i=i):
                for j in (0, 1):
                    for h, (a, row) in enumerate(where[2 * i + j]):
                        xs[j, h * half : (h + 1) * half, :] = ins[a][row : row + half, :]

        for j, (w_ref, g_ref, b_ref) in enumerate(
            ((wa_ref, ga_ref, ba_ref), (wb_ref, gb_ref, bb_ref))
        ):
            v = xs[j, :, 0:MFEAT].astype(F32)
            normed = (v - mean[:, 0:1]) * rstd[:, 0:1] * g_ref[0] + b_ref[0]
            acc[...] += jnp.dot(normed.astype(BF), w_ref[...], preferred_element_type=F32)

        @pl.when(k == N_HID // 2 - 1)
        def _():
            y = acc[...] + pb_ref[...]
            y = 0.5 * y * (1.0 + lax.erf(y * math.sqrt(0.5)))
            o_ref[...] = y.astype(BF)

    vec = lambda j: pl.BlockSpec((1, 1, MFEAT), lambda k, s: (s[2 * k + j], 0, 0))
    mat = lambda j: pl.BlockSpec((MFEAT, FEAT), lambda k, s: (s[2 * k + j], 0))
    return pl.pallas_call(
        kernel,
        out_shape=jax.ShapeDtypeStruct((TILE, FEAT), BF),
        grid_spec=pltpu.PrefetchScalarGridSpec(
            num_scalar_prefetch=1,
            grid=(N_HID // 2,),
            in_specs=[vmem() for _ in arrays]
            + [mat(0), mat(1), vec(0), vec(1), vec(0), vec(1)]
            + [pl.BlockSpec((1, FEAT), lambda k, s: (0, 0))],
            out_specs=pl.BlockSpec((TILE, FEAT), lambda k, s: (0, 0)),
            scratch_shapes=[
                VM((TILE, 128), F32),
                VM((TILE, 128), F32),
                VM((2, TILE, MPAD), BF),
                VM((TILE, FEAT), F32),
            ],
        ),
        compiler_params=params(16),
        cost_estimate=pl.CostEstimate(
            flops=2 * TILE * MERGED * FEAT, bytes_accessed=17 << 20, transcendentals=0
        ),
        name="project",
    )(sources, *arrays, in_hbm(weight), in_hbm(weight), gain, gain, bias, bias, out_bias)


def turn(v, cos, sin):
    return v * cos + pltpu.roll(v, HEAD_DIM // 2, 1) * sin


def qkv(arrays, where, weights, gain, cos, sin, sources, name):
    half = arrays[0].shape[0] // RING
    rows = 2 * half
    n = len(arrays)
    wide = 2 * FEAT

    def kernel(src_ref, *refs):
        ins = refs[:n]
        (qa_ref, qb_ref, ka_ref, kb_ref, ga_ref, gb_ref, cos_ref, sin_ref) = refs[n : n + 8]
        q_ref, kv_ref, xs, sq, acc = refs[n + 8 :]
        k = pl.program_id(0)

        @pl.when(k == 0)
        def _():
            acc[...] = jnp.zeros_like(acc)
            sq[...] = jnp.zeros_like(sq)

        for i in range(N_HID // 2):

            @pl.when(k == i)
            def _(i=i):
                for j in (0, 1):
                    for h, (a, row) in enumerate(where[2 * i + j]):
                        xs[h * half : (h + 1) * half, j * FEAT : (j + 1) * FEAT] = ins[a][
                            row : row + half, :
                        ]

        v = xs[...].astype(F32)
        w = v * v
        sq[...] += sum(w[:, c * 128 : (c + 1) * 128] for c in range(wide // 128))
        scaled = (v * jnp.concatenate([ga_ref[0], gb_ref[0]], axis=1)).astype(BF)
        block = jnp.concatenate(
            [
                jnp.concatenate([qa_ref[...], ka_ref[...]], axis=1),
                jnp.concatenate([qb_ref[...], kb_ref[...]], axis=1),
            ],
            axis=0,
        )
        acc[...] += jnp.dot(scaled, block, preferred_element_type=F32)

        @pl.when(k == N_HID // 2 - 1)
        def _():
            scale = lax.rsqrt(jnp.sum(sq[...], axis=1, keepdims=True) * (1.0 / D) + 1e-05)
            for h in range(FEAT // HEAD_DIM):
                part = acc[:, h * HEAD_DIM : (h + 1) * HEAD_DIM] * scale
                q_ref[:, h * HEAD_DIM : (h + 1) * HEAD_DIM] = turn(
                    part, cos_ref[...], sin_ref[...]
                ).astype(BF)
            kv_ref[...] = (acc[:, FEAT:] * scale).astype(BF)

    whole = lambda k, s: (0, 0)
    mat = lambda j, cols: pl.BlockSpec((FEAT, cols), lambda k, s: (s[2 * k + j], 0))
    vec = lambda j: pl.BlockSpec((1, 1, FEAT), lambda k, s: (s[2 * k + j], 0, 0))
    wq, wkv = in_hbm(weights[0]), in_hbm(weights[1])
    return pl.pallas_call(
        kernel,
        out_shape=(
            jax.ShapeDtypeStruct((rows, FEAT), BF),
            jax.ShapeDtypeStruct((rows, HEAD_DIM), BF),
        ),
        grid_spec=pltpu.PrefetchScalarGridSpec(
            num_scalar_prefetch=1,
            grid=(N_HID // 2,),
            in_specs=[vmem() for _ in arrays]
            + [mat(0, FEAT), mat(1, FEAT), mat(0, HEAD_DIM), mat(1, HEAD_DIM), vec(0), vec(1)]
            + [pl.BlockSpec((rows, HEAD_DIM), whole)] * 2,
            out_specs=(
                pl.BlockSpec((rows, FEAT), whole),
                pl.BlockSpec((rows, HEAD_DIM), whole),
            ),
            scratch_shapes=[
                VM((rows, wide), BF),
                VM((rows, HEAD_DIM), F32),
                VM((rows, FEAT + HEAD_DIM), F32),
            ],
        ),
        compiler_params=params(14),
        cost_estimate=pl.CostEstimate(
            flops=2 * rows * D * (FEAT + HEAD_DIM), bytes_accessed=12 << 20, transcendentals=0
        ),
        name=name,
    )(sources, *arrays, wq, wq, wkv, wkv, gain, gain, cos, sin)


def attend_kernel(
    low_ref, qt, qi, ot, pt, oi, pi, cos_ref, sin_ref, row_ref, col_ref, o_ref, keys, vals
):
    upper = low_ref[0] == 0
    lane = lax.broadcasted_iota(jnp.int32, (LIVE, HEAD_DIM), 1)
    own = jnp.concatenate([ot[...], oi[...]], axis=0).astype(F32)
    other = jnp.concatenate([pt[...], pi[...]], axis=0).astype(F32)
    low = jnp.where(upper, other, own)
    high = jnp.where(upper, own, other)
    key = jnp.where(lane < 64, low, pltpu.roll(high, 64, 1))
    val = jnp.where(lane < 64, pltpu.roll(low, 64, 1), high)
    keys[...] = turn(key, cos_ref[...], sin_ref[...]).astype(BF)
    vals[...] = val.astype(BF)
    code = col_ref[...]
    for blk in range(LIVE // 128):
        rows = slice(blk * 128, (blk + 1) * 128)
        mine = row_ref[rows, :]
        start = jnp.where(mine >= 1024, 1024, 0)
        live = jnp.logical_and(code <= mine, code >= start)
        for h in range(FEAT // HEAD_DIM):
            cols = slice(h * HEAD_DIM, (h + 1) * HEAD_DIM)
            if blk < TEXT // 128:
                q = qt[rows, cols]
            else:
                q = qi[blk * 128 - TEXT : blk * 128 - TEXT + 128, cols]
            s = lax.dot_general(
                q, keys[...], (((1,), (1,)), ((), ())), preferred_element_type=F32
            ) * (1.0 / math.sqrt(HEAD_DIM))
            s = jnp.where(live, s, -jnp.inf)
            w = jnp.exp(s - jnp.max(s, axis=1, keepdims=True))
            total = jnp.sum(w, axis=1, keepdims=True)
            mixed = jnp.dot(w.astype(BF), vals[...], preferred_element_type=F32)
            o_ref[rows, cols] = (mixed / total).astype(BF)


def attend(low, qt, qi, ot, pt, oi, pi, cos, sin, code):
    return pl.pallas_call(
        attend_kernel,
        out_shape=jax.ShapeDtypeStruct((LIVE, FEAT), BF),
        in_specs=[pl.BlockSpec(memory_space=pltpu.SMEM)] + [vmem()] * 10,
        out_specs=vmem(),
        scratch_shapes=[VM((LIVE, HEAD_DIM), BF), VM((LIVE, HEAD_DIM), BF)],
        compiler_params=params(24),
        cost_estimate=pl.CostEstimate(flops=1 << 30, bytes_accessed=2 << 20, transcendentals=0),
        name="attend",
    )(low, qt, qi, ot, pt, oi, pi, cos, sin, code[:, None], code[None, :])


def spread(attended, weight, blocks, sizes, added, name):
    n = blocks.shape[1]
    half = LIVE // 2
    lows = [sum(sizes[:i]) for i in range(len(sizes))]
    m = len(sizes)

    def kernel(src_ref, a_ref, wa_ref, wb_ref, *refs):
        k = pl.program_id(0)
        plus = refs[: len(added)]
        outs = refs[len(added) :]
        for first, w_ref in enumerate((wa_ref, wb_ref)):
            rows = slice(first * half, (first + 1) * half)
            product = jnp.dot(a_ref[rows], w_ref[...], preferred_element_type=F32)
            for i in range(m):

                @pl.when(jnp.logical_and(k >= lows[i], k < lows[i] + sizes[i]))
                def _(i=i, first=first, product=product):
                    value = product
                    if added:
                        value = value + plus[first * m + i][...].astype(F32)
                    outs[first * m + i][...] = value.astype(BF)

    def part(i):
        return pl.BlockSpec(
            (half, FEAT), lambda k, s: (jnp.clip(k - lows[i], 0, sizes[i] - 1), 0)
        )

    parts = [part(i) for i in range(m)] * 2
    weight = in_hbm(weight)
    return pl.pallas_call(
        kernel,
        out_shape=tuple(jax.ShapeDtypeStruct((size * half, FEAT), BF) for size in sizes) * 2,
        grid_spec=pltpu.PrefetchScalarGridSpec(
            num_scalar_prefetch=1,
            grid=(n,),
            in_specs=[
                pl.BlockSpec((LIVE, FEAT), lambda k, s: (0, 0)),
                pl.BlockSpec((FEAT, FEAT), lambda k, s: (0, s[0, k])),
                pl.BlockSpec((FEAT, FEAT), lambda k, s: (0, s[1, k])),
            ]
            + (parts if added else []),
            out_specs=tuple(parts),
        ),
        compiler_params=params(16),
        cost_estimate=pl.CostEstimate(
            flops=2 * LIVE * FEAT * FEAT * n, bytes_accessed=n << 20, transcendentals=0
        ),
        name=name,
    )(blocks, attended, weight, weight, *added)


def finish_kernel(text_ref, tile_ref, sum_ref, slot_ref, o_ref):
    for r in range(REQ_GRP):
        row = slot_ref[r]
        pick = (lax.broadcasted_iota(jnp.int32, (LEN_MAX, LIVE), 1) == row).astype(BF)
        moved = jnp.dot(pick, sum_ref[...], preferred_element_type=F32)
        image = jnp.dot(pick[:, TEXT:], tile_ref[...], preferred_element_type=F32)
        base = jnp.where(row >= TEXT, image, text_ref[r].astype(F32))
        o_ref[r] = (base + moved).astype(BF)


def finish(text, tile, sums, slots):
    return pl.pallas_call(
        finish_kernel,
        out_shape=jax.ShapeDtypeStruct((REQ_GRP, LEN_MAX, FEAT), BF),
        in_specs=[vmem()] * 4,
        out_specs=vmem(),
        compiler_params=params(24),
        name="finish",
    )(text, tile, sums, slots)


def shards(
    merged,
    ln_gain,
    ln_bias,
    proj_weight,
    proj_bias,
    text_embed,
    attn_gain,
    query_weight,
    key_weight,
    value_weight,
    out_weight,
    final_gain,
    head_weight,
    lengths,
    tile_request,
    insert_pos,
):
    hid = lax.axis_index("hid")
    me = lax.axis_index("req")
    owners = tile_request // REQ_GRP
    tiles = jnp.arange(N_REQ, dtype=jnp.int32)
    tile_order = jnp.sum(
        jnp.where(owners[None, :] == tiles[:, None], tiles[None, :], 0), axis=1
    ).astype(jnp.int32)
    mine = owners == me
    local_req = jnp.sum(jnp.where(mine, tile_request % REQ_GRP, 0))
    start = jnp.sum(jnp.where(mine, insert_pos, 0))
    len_a = lengths[0]
    first = local_req * len_a + start

    n = jnp.arange(LIVE, dtype=jnp.int32)
    packed = jnp.where(n < TEXT, jnp.where(n < first, n, n + TILE), n - TEXT + first)
    second = packed >= len_a
    pos = packed - jnp.where(second, len_a, 0)
    code = pos + jnp.where(second, 1024, 0)
    flat = pos + jnp.where(second, LEN_MAX, 0)
    slot = jnp.arange(LEN_MAX, dtype=jnp.int32)
    at = jnp.stack([slot, slot + len_a])
    in_tile = jnp.logical_and(at >= first, at < first + TILE)
    row_of = jnp.where(in_tile, at - first + TEXT, jnp.where(at < first, at, at - TILE))
    row_of = jnp.where(slot[None, :] < lengths[:, None], row_of, -1)

    half_dim = HEAD_DIM // 2
    inv_freq = jnp.exp(
        jnp.arange(half_dim, dtype=F32) * (-2.0 * math.log(1000000.0) / HEAD_DIM)
    )
    angles = pos.astype(F32)[:, None] * inv_freq[None, :]
    cosine, sine = jnp.cos(angles), jnp.sin(angles)
    cos = jnp.concatenate([cosine, cosine], axis=1)
    sin = jnp.concatenate([-sine, sine], axis=1)

    x, z = hid // RING, hid % RING
    rel = jnp.arange(N_HID, dtype=jnp.int32)
    sources = ((x + rel // RING) % RING) * RING + (z + rel % RING) % RING

    near = gather_near(pack(merged, tile_order))
    merged_blocks, merged_where = gather_far(near)

    pick = (flat[:TEXT, None] == jnp.arange(REQ_GRP * LEN_MAX)[None, :]).astype(BF)
    text_rows = jnp.dot(
        pick, text_embed.reshape(REQ_GRP * LEN_MAX, FEAT), preferred_element_type=F32
    ).astype(BF)
    text_out, *_ = lax.optimization_barrier((text_rows, *near[0][1:], *near[1][1:]))
    weights = (query_weight, jnp.concatenate([key_weight, value_weight], axis=1))
    gain = attn_gain.astype(F32).reshape(N_HID, 1, FEAT)
    partner = [(i, i ^ 1) for i in range(N_HID)]
    text_blocks, text_where = gather_far(gather_near(text_out))

    projected = project(
        merged_blocks,
        merged_where,
        proj_weight,
        ln_gain.astype(F32).reshape(N_HID, 1, MFEAT),
        ln_bias.astype(F32).reshape(N_HID, 1, MFEAT),
        proj_bias[None, :],
        sources,
    )
    tile = lax.all_to_all(
        projected.reshape(N_REQ, TILE // N_REQ, FEAT), "req", split_axis=0, concat_axis=0, tiled=True
    ).reshape(TILE, FEAT)
    q_text, kv_text = qkv(
        text_blocks, text_where, weights, gain, cos[:TEXT], sin[:TEXT], sources, "qkv_text"
    )
    other_text = lax.ppermute(kv_text, "hid", partner)
    tile_near = gather_near(tile)
    tile_near, q_text = lax.optimization_barrier((tile_near, q_text))
    tile_blocks, tile_where = gather_far(tile_near)
    q_tile, kv_tile = qkv(
        tile_blocks, tile_where, weights, gain, cos[TEXT:], sin[TEXT:], sources, "qkv_tile"
    )
    other_tile = lax.ppermute(kv_tile, "hid", partner)

    low = (hid % 2 == 0).astype(jnp.int32)[None]
    attended = attend(
        low, q_text, q_tile, kv_text, other_text, kv_tile, other_tile, cos, sin, code
    )
    step = jnp.arange(RING, dtype=jnp.int32)

    def targets(outer):
        return jnp.stack([
            ((x + outer) % RING) * RING + (z + step) % RING,
            ((x + step) % RING) * RING + (z + outer) % RING,
        ])

    above, below, own_line = targets(1), targets(3), targets(0)
    far = spread(attended, out_weight, targets(2), (2, 2), (), "spread_far")
    passed = []
    for first in (0, 1):
        _, outer = axes_of(first)
        passed += [outer(far[2 * first], -1), outer(far[2 * first + 1], 1)]
    rest = spread(
        attended,
        out_weight,
        jnp.concatenate([above[:, 2:], below[:, :2], own_line], axis=1),
        (2, 2, 4),
        (),
        "spread_rest",
    )
    joined = spread(
        attended,
        out_weight,
        jnp.concatenate([above[:, :2], below[:, 2:]], axis=1),
        (2, 2),
        tuple(passed),
        "spread_joined",
    )
    last = jnp.sum(jnp.where(slot[None, :] == lengths[:, None] - 1, row_of, 0), axis=1)
    pick_last = (last[:, None] == n[None, :]).astype(BF)
    rows_last = jnp.dot(pick_last, attended, preferred_element_type=F32).astype(BF)
    term = jnp.dot(rows_last, out_weight, preferred_element_type=F32)
    base = jnp.dot(pick_last[:, :TEXT], text_rows, preferred_element_type=F32) + jnp.dot(
        pick_last[:, TEXT:], tile, preferred_element_type=F32
    )
    spot = lax.broadcasted_iota(jnp.int32, (1, N_HID, 1), 1) == hid
    term = term + jnp.where(spot, base[:, None, :], 0.0).reshape(REQ_GRP, D)
    term = over_line(term, along_z)
    term, joined = lax.optimization_barrier((term, joined))
    full_width = over_line(term, along_x).astype(BF)
    half = LIVE // 2
    lines = []
    for first in (0, 1):
        _, outer = axes_of(first)
        up_late, down_early, own_part = rest[3 * first : 3 * first + 3]
        up_early, down_late = joined[2 * first : 2 * first + 2]
        early = join(own_part[: 2 * half], outer(down_early, 1), outer(up_early, -1))
        late = join(own_part[2 * half :], outer(up_late, -1), outer(down_late, 1))
        lines.append((early[:half], early[half:].astype(BF), late[:half].astype(BF), late[half:].astype(BF)))
    both = [full_width, shift_req(full_width, 0, 1)]
    core = me % 2
    pair = jnp.stack([jnp.where(core == 0, both[0], both[1]), jnp.where(core == 0, both[1], both[0])])
    y = me // 2
    here, back, ahead, far_pair = line_of(pair, along_y)
    line = jnp.stack([here, ahead, far_pair, back])
    wanted = (step[:, None] - y) % RING == step[None, :]
    all_last = jnp.sum(
        jnp.where(wanted[:, :, None, None, None], line[None], jnp.zeros((), BF)), axis=1
    ).reshape(N_REQ * REQ_GRP, D)
    last_values = all_last.astype(F32)
    last_squares = jnp.sum(last_values * last_values, axis=1)
    final_norm = jnp.sqrt(last_squares)
    final_scaled = (
        last_values * lax.rsqrt(last_squares / D + 1e-05)[:, None] * final_gain.astype(F32)
    ).astype(BF)
    logits = lax.dot_general(
        final_scaled, head_weight, (((1,), (1,)), ((), ())), preferred_element_type=F32
    )
    top = jnp.max(logits, axis=1)
    top, lines = lax.optimization_barrier((top, lines))
    sums = []
    for first in (0, 1):
        inner, _ = axes_of(first)
        a, b, c, d = lines[first]
        sums.append(join(a, inner(b, -1), inner(c, 2), inner(d, 1)).astype(BF))
    hidden = finish(text_embed, tile, jnp.concatenate(sums, axis=0), row_of[:, :, None])
    for move in (along_z, along_x, along_y):
        here, below, above, far_top = line_of(top, move)
        top = jnp.maximum(jnp.maximum(here, below), jnp.maximum(above, far_top))
    logit_max = jnp.maximum(top, shift_req(top, 0, 1))
    return (hidden, final_norm, logit_max)


def solution(mesh):
    return jax.shard_map(
        shards,
        mesh=mesh,
        in_specs=(
            P(None, "req", "hid"),
            P(),
            P(),
            P(None, "hid"),
            P("hid"),
            P("req", None, "hid"),
            P(),
            P(None, "hid"),
            P(None, "hid"),
            P(None, "hid"),
            P("hid", None),
            P(),
            P(("req", "hid"), None),
            P("req"),
            P(),
            P(),
        ),
        out_specs=(P("req", None, "hid"), P(), P()),
        check_vma=False,
    )
```

```python
import math

import jax
import jax.numpy as jnp
from jax import lax
from jax.experimental import pallas as pl
from jax.experimental.pallas import tpu as pltpu
from jax.sharding import PartitionSpec as P

HEAD_DIM = 128
D = 6144
MERGED = 12800
REQ_GRP = 2
LEN_MAX = 480
LIVE = 640
TILE = 256
TEXT = LIVE - TILE
N_HID = 16
N_REQ = 8
RING = 4
FEAT = D // N_HID
MFEAT = MERGED // N_HID
MPAD = 896
BF = jnp.bfloat16
F32 = jnp.float32
VM = pltpu.VMEM


def vmem():
    return pl.BlockSpec(memory_space=pltpu.VMEM)


def params(mib):
    return pltpu.CompilerParams(vmem_limit_bytes=mib << 20)


def shift(block, dx, dz):
    route = []
    for i in range(N_HID):
        x, z = divmod(i, RING)
        route.append((((x + dx) % RING) * RING + (z + dz) % RING, i))
    return lax.ppermute(block, "hid", route)


def shift_req(block, dy, dc):
    route = []
    for i in range(N_REQ):
        y, c = divmod(i, 2)
        route.append((((y + dy) % RING) * 2 + (c + dc) % 2, i))
    return lax.ppermute(block, "req", route)


def line_of(block, move):
    return [block, move(block, -1), move(block, 1), move(block, 2)]


def along_x(b, d):
    return shift(b, d, 0)


def along_z(b, d):
    return shift(b, 0, d)


def along_y(b, d):
    return shift_req(b, d, 0)


def join(*blocks):
    total = blocks[0].astype(F32)
    for b in blocks[1:]:
        total = total + b.astype(F32)
    return total


def over_line(block, move):
    own, below, above, far = line_of(block, move)
    return (own + far) + (below + above)


def axes_of(first):
    return (along_z, along_x) if first == 0 else (along_x, along_z)


def gather_near(shard):
    half = shard.shape[0] // 2
    near = []
    for first in (0, 1):
        inner, outer = axes_of(first)
        own = lax.slice_in_dim(shard, first * half, (first + 1) * half, axis=0)
        group = jnp.concatenate(line_of(own, inner), axis=0)
        near.append((group, outer(group, -1), outer(group, 1)))
    return near


def gather_far(near):
    arrays, tables = [], []
    for first in (0, 1):
        _, outer = axes_of(first)
        group, minus, plus = near[first]
        half = group.shape[0] // RING
        far_a = outer(lax.slice_in_dim(minus, 0, 2 * half, axis=0), -1)
        far_b = outer(lax.slice_in_dim(plus, 2 * half, 4 * half, axis=0), 1)
        offs = [0, -1, 1, 2]
        table = {}
        for array, out, part in (
            (group, 0, offs),
            (minus, -1, offs),
            (plus, 1, offs),
            (far_a, 2, offs[:2]),
            (far_b, 2, offs[2:]),
        ):
            arrays.append(array)
            for j, d in enumerate(part):
                rel = (out % RING, d % RING) if first == 0 else (d % RING, out % RING)
                table[rel] = (len(arrays) - 1, j * half)
        tables.append(table)
    order = [(dx, dz) for dx in range(RING) for dz in range(RING)]
    return arrays, [(tables[0][r], tables[1][r]) for r in order]


def in_hbm(x):
    return pltpu.with_memory_space_constraint(x, pltpu.HBM)


def pack_kernel(order_ref, x_ref, o_ref):
    for g in range(N_REQ):
        rows = x_ref[order_ref[g]]
        v = rows.astype(F32)
        stats = []
        for s in (jnp.sum(v, axis=1, keepdims=True), jnp.sum(v * v, axis=1, keepdims=True)):
            for _ in range(3):
                part = s.astype(BF)
                stats.append(part)
                s = s - part.astype(F32)
        lo, hi = g * 32, (g + 1) * 32
        lane = lax.broadcasted_iota(jnp.int32, (32, MPAD - 768), 1)
        tail = jnp.zeros((32, MPAD - 768), F32)
        for j, part in enumerate(stats):
            tail = jnp.where(lane == 32 + j, part.astype(F32), tail)
        o_ref[lo:hi, 0:768] = rows[:, 0:768]
        o_ref[lo:hi, 768:MPAD] = tail.astype(BF)
        o_ref[lo:hi, 768:800] = rows[:, 768:800]


def pack(merged, tile_order):
    return pl.pallas_call(
        pack_kernel,
        out_shape=jax.ShapeDtypeStruct((TILE, MPAD), BF),
        in_specs=[pl.BlockSpec(memory_space=pltpu.SMEM), vmem()],
        out_specs=vmem(),
        compiler_params=params(16),
        name="pack",
    )(tile_order, merged)


def project_kernel(x_hbm, w_hbm, g_ref, b_ref, pb_ref, o_ref, x, w, acc, x_sem, w_sem):
    def x_copy(k):
        rows = pl.ds(k * TILE, TILE)
        return pltpu.make_async_copy(x_hbm.at[rows, :], x.at[k], x_sem.at[k])

    def w_copy(k):
        rows = pl.ds(k * MFEAT, MFEAT)
        return pltpu.make_async_copy(w_hbm.at[rows, :], w.at[k], w_sem.at[k])

    for k in range(N_HID):
        x_copy(k).start()
    for k in range(N_HID):
        w_copy(k).start()
    total = jnp.zeros((TILE, 128), F32)
    for k in range(N_HID):
        x_copy(k).wait()
        total = total + x[k, :, 768:MPAD].astype(F32)
    mean = jnp.sum(total[:, 32:35], axis=1, keepdims=True) * (1.0 / MERGED)
    square = jnp.sum(total[:, 35:38], axis=1, keepdims=True) * (1.0 / MERGED)
    rstd = lax.rsqrt(square - mean * mean + 1e-05)
    acc[...] = jnp.zeros_like(acc)

    def step(i, carry):
        parts = []
        for j in (0, 1):
            k = 2 * i + j
            w_copy(k).wait()
            v = x[k, :, 0:MFEAT].astype(F32)
            normed = (v - mean) * rstd * g_ref[k] + b_ref[k]
            parts.append(jnp.dot(normed.astype(BF), w[k], preferred_element_type=F32))
        acc[...] += parts[0] + parts[1]
        return carry

    lax.fori_loop(0, N_HID // 2, step, 0)
    y = acc[...] + pb_ref[...]
    y = 0.5 * y * (1.0 + lax.erf(y * math.sqrt(0.5)))
    o_ref[...] = y.astype(BF)


def project(gathered, weight, gain, bias, out_bias):
    return pl.pallas_call(
        project_kernel,
        out_shape=jax.ShapeDtypeStruct((TILE, FEAT), BF),
        in_specs=[pl.BlockSpec(memory_space=pl.ANY)] * 2 + [vmem()] * 3,
        out_specs=vmem(),
        scratch_shapes=[
            VM((N_HID, TILE, MPAD), BF),
            VM((N_HID, MFEAT, FEAT), BF),
            VM((TILE, FEAT), F32),
            pltpu.SemaphoreType.DMA((N_HID,)),
            pltpu.SemaphoreType.DMA((N_HID,)),
        ],
        compiler_params=params(28),
        cost_estimate=pl.CostEstimate(
            flops=2 * TILE * MERGED * FEAT, bytes_accessed=17 << 20, transcendentals=0
        ),
        name="project",
    )(in_hbm(gathered), in_hbm(weight), gain, bias, out_bias)


def turn(v, cos, sin):
    return v * cos + pltpu.roll(v, HEAD_DIM // 2, 1) * sin


def qkv(arrays, where, weight, cos, sin, sources, name):
    half = arrays[0].shape[0] // RING
    rows = 2 * half
    n = len(arrays)
    deep = 4 * FEAT
    cols = FEAT + HEAD_DIM

    def kernel(src_ref, *refs):
        ins = refs[:n]
        w_hbm, cos_ref, sin_ref, q_ref, kv_ref, xs, w, acc, sem = refs[n:]

        def copy(k):
            there = pl.ds(pl.multiple_of(src_ref[k] * FEAT, FEAT), FEAT)
            here = pl.ds(k * FEAT, FEAT)
            return pltpu.make_async_copy(w_hbm.at[there, :], w.at[here, :], sem.at[k])

        for k in range(N_HID):
            copy(k).start()
        square = jnp.zeros((rows, HEAD_DIM), F32)
        for k in range(N_HID):
            block = jnp.concatenate([ins[a][row : row + half, :] for a, row in where[k]], axis=0)
            xs[:, k * FEAT : (k + 1) * FEAT] = block
            v = block.astype(F32)
            v = v * v
            square = square + (v[:, 0:128] + v[:, 128:256] + v[:, 256:384])
        acc[...] = jnp.zeros_like(acc)

        def step(i, carry):
            for j in range(4):
                copy(4 * i + j).wait()
            here = pl.ds(pl.multiple_of(i * deep, deep), deep)
            acc[...] += jnp.dot(xs[:, here], w[here, :], preferred_element_type=F32)
            return carry

        lax.fori_loop(0, RING, step, 0)
        scale = lax.rsqrt(jnp.sum(square, axis=1, keepdims=True) * (1.0 / D) + 1e-05)
        for h in range(FEAT // HEAD_DIM):
            part = acc[:, h * HEAD_DIM : (h + 1) * HEAD_DIM] * scale
            q_ref[:, h * HEAD_DIM : (h + 1) * HEAD_DIM] = turn(
                part, cos_ref[...], sin_ref[...]
            ).astype(BF)
        kv_ref[...] = (acc[:, FEAT:] * scale).astype(BF)

    return pl.pallas_call(
        kernel,
        out_shape=(
            jax.ShapeDtypeStruct((rows, FEAT), BF),
            jax.ShapeDtypeStruct((rows, HEAD_DIM), BF),
        ),
        in_specs=[pl.BlockSpec(memory_space=pltpu.SMEM)]
        + [vmem() for _ in arrays]
        + [pl.BlockSpec(memory_space=pl.ANY), vmem(), vmem()],
        out_specs=(vmem(), vmem()),
        scratch_shapes=[
            VM((rows, D), BF),
            VM((D, cols), BF),
            VM((rows, cols), F32),
            pltpu.SemaphoreType.DMA((N_HID,)),
        ],
        compiler_params=params(20),
        cost_estimate=pl.CostEstimate(
            flops=2 * rows * D * cols, bytes_accessed=12 << 20, transcendentals=0
        ),
        name=name,
    )(sources, *arrays, in_hbm(weight), cos, sin)


def attend_kernel(
    low_ref, qt, qi, ot, pt, oi, pi, cos_ref, sin_ref, row_ref, col_ref, o_ref, keys, vals
):
    upper = low_ref[0] == 0
    lane = lax.broadcasted_iota(jnp.int32, (LIVE, HEAD_DIM), 1)
    own = jnp.concatenate([ot[...], oi[...]], axis=0).astype(F32)
    other = jnp.concatenate([pt[...], pi[...]], axis=0).astype(F32)
    low = jnp.where(upper, other, own)
    high = jnp.where(upper, own, other)
    key = jnp.where(lane < 64, low, pltpu.roll(high, 64, 1))
    val = jnp.where(lane < 64, pltpu.roll(low, 64, 1), high)
    keys[...] = turn(key, cos_ref[...], sin_ref[...]).astype(BF)
    vals[...] = val.astype(BF)
    code = col_ref[...]
    for blk in range(LIVE // 128):
        rows = slice(blk * 128, (blk + 1) * 128)
        mine = row_ref[rows, :]
        start = jnp.where(mine >= 1024, 1024, 0)
        live = jnp.logical_and(code <= mine, code >= start)
        for h in range(FEAT // HEAD_DIM):
            cols = slice(h * HEAD_DIM, (h + 1) * HEAD_DIM)
            if blk < TEXT // 128:
                q = qt[rows, cols]
            else:
                q = qi[blk * 128 - TEXT : blk * 128 - TEXT + 128, cols]
            s = lax.dot_general(
                q, keys[...], (((1,), (1,)), ((), ())), preferred_element_type=F32
            ) * (1.0 / math.sqrt(HEAD_DIM))
            s = jnp.where(live, s, -jnp.inf)
            w = jnp.exp(s - jnp.max(s, axis=1, keepdims=True))
            total = jnp.sum(w, axis=1, keepdims=True)
            mixed = jnp.dot(w.astype(BF), vals[...], preferred_element_type=F32)
            o_ref[rows, cols] = (mixed / total).astype(BF)


def attend(low, qt, qi, ot, pt, oi, pi, cos, sin, code):
    return pl.pallas_call(
        attend_kernel,
        out_shape=jax.ShapeDtypeStruct((LIVE, FEAT), BF),
        in_specs=[pl.BlockSpec(memory_space=pltpu.SMEM)] + [vmem()] * 10,
        out_specs=vmem(),
        scratch_shapes=[VM((LIVE, HEAD_DIM), BF), VM((LIVE, HEAD_DIM), BF)],
        compiler_params=params(24),
        cost_estimate=pl.CostEstimate(flops=1 << 30, bytes_accessed=2 << 20, transcendentals=0),
        name="attend",
    )(low, qt, qi, ot, pt, oi, pi, cos, sin, code[:, None], code[None, :])


def spread_kernel(a_ref, w_hbm, o_ref, w, sem):
    k = pl.program_id(0)
    two = 2 * FEAT

    def copy(i):
        cols = pl.ds(pl.multiple_of(i * two, two), two)
        return pltpu.make_async_copy(w_hbm.at[:, cols], w.at[i], sem.at[i])

    @pl.when(k == 0)
    def _():
        for i in range(N_HID // 2):
            copy(i).start()

    copy(k).wait()
    product = jnp.dot(a_ref[...], w[k], preferred_element_type=F32).astype(BF)
    o_ref[0] = product[:, :FEAT]
    o_ref[1] = product[:, FEAT:]


def spread(attended, weight):
    return pl.pallas_call(
        spread_kernel,
        out_shape=jax.ShapeDtypeStruct((N_HID, LIVE, FEAT), BF),
        grid=(N_HID // 2,),
        in_specs=[
            pl.BlockSpec(memory_space=pltpu.VMEM),
            pl.BlockSpec(memory_space=pl.ANY),
        ],
        out_specs=pl.BlockSpec((2, LIVE, FEAT), lambda k: (k, 0, 0)),
        scratch_shapes=[
            VM((N_HID // 2, FEAT, 2 * FEAT), BF),
            pltpu.SemaphoreType.DMA((N_HID // 2,)),
        ],
        compiler_params=params(58),
        cost_estimate=pl.CostEstimate(
            flops=2 * LIVE * FEAT * D, bytes_accessed=13 << 20, transcendentals=0
        ),
        name="spread",
    )(attended, in_hbm(weight))


def finish_kernel(text_ref, tile_ref, sum_ref, slot_ref, o_ref):
    for r in range(REQ_GRP):
        row = slot_ref[r]
        pick = (lax.broadcasted_iota(jnp.int32, (LEN_MAX, LIVE), 1) == row).astype(BF)
        moved = jnp.dot(pick, sum_ref[...], preferred_element_type=F32)
        image = jnp.dot(pick[:, TEXT:], tile_ref[...], preferred_element_type=F32)
        base = jnp.where(row >= TEXT, image, text_ref[r].astype(F32))
        o_ref[r] = (base + moved).astype(BF)


def finish(text, tile, sums, slots):
    return pl.pallas_call(
        finish_kernel,
        out_shape=jax.ShapeDtypeStruct((REQ_GRP, LEN_MAX, FEAT), BF),
        in_specs=[vmem()] * 4,
        out_specs=vmem(),
        compiler_params=params(24),
        name="finish",
    )(text, tile, sums, slots)


def shards(
    merged,
    ln_gain,
    ln_bias,
    proj_weight,
    proj_bias,
    text_embed,
    attn_gain,
    query_weight,
    key_weight,
    value_weight,
    out_weight,
    final_gain,
    head_weight,
    lengths,
    tile_request,
    insert_pos,
):
    hid = lax.axis_index("hid")
    me = lax.axis_index("req")
    owners = tile_request // REQ_GRP
    tiles = jnp.arange(N_REQ, dtype=jnp.int32)
    tile_order = jnp.sum(
        jnp.where(owners[None, :] == tiles[:, None], tiles[None, :], 0), axis=1
    ).astype(jnp.int32)
    mine = owners == me
    local_req = jnp.sum(jnp.where(mine, tile_request % REQ_GRP, 0))
    start = jnp.sum(jnp.where(mine, insert_pos, 0))
    len_a = lengths[0]
    first = local_req * len_a + start

    n = jnp.arange(LIVE, dtype=jnp.int32)
    packed = jnp.where(n < TEXT, jnp.where(n < first, n, n + TILE), n - TEXT + first)
    second = packed >= len_a
    pos = packed - jnp.where(second, len_a, 0)
    code = pos + jnp.where(second, 1024, 0)
    flat = pos + jnp.where(second, LEN_MAX, 0)
    slot = jnp.arange(LEN_MAX, dtype=jnp.int32)
    at = jnp.stack([slot, slot + len_a])
    in_tile = jnp.logical_and(at >= first, at < first + TILE)
    row_of = jnp.where(in_tile, at - first + TEXT, jnp.where(at < first, at, at - TILE))
    row_of = jnp.where(slot[None, :] < lengths[:, None], row_of, -1)

    half_dim = HEAD_DIM // 2
    inv_freq = jnp.exp(
        jnp.arange(half_dim, dtype=F32) * (-2.0 * math.log(1000000.0) / HEAD_DIM)
    )
    angles = pos.astype(F32)[:, None] * inv_freq[None, :]
    cosine, sine = jnp.cos(angles), jnp.sin(angles)
    cos = jnp.concatenate([cosine, cosine], axis=1)
    sin = jnp.concatenate([-sine, sine], axis=1)

    x, z = hid // RING, hid % RING
    rel = jnp.arange(N_HID, dtype=jnp.int32)
    sources = ((x + rel // RING) % RING) * RING + (z + rel % RING) % RING

    gathered = lax.all_gather(pack(merged, tile_order), "hid", axis=0, tiled=True)

    pick = (flat[:TEXT, None] == jnp.arange(REQ_GRP * LEN_MAX)[None, :]).astype(BF)
    text_rows = jnp.dot(
        pick, text_embed.reshape(REQ_GRP * LEN_MAX, FEAT), preferred_element_type=F32
    ).astype(BF)
    weight = (
        jnp.concatenate([query_weight, key_weight, value_weight], axis=1).astype(F32)
        * attn_gain.astype(F32)[:, None]
    ).astype(BF)
    partner = [(i, i ^ 1) for i in range(N_HID)]
    text_blocks, text_where = gather_far(gather_near(text_rows))
    q_text, kv_text = qkv(
        text_blocks, text_where, weight, cos[:TEXT], sin[:TEXT], sources, "qkv_text"
    )
    gathered, q_text, kv_text = lax.optimization_barrier((gathered, q_text, kv_text))
    projected = project(
        gathered,
        proj_weight,
        ln_gain.astype(F32).reshape(N_HID, 1, MFEAT),
        ln_bias.astype(F32).reshape(N_HID, 1, MFEAT),
        proj_bias[None, :],
    )
    tile = lax.all_to_all(
        projected.reshape(N_REQ, TILE // N_REQ, FEAT), "req", split_axis=0, concat_axis=0, tiled=True
    ).reshape(TILE, FEAT)
    other_text = lax.ppermute(kv_text, "hid", partner)
    tile_blocks, tile_where = gather_far(gather_near(tile))
    q_tile, kv_tile = qkv(
        tile_blocks, tile_where, weight, cos[TEXT:], sin[TEXT:], sources, "qkv_tile"
    )
    other_tile = lax.ppermute(kv_tile, "hid", partner)

    low = (hid % 2 == 0).astype(jnp.int32)[None]
    attended = attend(
        low, q_text, q_tile, kv_text, other_text, kv_tile, other_tile, cos, sin, code
    )
    step = jnp.arange(RING, dtype=jnp.int32)
    partial = spread(attended, out_weight)
    partial, attended = lax.optimization_barrier((partial, attended))
    sums = lax.psum_scatter(
        partial.reshape(N_HID * LIVE, FEAT), "hid", scatter_dimension=0, tiled=True
    )
    hidden = finish(text_embed, tile, sums, row_of[:, :, None])

    last = jnp.sum(jnp.where(slot[None, :] == lengths[:, None] - 1, row_of, 0), axis=1)
    pick_last = (last[:, None] == n[None, :]).astype(BF)
    rows_last = jnp.dot(pick_last, attended, preferred_element_type=F32).astype(BF)
    term = jnp.dot(rows_last, out_weight, preferred_element_type=F32)
    base = jnp.dot(pick_last[:, :TEXT], text_rows, preferred_element_type=F32) + jnp.dot(
        pick_last[:, TEXT:], tile, preferred_element_type=F32
    )
    spot = lax.broadcasted_iota(jnp.int32, (1, N_HID, 1), 1) == hid
    term = term + jnp.where(spot, base[:, None, :], 0.0).reshape(REQ_GRP, D)
    term = over_line(term, along_z)
    full_width = over_line(term, along_x).astype(BF)
    both = [full_width, shift_req(full_width, 0, 1)]
    core = me % 2
    pair = jnp.stack([jnp.where(core == 0, both[0], both[1]), jnp.where(core == 0, both[1], both[0])])
    y = me // 2
    here, back, ahead, far_pair = line_of(pair, along_y)
    line = jnp.stack([here, ahead, far_pair, back])
    wanted = (step[:, None] - y) % RING == step[None, :]
    all_last = jnp.sum(
        jnp.where(wanted[:, :, None, None, None], line[None], jnp.zeros((), BF)), axis=1
    ).reshape(N_REQ * REQ_GRP, D)
    last_values = all_last.astype(F32)
    last_squares = jnp.sum(last_values * last_values, axis=1)
    final_norm = jnp.sqrt(last_squares)
    final_scaled = (
        last_values * lax.rsqrt(last_squares / D + 1e-05)[:, None] * final_gain.astype(F32)
    ).astype(BF)
    logits = lax.dot_general(
        final_scaled, head_weight, (((1,), (1,)), ((), ())), preferred_element_type=F32
    )
    top = jnp.max(logits, axis=1)
    for move in (along_z, along_x, along_y):
        here, below, above, far_top = line_of(top, move)
        top = jnp.maximum(jnp.maximum(here, below), jnp.maximum(above, far_top))
    logit_max = jnp.maximum(top, shift_req(top, 0, 1))
    return (hidden, final_norm, logit_max)


def solution(mesh):
    return jax.shard_map(
        shards,
        mesh=mesh,
        in_specs=(
            P(None, "req", "hid"),
            P(),
            P(),
            P(None, "hid"),
            P("hid"),
            P("req", None, "hid"),
            P(),
            P(None, "hid"),
            P(None, "hid"),
            P(None, "hid"),
            P("hid", None),
            P(),
            P(("req", "hid"), None),
            P("req"),
            P(),
            P(),
        ),
        out_specs=(P("req", None, "hid"), P(), P()),
        check_vma=False,
    )
```

```python
import math

import jax
import jax.numpy as jnp
from jax import lax
from jax.experimental import pallas as pl
from jax.experimental.pallas import tpu as pltpu
from jax.sharding import PartitionSpec as P

HEAD_DIM = 128
D = 6144
MERGED = 12800
REQ_GRP = 2
LEN_MAX = 480
LIVE = 640
TILE = 256
TEXT = LIVE - TILE
N_HID = 16
N_REQ = 8
RING = 4
FEAT = D // N_HID
MFEAT = MERGED // N_HID
MAIN = 768
MPAD = 896
BF = jnp.bfloat16
F32 = jnp.float32
VM = pltpu.VMEM


def vmem():
    return pl.BlockSpec(memory_space=pltpu.VMEM)


def params(mib):
    return pltpu.CompilerParams(vmem_limit_bytes=mib << 20)


def shift(block, dx, dz):
    route = []
    for i in range(N_HID):
        x, z = divmod(i, RING)
        route.append((((x + dx) % RING) * RING + (z + dz) % RING, i))
    return lax.ppermute(block, "hid", route)


def shift_req(block, dy, dc):
    route = []
    for i in range(N_REQ):
        y, c = divmod(i, 2)
        route.append((((y + dy) % RING) * 2 + (c + dc) % 2, i))
    return lax.ppermute(block, "req", route)


def line_of(block, move):
    return [block, move(block, -1), move(block, 1), move(block, 2)]


def along_x(b, d):
    return shift(b, d, 0)


def along_z(b, d):
    return shift(b, 0, d)


def along_y(b, d):
    return shift_req(b, d, 0)


def join(*blocks):
    total = blocks[0].astype(F32)
    for b in blocks[1:]:
        total = total + b.astype(F32)
    return total


def over_line(block, move):
    own, below, above, far = line_of(block, move)
    return (own + far) + (below + above)


def axes_of(first):
    return (along_z, along_x) if first == 0 else (along_x, along_z)


def gather_near(shard):
    half = shard.shape[0] // 2
    near = []
    for first in (0, 1):
        inner, outer = axes_of(first)
        own = lax.slice_in_dim(shard, first * half, (first + 1) * half, axis=0)
        group = jnp.concatenate(line_of(own, inner), axis=0)
        near.append((group, outer(group, -1), outer(group, 1)))
    return near


def gather_far(near, relay=True):
    arrays, tables = [], []
    for first in (0, 1):
        _, outer = axes_of(first)
        group, minus, plus = near[first]
        half = group.shape[0] // RING
        offs = [0, -1, 1, 2]
        if relay:
            far_a = outer(lax.slice_in_dim(minus, 0, 2 * half, axis=0), -1)
            far_b = outer(lax.slice_in_dim(plus, 2 * half, 4 * half, axis=0), 1)
            far = [(far_a, 2, offs[:2]), (far_b, 2, offs[2:])]
        else:
            far = [(outer(group, 2), 2, offs)]
        table = {}
        for array, out, part in [
            (group, 0, offs),
            (minus, -1, offs),
            (plus, 1, offs),
        ] + far:
            arrays.append(array)
            for j, d in enumerate(part):
                rel = (out % RING, d % RING) if first == 0 else (d % RING, out % RING)
                table[rel] = (len(arrays) - 1, j * half)
        tables.append(table)
    order = [(dx, dz) for dx in range(RING) for dz in range(RING)]
    return arrays, [(tables[0][r], tables[1][r]) for r in order]


def in_hbm(x):
    return pltpu.with_memory_space_constraint(x, pltpu.HBM)


def pack_kernel(order_ref, place_ref, x_ref, o_ref, tail):
    for g in range(N_REQ):
        rows = x_ref[order_ref[g]]
        v = rows.astype(F32)
        lo, hi = g * 32, (g + 1) * 32
        lane = lax.broadcasted_iota(jnp.int32, (32, 128), 1)
        block = jnp.zeros((32, 128), F32)
        j = 32
        for s in (jnp.sum(v, axis=1, keepdims=True), jnp.sum(v * v, axis=1, keepdims=True)):
            for _ in range(3):
                part = s.astype(BF).astype(F32)
                block = jnp.where(lane == j, part, block)
                s = s - part
                j += 1
        o_ref[lo:hi, 0:MAIN] = rows[:, 0:MAIN]
        tail[lo:hi, :] = block
        tail[lo:hi, 0:32] = v[:, MAIN:MFEAT]
    o_ref[:, MAIN:MPAD] = pltpu.roll(tail[...], place_ref[0] * 32, 1).astype(BF)


def pack(merged, tile_order, place):
    return pl.pallas_call(
        pack_kernel,
        out_shape=jax.ShapeDtypeStruct((TILE, MPAD), BF),
        in_specs=[pl.BlockSpec(memory_space=pltpu.SMEM)] * 2 + [vmem()],
        out_specs=vmem(),
        scratch_shapes=[VM((TILE, 128), F32)],
        compiler_params=params(16),
        name="pack",
    )(tile_order, place, merged)


def project_kernel(
    x_hbm, w_hbm, g_ref, b_ref, gl_ref, bl_ref, pb_ref, o_ref, tail, x, w, wl, acc, sem, x_sem, w_sem
):
    deep = 2 * MAIN
    tails = pltpu.make_async_copy(x_hbm.at[:, pl.ds(MAIN, 128)], tail, sem.at[0])
    lefts = pltpu.make_async_copy(w_hbm.at[:, pl.ds(MAIN, 32), :], wl, sem.at[1])

    def x_copy(k):
        here = pl.ds(pl.multiple_of(k * MAIN, MAIN), MAIN)
        there = x_hbm.at[pl.ds(k * TILE, TILE), pl.ds(0, MAIN)]
        return pltpu.make_async_copy(there, x.at[:, here], x_sem.at[k])

    def w_copy(k):
        here = pl.ds(k * MAIN, MAIN)
        return pltpu.make_async_copy(w_hbm.at[k, pl.ds(0, MAIN), :], w.at[here, :], w_sem.at[k])

    tails.start()
    for k in range(N_HID):
        x_copy(k).start()
        w_copy(k).start()
    lefts.start()
    tails.wait()
    quarter = lax.broadcasted_iota(jnp.int32, (TILE, 128), 1) // 32
    mean = jnp.zeros((TILE, 1), F32)
    square = jnp.zeros((TILE, 1), F32)
    for j in range(RING):
        total = jnp.zeros((TILE, 128), F32)
        for i in range(RING):
            k = RING * i + j
            total = total + tail[k * TILE : (k + 1) * TILE, :].astype(F32)
        at = 32 * ((j + 1) % RING)
        mean = mean + jnp.sum(total[:, at : at + 3], axis=1, keepdims=True)
        square = square + jnp.sum(total[:, at + 3 : at + 6], axis=1, keepdims=True)
    mean = mean * (1.0 / MERGED)
    rstd = lax.rsqrt(square * (1.0 / MERGED) - mean * mean + 1e-05)
    acc[...] = jnp.zeros_like(acc)

    def step(i, carry):
        for j in (0, 1):
            x_copy(2 * i + j).wait()
            w_copy(2 * i + j).wait()
        here = pl.ds(pl.multiple_of(i * deep, deep), deep)
        v = x[:, here].astype(F32)
        normed = (v - mean) * rstd * g_ref[i] + b_ref[i]
        acc[...] += jnp.dot(normed.astype(BF), w[here, :], preferred_element_type=F32)
        return carry

    lax.fori_loop(0, N_HID // 2, step, 0)
    lefts.wait()
    blocks = []
    for i in range(RING):
        v = jnp.zeros((TILE, 128), F32)
        for j in range(RING):
            k = RING * i + j
            v = jnp.where(quarter == j, tail[k * TILE : (k + 1) * TILE, :].astype(F32), v)
        blocks.append(((v - mean) * rstd * gl_ref[i] + bl_ref[i]).astype(BF))
    rest = jnp.concatenate(blocks, axis=1)
    y = acc[...] + pb_ref[...] + jnp.dot(
        rest, wl[...].reshape(N_HID * 32, FEAT), preferred_element_type=F32
    )
    y = 0.5 * y * (1.0 + lax.erf(y * math.sqrt(0.5)))
    o_ref[...] = y.astype(BF)


def project(gathered, weight, gain, bias, out_bias):
    def parts(v):
        v = v.astype(F32).reshape(N_HID, MFEAT)
        return (
            v[:, :MAIN].reshape(N_HID // 2, 1, 2 * MAIN),
            v[:, MAIN:].reshape(RING, 1, 128),
        )

    gain, gain_left = parts(gain)
    bias, bias_left = parts(bias)
    return pl.pallas_call(
        project_kernel,
        out_shape=jax.ShapeDtypeStruct((TILE, FEAT), BF),
        in_specs=[pl.BlockSpec(memory_space=pl.ANY)] * 2 + [vmem()] * 5,
        out_specs=vmem(),
        scratch_shapes=[
            VM((N_HID * TILE, 128), BF),
            VM((TILE, N_HID * MAIN), BF),
            VM((N_HID * MAIN, FEAT), BF),
            VM((N_HID, 32, FEAT), BF),
            VM((TILE, FEAT), F32),
            pltpu.SemaphoreType.DMA((2,)),
            pltpu.SemaphoreType.DMA((N_HID,)),
            pltpu.SemaphoreType.DMA((N_HID,)),
        ],
        compiler_params=params(30),
        cost_estimate=pl.CostEstimate(
            flops=2 * TILE * MERGED * FEAT, bytes_accessed=17 << 20, transcendentals=0
        ),
        name="project",
    )(
        in_hbm(gathered),
        in_hbm(weight.reshape(N_HID, MFEAT, FEAT)),
        gain,
        bias,
        gain_left,
        bias_left,
        out_bias,
    )


def turn(v, cos, sin):
    return v * cos + pltpu.roll(v, HEAD_DIM // 2, 1) * sin


def qkv(arrays, where, weight, cos, sin, sources, name):
    half = arrays[0].shape[0] // RING
    rows = 2 * half
    n = len(arrays)
    deep = 4 * FEAT
    cols = FEAT + HEAD_DIM

    def kernel(src_ref, *refs):
        ins = refs[:n]
        w_hbm, cos_ref, sin_ref, q_ref, kv_ref, xs, w, acc, sem = refs[n:]

        def copy(k):
            there = pl.ds(pl.multiple_of(src_ref[k] * FEAT, FEAT), FEAT)
            here = pl.ds(k * FEAT, FEAT)
            return pltpu.make_async_copy(w_hbm.at[there, :], w.at[here, :], sem.at[k])

        for k in range(N_HID):
            copy(k).start()
        square = jnp.zeros((rows, HEAD_DIM), F32)
        for k in range(N_HID):
            block = jnp.concatenate([ins[a][row : row + half, :] for a, row in where[k]], axis=0)
            xs[:, k * FEAT : (k + 1) * FEAT] = block
            v = block.astype(F32)
            v = v * v
            square = square + (v[:, 0:128] + v[:, 128:256] + v[:, 256:384])
        acc[...] = jnp.zeros_like(acc)

        def step(i, carry):
            for j in range(4):
                copy(4 * i + j).wait()
            here = pl.ds(pl.multiple_of(i * deep, deep), deep)
            acc[...] += jnp.dot(xs[:, here], w[here, :], preferred_element_type=F32)
            return carry

        lax.fori_loop(0, RING, step, 0)
        scale = lax.rsqrt(jnp.sum(square, axis=1, keepdims=True) * (1.0 / D) + 1e-05)
        for h in range(FEAT // HEAD_DIM):
            part = acc[:, h * HEAD_DIM : (h + 1) * HEAD_DIM] * scale
            q_ref[:, h * HEAD_DIM : (h + 1) * HEAD_DIM] = turn(
                part, cos_ref[...], sin_ref[...]
            ).astype(BF)
        kv_ref[...] = (acc[:, FEAT:] * scale).astype(BF)

    return pl.pallas_call(
        kernel,
        out_shape=(
            jax.ShapeDtypeStruct((rows, FEAT), BF),
            jax.ShapeDtypeStruct((rows, HEAD_DIM), BF),
        ),
        in_specs=[pl.BlockSpec(memory_space=pltpu.SMEM)]
        + [vmem() for _ in arrays]
        + [pl.BlockSpec(memory_space=pl.ANY), vmem(), vmem()],
        out_specs=(vmem(), vmem()),
        scratch_shapes=[
            VM((rows, D), BF),
            VM((D, cols), BF),
            VM((rows, cols), F32),
            pltpu.SemaphoreType.DMA((N_HID,)),
        ],
        compiler_params=params(20),
        cost_estimate=pl.CostEstimate(
            flops=2 * rows * D * cols, bytes_accessed=12 << 20, transcendentals=0
        ),
        name=name,
    )(sources, *arrays, in_hbm(weight), cos, sin)


def attend_kernel(
    low_ref, qt, qi, ot, pt, oi, pi, cos_ref, sin_ref, row_ref, col_ref, o_ref, keys, vals
):
    upper = low_ref[0] == 0
    lane = lax.broadcasted_iota(jnp.int32, (LIVE, HEAD_DIM), 1)
    own = jnp.concatenate([ot[...], oi[...]], axis=0).astype(F32)
    other = jnp.concatenate([pt[...], pi[...]], axis=0).astype(F32)
    low = jnp.where(upper, other, own)
    high = jnp.where(upper, own, other)
    key = jnp.where(lane < 64, low, pltpu.roll(high, 64, 1))
    val = jnp.where(lane < 64, pltpu.roll(low, 64, 1), high)
    keys[...] = turn(key, cos_ref[...], sin_ref[...]).astype(BF)
    vals[...] = val.astype(BF)
    code = col_ref[...]
    for blk in range(LIVE // 128):
        rows = slice(blk * 128, (blk + 1) * 128)
        mine = row_ref[rows, :]
        start = jnp.where(mine >= 1024, 1024, 0)
        live = jnp.logical_and(code <= mine, code >= start)
        for h in range(FEAT // HEAD_DIM):
            cols = slice(h * HEAD_DIM, (h + 1) * HEAD_DIM)
            if blk < TEXT // 128:
                q = qt[rows, cols]
            else:
                q = qi[blk * 128 - TEXT : blk * 128 - TEXT + 128, cols]
            s = lax.dot_general(
                q, keys[...], (((1,), (1,)), ((), ())), preferred_element_type=F32
            ) * (1.0 / math.sqrt(HEAD_DIM))
            s = jnp.where(live, s, -jnp.inf)
            w = jnp.exp(s - jnp.max(s, axis=1, keepdims=True))
            total = jnp.sum(w, axis=1, keepdims=True)
            mixed = jnp.dot(w.astype(BF), vals[...], preferred_element_type=F32)
            o_ref[rows, cols] = (mixed / total).astype(BF)


def attend(low, qt, qi, ot, pt, oi, pi, cos, sin, code):
    return pl.pallas_call(
        attend_kernel,
        out_shape=jax.ShapeDtypeStruct((LIVE, FEAT), BF),
        in_specs=[pl.BlockSpec(memory_space=pltpu.SMEM)] + [vmem()] * 10,
        out_specs=vmem(),
        scratch_shapes=[VM((LIVE, HEAD_DIM), BF), VM((LIVE, HEAD_DIM), BF)],
        compiler_params=params(24),
        cost_estimate=pl.CostEstimate(flops=1 << 30, bytes_accessed=2 << 20, transcendentals=0),
        name="attend",
    )(low, qt, qi, ot, pt, oi, pi, cos, sin, code[:, None], code[None, :])


def spread_kernel(a_ref, w_hbm, o_ref, w, sem):
    k = pl.program_id(0)
    two = 2 * FEAT

    def copy(i):
        cols = pl.ds(pl.multiple_of(i * two, two), two)
        return pltpu.make_async_copy(w_hbm.at[:, cols], w.at[i], sem.at[i])

    @pl.when(k == 0)
    def _():
        for i in range(N_HID // 2):
            copy(i).start()

    copy(k).wait()
    product = jnp.dot(a_ref[...], w[k], preferred_element_type=F32).astype(BF)
    o_ref[0] = product[:, :FEAT]
    o_ref[1] = product[:, FEAT:]


def spread(attended, weight):
    return pl.pallas_call(
        spread_kernel,
        out_shape=jax.ShapeDtypeStruct((N_HID, LIVE, FEAT), BF),
        grid=(N_HID // 2,),
        in_specs=[
            pl.BlockSpec(memory_space=pltpu.VMEM),
            pl.BlockSpec(memory_space=pl.ANY),
        ],
        out_specs=pl.BlockSpec((2, LIVE, FEAT), lambda k: (k, 0, 0)),
        scratch_shapes=[
            VM((N_HID // 2, FEAT, 2 * FEAT), BF),
            pltpu.SemaphoreType.DMA((N_HID // 2,)),
        ],
        compiler_params=params(58),
        cost_estimate=pl.CostEstimate(
            flops=2 * LIVE * FEAT * D, bytes_accessed=13 << 20, transcendentals=0
        ),
        name="spread",
    )(attended, in_hbm(weight))


def finish_kernel(text_ref, tile_ref, sum_ref, slot_ref, o_ref):
    for r in range(REQ_GRP):
        row = slot_ref[r]
        pick = (lax.broadcasted_iota(jnp.int32, (LEN_MAX, LIVE), 1) == row).astype(BF)
        moved = jnp.dot(pick, sum_ref[...], preferred_element_type=F32)
        image = jnp.dot(pick[:, TEXT:], tile_ref[...], preferred_element_type=F32)
        base = jnp.where(row >= TEXT, image, text_ref[r].astype(F32))
        o_ref[r] = (base + moved).astype(BF)


def finish(text, tile, sums, slots):
    return pl.pallas_call(
        finish_kernel,
        out_shape=jax.ShapeDtypeStruct((REQ_GRP, LEN_MAX, FEAT), BF),
        in_specs=[vmem()] * 4,
        out_specs=vmem(),
        compiler_params=params(24),
        name="finish",
    )(text, tile, sums, slots)


def shards(
    merged,
    ln_gain,
    ln_bias,
    proj_weight,
    proj_bias,
    text_embed,
    attn_gain,
    query_weight,
    key_weight,
    value_weight,
    out_weight,
    final_gain,
    head_weight,
    lengths,
    tile_request,
    insert_pos,
):
    hid = lax.axis_index("hid")
    me = lax.axis_index("req")
    owners = tile_request // REQ_GRP
    tiles = jnp.arange(N_REQ, dtype=jnp.int32)
    tile_order = jnp.sum(
        jnp.where(owners[None, :] == tiles[:, None], tiles[None, :], 0), axis=1
    ).astype(jnp.int32)
    mine = owners == me
    local_req = jnp.sum(jnp.where(mine, tile_request % REQ_GRP, 0))
    start = jnp.sum(jnp.where(mine, insert_pos, 0))
    len_a = lengths[0]
    first = local_req * len_a + start

    n = jnp.arange(LIVE, dtype=jnp.int32)
    packed = jnp.where(n < TEXT, jnp.where(n < first, n, n + TILE), n - TEXT + first)
    second = packed >= len_a
    pos = packed - jnp.where(second, len_a, 0)
    code = pos + jnp.where(second, 1024, 0)
    flat = pos + jnp.where(second, LEN_MAX, 0)
    slot = jnp.arange(LEN_MAX, dtype=jnp.int32)
    at = jnp.stack([slot, slot + len_a])
    in_tile = jnp.logical_and(at >= first, at < first + TILE)
    row_of = jnp.where(in_tile, at - first + TEXT, jnp.where(at < first, at, at - TILE))
    row_of = jnp.where(slot[None, :] < lengths[:, None], row_of, -1)

    half_dim = HEAD_DIM // 2
    inv_freq = jnp.exp(
        jnp.arange(half_dim, dtype=F32) * (-2.0 * math.log(1000000.0) / HEAD_DIM)
    )
    angles = pos.astype(F32)[:, None] * inv_freq[None, :]
    cosine, sine = jnp.cos(angles), jnp.sin(angles)
    cos = jnp.concatenate([cosine, cosine], axis=1)
    sin = jnp.concatenate([-sine, sine], axis=1)

    x, z = hid // RING, hid % RING
    rel = jnp.arange(N_HID, dtype=jnp.int32)
    sources = ((x + rel // RING) % RING) * RING + (z + rel % RING) % RING

    gathered = lax.all_gather(pack(merged, tile_order, (hid % RING)[None]), "hid", axis=0, tiled=True)

    pick = (flat[:TEXT, None] == jnp.arange(REQ_GRP * LEN_MAX)[None, :]).astype(BF)
    text_rows = jnp.dot(
        pick, text_embed.reshape(REQ_GRP * LEN_MAX, FEAT), preferred_element_type=F32
    ).astype(BF)
    weight = (
        jnp.concatenate([query_weight, key_weight, value_weight], axis=1).astype(F32)
        * attn_gain.astype(F32)[:, None]
    ).astype(BF)
    partner = [(i, i ^ 1) for i in range(N_HID)]
    text_blocks, text_where = gather_far(gather_near(text_rows))
    q_text, kv_text = qkv(
        text_blocks, text_where, weight, cos[:TEXT], sin[:TEXT], sources, "qkv_text"
    )
    gathered, q_text, kv_text = lax.optimization_barrier((gathered, q_text, kv_text))
    projected = project(
        gathered,
        proj_weight,
        ln_gain,
        ln_bias,
        proj_bias[None, :],
    )
    tile = lax.all_to_all(
        projected.reshape(N_REQ, TILE // N_REQ, FEAT), "req", split_axis=0, concat_axis=0, tiled=True
    ).reshape(TILE, FEAT)
    other_text = lax.ppermute(kv_text, "hid", partner)
    tile_blocks, tile_where = gather_far(gather_near(tile), relay=False)
    q_tile, kv_tile = qkv(
        tile_blocks, tile_where, weight, cos[TEXT:], sin[TEXT:], sources, "qkv_tile"
    )
    other_tile = lax.ppermute(kv_tile, "hid", partner)

    low = (hid % 2 == 0).astype(jnp.int32)[None]
    attended = attend(
        low, q_text, q_tile, kv_text, other_text, kv_tile, other_tile, cos, sin, code
    )
    step = jnp.arange(RING, dtype=jnp.int32)
    partial = spread(attended, out_weight)
    partial, attended = lax.optimization_barrier((partial, attended))
    sums = lax.psum_scatter(
        partial.reshape(N_HID * LIVE, FEAT), "hid", scatter_dimension=0, tiled=True
    )
    hidden = finish(text_embed, tile, sums, row_of[:, :, None])

    last = jnp.sum(jnp.where(slot[None, :] == lengths[:, None] - 1, row_of, 0), axis=1)
    pick_last = (last[:, None] == n[None, :]).astype(BF)
    rows_last = jnp.dot(pick_last, attended, preferred_element_type=F32).astype(BF)
    term = jnp.dot(rows_last, out_weight, preferred_element_type=F32)
    base = jnp.dot(pick_last[:, :TEXT], text_rows, preferred_element_type=F32) + jnp.dot(
        pick_last[:, TEXT:], tile, preferred_element_type=F32
    )
    spot = lax.broadcasted_iota(jnp.int32, (1, N_HID, 1), 1) == hid
    term = term + jnp.where(spot, base[:, None, :], 0.0).reshape(REQ_GRP, D)
    term = over_line(term, along_z)
    full_width = over_line(term, along_x).astype(BF)
    both = [full_width, shift_req(full_width, 0, 1)]
    core = me % 2
    pair = jnp.stack([jnp.where(core == 0, both[0], both[1]), jnp.where(core == 0, both[1], both[0])])
    y = me // 2
    here, back, ahead, far_pair = line_of(pair, along_y)
    line = jnp.stack([here, ahead, far_pair, back])
    wanted = (step[:, None] - y) % RING == step[None, :]
    all_last = jnp.sum(
        jnp.where(wanted[:, :, None, None, None], line[None], jnp.zeros((), BF)), axis=1
    ).reshape(N_REQ * REQ_GRP, D)
    last_values = all_last.astype(F32)
    last_squares = jnp.sum(last_values * last_values, axis=1)
    final_norm = jnp.sqrt(last_squares)
    final_scaled = (
        last_values * lax.rsqrt(last_squares / D + 1e-05)[:, None] * final_gain.astype(F32)
    ).astype(BF)
    logits = lax.dot_general(
        final_scaled, head_weight, (((1,), (1,)), ((), ())), preferred_element_type=F32
    )
    top = jnp.max(logits, axis=1)
    for move in (along_z, along_x, along_y):
        here, below, above, far_top = line_of(top, move)
        top = jnp.maximum(jnp.maximum(here, below), jnp.maximum(above, far_top))
    logit_max = jnp.maximum(top, shift_req(top, 0, 1))
    return (hidden, final_norm, logit_max)


def solution(mesh):
    return jax.shard_map(
        shards,
        mesh=mesh,
        in_specs=(
            P(None, "req", "hid"),
            P(),
            P(),
            P(None, "hid"),
            P("hid"),
            P("req", None, "hid"),
            P(),
            P(None, "hid"),
            P(None, "hid"),
            P(None, "hid"),
            P("hid", None),
            P(),
            P(("req", "hid"), None),
            P("req"),
            P(),
            P(),
        ),
        out_specs=(P("req", None, "hid"), P(), P()),
        check_vma=False,
    )
```

```python
import math

import jax
import jax.numpy as jnp
from jax import lax
from jax.experimental import pallas as pl
from jax.experimental.pallas import tpu as pltpu
from jax.sharding import PartitionSpec as P

HEAD_DIM = 128
D = 6144
MERGED = 12800
REQ_GRP = 2
LEN_MAX = 480
LIVE = 640
TILE = 256
TEXT = LIVE - TILE
N_HID = 16
N_REQ = 8
RING = 4
FEAT = D // N_HID
MFEAT = MERGED // N_HID
MAIN = 768
MPAD = 896
BF = jnp.bfloat16
F32 = jnp.float32
VM = pltpu.VMEM


def vmem():
    return pl.BlockSpec(memory_space=pltpu.VMEM)


def params(mib):
    return pltpu.CompilerParams(vmem_limit_bytes=mib << 20)


def shift(block, dx, dz):
    route = []
    for i in range(N_HID):
        x, z = divmod(i, RING)
        route.append((((x + dx) % RING) * RING + (z + dz) % RING, i))
    return lax.ppermute(block, "hid", route)


def line_of(block, move):
    return [block, move(block, -1), move(block, 1), move(block, 2)]


def along_x(b, d):
    return shift(b, d, 0)


def along_z(b, d):
    return shift(b, 0, d)


def join(*blocks):
    total = blocks[0].astype(F32)
    for b in blocks[1:]:
        total = total + b.astype(F32)
    return total


def over_line(block, move):
    own, below, above, far = line_of(block, move)
    return (own + far) + (below + above)


def axes_of(first):
    return (along_z, along_x) if first == 0 else (along_x, along_z)


def gather_near(shard):
    half = shard.shape[0] // 2
    near = []
    for first in (0, 1):
        inner, outer = axes_of(first)
        own = lax.slice_in_dim(shard, first * half, (first + 1) * half, axis=0)
        group = jnp.concatenate(line_of(own, inner), axis=0)
        near.append((group, outer(group, -1), outer(group, 1)))
    return near


def gather_far(near):
    arrays, tables = [], []
    for first in (0, 1):
        _, outer = axes_of(first)
        group, minus, plus = near[first]
        half = group.shape[0] // RING
        far_a = outer(lax.slice_in_dim(minus, 0, 2 * half, axis=0), -1)
        far_b = outer(lax.slice_in_dim(plus, 2 * half, 4 * half, axis=0), 1)
        offs = [0, -1, 1, 2]
        table = {}
        for array, out, part in (
            (group, 0, offs),
            (minus, -1, offs),
            (plus, 1, offs),
            (far_a, 2, offs[:2]),
            (far_b, 2, offs[2:]),
        ):
            arrays.append(array)
            for j, d in enumerate(part):
                rel = (out % RING, d % RING) if first == 0 else (d % RING, out % RING)
                table[rel] = (len(arrays) - 1, j * half)
        tables.append(table)
    order = [(dx, dz) for dx in range(RING) for dz in range(RING)]
    return arrays, [(tables[0][r], tables[1][r]) for r in order]


def in_hbm(x):
    return pltpu.with_memory_space_constraint(x, pltpu.HBM)


def pack_kernel(order_ref, place_ref, x_ref, o_ref, tail):
    def step(g, carry):
        rows = x_ref[order_ref[g]]
        v = rows.astype(F32)
        here = pl.ds(pl.multiple_of(g * 32, 32), 32)
        lane = lax.broadcasted_iota(jnp.int32, (32, 128), 1)
        block = jnp.zeros((32, 128), F32)
        j = 32
        for s in (jnp.sum(v, axis=1, keepdims=True), jnp.sum(v * v, axis=1, keepdims=True)):
            for _ in range(3):
                part = s.astype(BF).astype(F32)
                block = jnp.where(lane == j, part, block)
                s = s - part
                j += 1
        o_ref[here, 0:MAIN] = rows[:, 0:MAIN]
        tail[here, :] = block
        tail[here, 0:32] = v[:, MAIN:MFEAT]
        return carry

    lax.fori_loop(0, N_REQ, step, 0)
    o_ref[:, MAIN:MPAD] = pltpu.roll(tail[...], place_ref[0] * 32, 1).astype(BF)


def pack(merged, tile_order, place):
    return pl.pallas_call(
        pack_kernel,
        out_shape=jax.ShapeDtypeStruct((TILE, MPAD), BF),
        in_specs=[pl.BlockSpec(memory_space=pltpu.SMEM)] * 2 + [vmem()],
        out_specs=vmem(),
        scratch_shapes=[VM((TILE, 128), F32)],
        compiler_params=params(16),
        name="pack",
    )(tile_order, place, merged)


def project_kernel(
    x_hbm, w_hbm, g_ref, b_ref, gl_ref, bl_ref, pb_ref, o_ref, tail, x, w, wl, acc, sem, x_sem, w_sem
):
    deep = 2 * MAIN
    tails = pltpu.make_async_copy(x_hbm.at[:, pl.ds(MAIN, 128)], tail, sem.at[0])
    lefts = pltpu.make_async_copy(w_hbm.at[:, pl.ds(MAIN, 32), :], wl, sem.at[1])

    def x_copy(k):
        here = pl.ds(pl.multiple_of(k * MAIN, MAIN), MAIN)
        there = x_hbm.at[pl.ds(k * TILE, TILE), pl.ds(0, MAIN)]
        return pltpu.make_async_copy(there, x.at[:, here], x_sem.at[k])

    def w_copy(k):
        here = pl.ds(k * MAIN, MAIN)
        return pltpu.make_async_copy(w_hbm.at[k, pl.ds(0, MAIN), :], w.at[here, :], w_sem.at[k])

    tails.start()
    for k in range(N_HID):
        x_copy(k).start()
        w_copy(k).start()
    lefts.start()
    tails.wait()
    quarter = lax.broadcasted_iota(jnp.int32, (TILE, 128), 1) // 32
    mean = jnp.zeros((TILE, 1), F32)
    square = jnp.zeros((TILE, 1), F32)
    for j in range(RING):
        total = jnp.zeros((TILE, 128), F32)
        for i in range(RING):
            k = RING * i + j
            total = total + tail[k * TILE : (k + 1) * TILE, :].astype(F32)
        at = 32 * ((j + 1) % RING)
        mean = mean + jnp.sum(total[:, at : at + 3], axis=1, keepdims=True)
        square = square + jnp.sum(total[:, at + 3 : at + 6], axis=1, keepdims=True)
    mean = mean * (1.0 / MERGED)
    rstd = lax.rsqrt(square * (1.0 / MERGED) - mean * mean + 1e-05)
    acc[...] = jnp.zeros_like(acc)

    def step(i, carry):
        for j in (0, 1):
            x_copy(2 * i + j).wait()
            w_copy(2 * i + j).wait()
        here = pl.ds(pl.multiple_of(i * deep, deep), deep)
        v = x[:, here].astype(F32)
        normed = (v - mean) * rstd * g_ref[i] + b_ref[i]
        acc[...] += jnp.dot(normed.astype(BF), w[here, :], preferred_element_type=F32)
        return carry

    lax.fori_loop(0, N_HID // 2, step, 0)
    lefts.wait()
    blocks = []
    for i in range(RING):
        v = jnp.zeros((TILE, 128), F32)
        for j in range(RING):
            k = RING * i + j
            v = jnp.where(quarter == j, tail[k * TILE : (k + 1) * TILE, :].astype(F32), v)
        blocks.append(((v - mean) * rstd * gl_ref[i] + bl_ref[i]).astype(BF))
    rest = jnp.concatenate(blocks, axis=1)
    y = acc[...] + pb_ref[...] + jnp.dot(
        rest, wl[...].reshape(N_HID * 32, FEAT), preferred_element_type=F32
    )
    y = 0.5 * y * (1.0 + lax.erf(y * math.sqrt(0.5)))
    o_ref[...] = y.astype(BF)


def project(gathered, weight, gain, bias, out_bias):
    def parts(v):
        v = v.astype(F32).reshape(N_HID, MFEAT)
        return (
            v[:, :MAIN].reshape(N_HID // 2, 1, 2 * MAIN),
            v[:, MAIN:].reshape(RING, 1, 128),
        )

    gain, gain_left = parts(gain)
    bias, bias_left = parts(bias)
    return pl.pallas_call(
        project_kernel,
        out_shape=jax.ShapeDtypeStruct((TILE, FEAT), BF),
        in_specs=[pl.BlockSpec(memory_space=pl.ANY)] * 2 + [vmem()] * 5,
        out_specs=vmem(),
        scratch_shapes=[
            VM((N_HID * TILE, 128), BF),
            VM((TILE, N_HID * MAIN), BF),
            VM((N_HID * MAIN, FEAT), BF),
            VM((N_HID, 32, FEAT), BF),
            VM((TILE, FEAT), F32),
            pltpu.SemaphoreType.DMA((2,)),
            pltpu.SemaphoreType.DMA((N_HID,)),
            pltpu.SemaphoreType.DMA((N_HID,)),
        ],
        compiler_params=params(30),
        cost_estimate=pl.CostEstimate(
            flops=2 * TILE * MERGED * FEAT, bytes_accessed=17 << 20, transcendentals=0
        ),
        name="project",
    )(
        in_hbm(gathered),
        in_hbm(weight.reshape(N_HID, MFEAT, FEAT)),
        gain,
        bias,
        gain_left,
        bias_left,
        out_bias,
    )


def turn(v, cos, sin):
    return v * cos + pltpu.roll(v, HEAD_DIM // 2, 1) * sin


def qkv(arrays, where, weight, cos, sin, sources, name):
    half = arrays[0].shape[0] // RING
    rows = 2 * half
    n = len(arrays)
    deep = 2 * FEAT
    cols = FEAT + HEAD_DIM

    def kernel(src_ref, *refs):
        ins = refs[:n]
        w_hbm, cos_ref, sin_ref, q_ref, kv_ref, xs, w, acc, sq, sem = refs[n:]

        def copy(k):
            there = pl.ds(pl.multiple_of(src_ref[k] * FEAT, FEAT), FEAT)
            here = pl.ds(k * FEAT, FEAT)
            return pltpu.make_async_copy(w_hbm.at[there, :], w.at[here, :], sem.at[k])

        for k in range(N_HID):
            copy(k).start()
        for k in range(N_HID):
            block = jnp.concatenate([ins[a][row : row + half, :] for a, row in where[k]], axis=0)
            xs[:, k * FEAT : (k + 1) * FEAT] = block
        acc[...] = jnp.zeros_like(acc)
        sq[...] = jnp.zeros_like(sq)

        def step(i, carry):
            for j in range(2):
                copy(2 * i + j).wait()
            here = pl.ds(pl.multiple_of(i * deep, deep), deep)
            acc[...] += jnp.dot(xs[:, here], w[here, :], preferred_element_type=F32)
            v = xs[:, here].astype(F32)
            v = v * v
            sq[...] += sum(v[:, c : c + 128] for c in range(0, deep, 128))
            return carry

        lax.fori_loop(0, N_HID // 2, step, 0)
        scale = lax.rsqrt(jnp.sum(sq[...], axis=1, keepdims=True) * (1.0 / D) + 1e-05)
        for h in range(FEAT // HEAD_DIM):
            part = acc[:, h * HEAD_DIM : (h + 1) * HEAD_DIM] * scale
            q_ref[:, h * HEAD_DIM : (h + 1) * HEAD_DIM] = turn(
                part, cos_ref[...], sin_ref[...]
            ).astype(BF)
        kv_ref[...] = (acc[:, FEAT:] * scale).astype(BF)

    return pl.pallas_call(
        kernel,
        out_shape=(
            jax.ShapeDtypeStruct((rows, FEAT), BF),
            jax.ShapeDtypeStruct((rows, HEAD_DIM), BF),
        ),
        in_specs=[pl.BlockSpec(memory_space=pltpu.SMEM)]
        + [vmem() for _ in arrays]
        + [pl.BlockSpec(memory_space=pl.ANY), vmem(), vmem()],
        out_specs=(vmem(), vmem()),
        scratch_shapes=[
            VM((rows, D), BF),
            VM((D, cols), BF),
            VM((rows, cols), F32),
            VM((rows, HEAD_DIM), F32),
            pltpu.SemaphoreType.DMA((N_HID,)),
        ],
        compiler_params=params(20),
        cost_estimate=pl.CostEstimate(
            flops=2 * rows * D * cols, bytes_accessed=12 << 20, transcendentals=0
        ),
        name=name,
    )(sources, *arrays, in_hbm(weight), cos, sin)


def attend_kernel(
    low_ref, qt, qi, ot, pt, oi, pi, cos_ref, sin_ref, row_ref, col_ref, o_ref, qs, keys, vals
):
    upper = low_ref[0] == 0
    lane = lax.broadcasted_iota(jnp.int32, (LIVE, HEAD_DIM), 1)
    own = jnp.concatenate([ot[...], oi[...]], axis=0).astype(F32)
    other = jnp.concatenate([pt[...], pi[...]], axis=0).astype(F32)
    low = jnp.where(upper, other, own)
    high = jnp.where(upper, own, other)
    key = jnp.where(lane < 64, low, pltpu.roll(high, 64, 1))
    val = jnp.where(lane < 64, pltpu.roll(low, 64, 1), high)
    keys[...] = turn(key, cos_ref[...], sin_ref[...]).astype(BF)
    vals[...] = val.astype(BF)
    qs[:TEXT] = qt[...]
    qs[TEXT:] = qi[...]
    code = col_ref[...]

    def block(i, carry):
        rows = pl.ds(pl.multiple_of(i * 128, 128), 128)
        mine = row_ref[rows, :]
        start = jnp.where(mine >= 1024, 1024, 0)
        live = jnp.logical_and(code <= mine, code >= start)
        for h in range(FEAT // HEAD_DIM):
            cols = slice(h * HEAD_DIM, (h + 1) * HEAD_DIM)
            s = lax.dot_general(
                qs[rows, cols], keys[...], (((1,), (1,)), ((), ())), preferred_element_type=F32
            ) * (1.0 / math.sqrt(HEAD_DIM))
            s = jnp.where(live, s, -jnp.inf)
            w = jnp.exp(s - jnp.max(s, axis=1, keepdims=True))
            total = jnp.sum(w, axis=1, keepdims=True)
            mixed = jnp.dot(w.astype(BF), vals[...], preferred_element_type=F32)
            o_ref[rows, cols] = (mixed / total).astype(BF)
        return carry

    lax.fori_loop(0, LIVE // 128, block, 0)


def attend(low, qt, qi, ot, pt, oi, pi, cos, sin, code):
    return pl.pallas_call(
        attend_kernel,
        out_shape=jax.ShapeDtypeStruct((LIVE, FEAT), BF),
        in_specs=[pl.BlockSpec(memory_space=pltpu.SMEM)] + [vmem()] * 10,
        out_specs=vmem(),
        scratch_shapes=[VM((LIVE, FEAT), BF), VM((LIVE, HEAD_DIM), BF), VM((LIVE, HEAD_DIM), BF)],
        compiler_params=params(24),
        cost_estimate=pl.CostEstimate(flops=1 << 30, bytes_accessed=2 << 20, transcendentals=0),
        name="attend",
    )(low, qt, qi, ot, pt, oi, pi, cos, sin, code[:, None], code[None, :])


def spread_kernel(a_ref, w_hbm, o_ref, w, sem):
    k = pl.program_id(0)
    two = 2 * FEAT

    def copy(i):
        cols = pl.ds(pl.multiple_of(i * two, two), two)
        return pltpu.make_async_copy(w_hbm.at[:, cols], w.at[i], sem.at[i])

    @pl.when(k == 0)
    def _():
        for i in range(N_HID // 2):
            copy(i).start()

    copy(k).wait()
    product = jnp.dot(a_ref[...], w[k], preferred_element_type=F32).astype(BF)
    o_ref[0] = product[:, :FEAT]
    o_ref[1] = product[:, FEAT:]


def spread(attended, weight):
    return pl.pallas_call(
        spread_kernel,
        out_shape=jax.ShapeDtypeStruct((N_HID, LIVE, FEAT), BF),
        grid=(N_HID // 2,),
        in_specs=[
            pl.BlockSpec(memory_space=pltpu.VMEM),
            pl.BlockSpec(memory_space=pl.ANY),
        ],
        out_specs=pl.BlockSpec((2, LIVE, FEAT), lambda k: (k, 0, 0)),
        scratch_shapes=[
            VM((N_HID // 2, FEAT, 2 * FEAT), BF),
            pltpu.SemaphoreType.DMA((N_HID // 2,)),
        ],
        compiler_params=params(58),
        cost_estimate=pl.CostEstimate(
            flops=2 * LIVE * FEAT * D, bytes_accessed=13 << 20, transcendentals=0
        ),
        name="spread",
    )(attended, in_hbm(weight))


def finish_kernel(text_ref, tile_ref, sum_ref, slot_ref, o_ref):
    def one(r, carry):
        row = slot_ref[r]
        pick = (lax.broadcasted_iota(jnp.int32, (LEN_MAX, LIVE), 1) == row).astype(BF)
        moved = jnp.dot(pick, sum_ref[...], preferred_element_type=F32)
        image = jnp.dot(pick[:, TEXT:], tile_ref[...], preferred_element_type=F32)
        base = jnp.where(row >= TEXT, image, text_ref[r].astype(F32))
        o_ref[r] = (base + moved).astype(BF)
        return carry

    lax.fori_loop(0, REQ_GRP, one, 0)


def finish(text, tile, sums, slots):
    return pl.pallas_call(
        finish_kernel,
        out_shape=jax.ShapeDtypeStruct((REQ_GRP, LEN_MAX, FEAT), BF),
        in_specs=[vmem()] * 4,
        out_specs=vmem(),
        compiler_params=params(24),
        name="finish",
    )(text, tile, sums, slots)


def shards(
    merged,
    ln_gain,
    ln_bias,
    proj_weight,
    proj_bias,
    text_embed,
    attn_gain,
    query_weight,
    key_weight,
    value_weight,
    out_weight,
    final_gain,
    head_weight,
    lengths,
    tile_request,
    insert_pos,
):
    hid = lax.axis_index("hid")
    me = lax.axis_index("req")
    owners = tile_request // REQ_GRP
    tiles = jnp.arange(N_REQ, dtype=jnp.int32)
    tile_order = jnp.sum(
        jnp.where(owners[None, :] == tiles[:, None], tiles[None, :], 0), axis=1
    ).astype(jnp.int32)
    mine = owners == me
    local_req = jnp.sum(jnp.where(mine, tile_request % REQ_GRP, 0))
    start = jnp.sum(jnp.where(mine, insert_pos, 0))
    len_a = lengths[0]
    first = local_req * len_a + start

    n = jnp.arange(LIVE, dtype=jnp.int32)
    packed = jnp.where(n < TEXT, jnp.where(n < first, n, n + TILE), n - TEXT + first)
    second = packed >= len_a
    pos = packed - jnp.where(second, len_a, 0)
    code = pos + jnp.where(second, 1024, 0)
    flat = pos + jnp.where(second, LEN_MAX, 0)
    slot = jnp.arange(LEN_MAX, dtype=jnp.int32)
    at = jnp.stack([slot, slot + len_a])
    in_tile = jnp.logical_and(at >= first, at < first + TILE)
    row_of = jnp.where(in_tile, at - first + TEXT, jnp.where(at < first, at, at - TILE))
    row_of = jnp.where(slot[None, :] < lengths[:, None], row_of, -1)

    half_dim = HEAD_DIM // 2
    inv_freq = jnp.exp(
        jnp.arange(half_dim, dtype=F32) * (-2.0 * math.log(1000000.0) / HEAD_DIM)
    )
    angles = pos.astype(F32)[:, None] * inv_freq[None, :]
    cosine, sine = jnp.cos(angles), jnp.sin(angles)
    cos = jnp.concatenate([cosine, cosine], axis=1)
    sin = jnp.concatenate([-sine, sine], axis=1)

    x, z = hid // RING, hid % RING
    rel = jnp.arange(N_HID, dtype=jnp.int32)
    sources = ((x + rel // RING) % RING) * RING + (z + rel % RING) % RING

    gathered = lax.all_gather(pack(merged, tile_order, (hid % RING)[None]), "hid", axis=0, tiled=True)

    pick = (flat[:TEXT, None] == jnp.arange(REQ_GRP * LEN_MAX)[None, :]).astype(BF)
    text_rows = jnp.dot(
        pick, text_embed.reshape(REQ_GRP * LEN_MAX, FEAT), preferred_element_type=F32
    ).astype(BF)
    weight = (
        jnp.concatenate([query_weight, key_weight, value_weight], axis=1).astype(F32)
        * attn_gain.astype(F32)[:, None]
    ).astype(BF)
    partner = [(i, i ^ 1) for i in range(N_HID)]
    text_blocks, text_where = gather_far(gather_near(text_rows))
    q_text, kv_text = qkv(
        text_blocks, text_where, weight, cos[:TEXT], sin[:TEXT], sources, "qkv_text"
    )
    gathered, q_text, kv_text = lax.optimization_barrier((gathered, q_text, kv_text))
    projected = project(
        gathered,
        proj_weight,
        ln_gain,
        ln_bias,
        proj_bias[None, :],
    )
    tile = lax.all_to_all(
        projected.reshape(N_REQ, TILE // N_REQ, FEAT), "req", split_axis=0, concat_axis=0, tiled=True
    ).reshape(TILE, FEAT)
    other_text = lax.ppermute(kv_text, "hid", partner)
    tile_blocks, tile_where = gather_far(gather_near(tile))
    q_tile, kv_tile = qkv(
        tile_blocks, tile_where, weight, cos[TEXT:], sin[TEXT:], sources, "qkv_tile"
    )
    other_tile = lax.ppermute(kv_tile, "hid", partner)

    low = (hid % 2 == 0).astype(jnp.int32)[None]
    attended = attend(
        low, q_text, q_tile, kv_text, other_text, kv_tile, other_tile, cos, sin, code
    )
    partial = spread(attended, out_weight)
    partial, attended = lax.optimization_barrier((partial, attended))
    sums = lax.psum_scatter(
        partial.reshape(N_HID * LIVE, FEAT), "hid", scatter_dimension=0, tiled=True
    )
    hidden = finish(text_embed, tile, sums, row_of[:, :, None])

    last = jnp.sum(jnp.where(slot[None, :] == lengths[:, None] - 1, row_of, 0), axis=1)
    pick_last = (last[:, None] == n[None, :]).astype(BF)
    rows_last = jnp.dot(pick_last, attended, preferred_element_type=F32).astype(BF)
    term = jnp.dot(rows_last, out_weight, preferred_element_type=F32)
    base = jnp.dot(pick_last[:, :TEXT], text_rows, preferred_element_type=F32) + jnp.dot(
        pick_last[:, TEXT:], tile, preferred_element_type=F32
    )
    spot = lax.broadcasted_iota(jnp.int32, (1, N_HID, 1), 1) == hid
    term = term + jnp.where(spot, base[:, None, :], 0.0).reshape(REQ_GRP, D)
    term = over_line(term, along_z)
    full_width = over_line(term, along_x).astype(BF)
    all_last = lax.all_gather(full_width, "req", axis=0, tiled=True)
    last_values = all_last.astype(F32)
    last_squares = jnp.sum(last_values * last_values, axis=1)
    final_norm = jnp.sqrt(last_squares)
    final_scaled = (
        last_values * lax.rsqrt(last_squares / D + 1e-05)[:, None] * final_gain.astype(F32)
    ).astype(BF)
    logits = lax.dot_general(
        final_scaled, head_weight, (((1,), (1,)), ((), ())), preferred_element_type=F32
    )
    top = jnp.max(logits, axis=1)
    for move in (along_z, along_x):
        here, below, above, far_top = line_of(top, move)
        top = jnp.maximum(jnp.maximum(here, below), jnp.maximum(above, far_top))
    logit_max = lax.pmax(top, "req")
    return (hidden, final_norm, logit_max)


def solution(mesh):
    return jax.shard_map(
        shards,
        mesh=mesh,
        in_specs=(
            P(None, "req", "hid"),
            P(),
            P(),
            P(None, "hid"),
            P("hid"),
            P("req", None, "hid"),
            P(),
            P(None, "hid"),
            P(None, "hid"),
            P(None, "hid"),
            P("hid", None),
            P(),
            P(("req", "hid"), None),
            P("req"),
            P(),
            P(),
        ),
        out_specs=(P("req", None, "hid"), P(), P()),
        check_vma=False,
    )
```

```python
import math

import jax
import jax.numpy as jnp
from jax import lax
from jax.experimental import pallas as pl
from jax.experimental.pallas import tpu as pltpu
from jax.sharding import PartitionSpec as P

HEAD_DIM = 128
D = 6144
MERGED = 12800
REQ_GRP = 2
LEN_MAX = 480
LIVE = 640
TILE = 256
TEXT = LIVE - TILE
N_HID = 16
N_REQ = 8
RING = 4
FEAT = D // N_HID
MFEAT = MERGED // N_HID
MAIN = 768
MPAD = 896
BF = jnp.bfloat16
F32 = jnp.float32
VM = pltpu.VMEM


def vmem():
    return pl.BlockSpec(memory_space=pltpu.VMEM)


def params(mib):
    return pltpu.CompilerParams(vmem_limit_bytes=mib << 20)


def shift(block, dx, dz):
    route = []
    for i in range(N_HID):
        x, z = divmod(i, RING)
        route.append((((x + dx) % RING) * RING + (z + dz) % RING, i))
    return lax.ppermute(block, "hid", route)


def line_of(block, move):
    return [block, move(block, -1), move(block, 1), move(block, 2)]


def along_x(b, d):
    return shift(b, d, 0)


def along_z(b, d):
    return shift(b, 0, d)


def join(*blocks):
    total = blocks[0].astype(F32)
    for b in blocks[1:]:
        total = total + b.astype(F32)
    return total


def over_line(block, move):
    own, below, above, far = line_of(block, move)
    return (own + far) + (below + above)


def axes_of(first):
    return (along_z, along_x) if first == 0 else (along_x, along_z)


def gather_near(shard):
    half = shard.shape[0] // 2
    near = []
    for first in (0, 1):
        inner, outer = axes_of(first)
        own = lax.slice_in_dim(shard, first * half, (first + 1) * half, axis=0)
        group = jnp.concatenate(line_of(own, inner), axis=0)
        near.append((group, outer(group, -1), outer(group, 1)))
    return near


def gather_far(near):
    arrays, tables = [], []
    for first in (0, 1):
        _, outer = axes_of(first)
        group, minus, plus = near[first]
        half = group.shape[0] // RING
        far_a = outer(lax.slice_in_dim(minus, 0, 2 * half, axis=0), -1)
        far_b = outer(lax.slice_in_dim(plus, 2 * half, 4 * half, axis=0), 1)
        offs = [0, -1, 1, 2]
        table = {}
        for array, out, part in (
            (group, 0, offs),
            (minus, -1, offs),
            (plus, 1, offs),
            (far_a, 2, offs[:2]),
            (far_b, 2, offs[2:]),
        ):
            arrays.append(array)
            for j, d in enumerate(part):
                rel = (out % RING, d % RING) if first == 0 else (d % RING, out % RING)
                table[rel] = (len(arrays) - 1, j * half)
        tables.append(table)
    order = [(dx, dz) for dx in range(RING) for dz in range(RING)]
    return arrays, [(tables[0][r], tables[1][r]) for r in order]


def in_hbm(x):
    return pltpu.with_memory_space_constraint(x, pltpu.HBM)


def pack_kernel(order_ref, place_ref, x_ref, o_ref, tail):
    def step(g, carry):
        rows = x_ref[order_ref[g]]
        v = rows.astype(F32)
        here = pl.ds(pl.multiple_of(g * 32, 32), 32)
        lane = lax.broadcasted_iota(jnp.int32, (32, 128), 1)
        block = jnp.zeros((32, 128), F32)
        j = 32
        for s in (jnp.sum(v, axis=1, keepdims=True), jnp.sum(v * v, axis=1, keepdims=True)):
            for _ in range(3):
                part = s.astype(BF).astype(F32)
                block = jnp.where(lane == j, part, block)
                s = s - part
                j += 1
        o_ref[here, 0:MAIN] = rows[:, 0:MAIN]
        tail[here, :] = block
        tail[here, 0:32] = v[:, MAIN:MFEAT]
        return carry

    lax.fori_loop(0, N_REQ, step, 0)
    o_ref[:, MAIN:MPAD] = pltpu.roll(tail[...], place_ref[0] * 32, 1).astype(BF)


def pack(merged, tile_order, place):
    return pl.pallas_call(
        pack_kernel,
        out_shape=jax.ShapeDtypeStruct((TILE, MPAD), BF),
        in_specs=[pl.BlockSpec(memory_space=pltpu.SMEM)] * 2 + [vmem()],
        out_specs=vmem(),
        scratch_shapes=[VM((TILE, 128), F32)],
        compiler_params=params(16),
        name="pack",
    )(tile_order, place, merged)


def project_kernel(
    x_hbm, w_hbm, gb_ref, left_ref, pb_ref, o_ref, tail, x, w, wl, acc, sem, x_sem, w_sem
):
    deep = 2 * MAIN
    tails = pltpu.make_async_copy(x_hbm.at[:, pl.ds(MAIN, 128)], tail, sem.at[0])
    lefts = pltpu.make_async_copy(w_hbm.at[:, pl.ds(MAIN, 32), :], wl, sem.at[1])

    def x_copy(k):
        here = pl.ds(pl.multiple_of(k * MAIN, MAIN), MAIN)
        there = x_hbm.at[pl.ds(k * TILE, TILE), pl.ds(0, MAIN)]
        return pltpu.make_async_copy(there, x.at[:, here], x_sem.at[k])

    def pair(part, i):
        return jnp.concatenate([gb_ref[part, pl.ds(2 * i + j, 1), :] for j in (0, 1)], axis=1)

    def w_copy(k):
        here = pl.ds(k * MAIN, MAIN)
        return pltpu.make_async_copy(w_hbm.at[k, pl.ds(0, MAIN), :], w.at[here, :], w_sem.at[k])

    tails.start()
    for k in range(N_HID):
        x_copy(k).start()
        w_copy(k).start()
    lefts.start()
    tails.wait()
    quarter = lax.broadcasted_iota(jnp.int32, (TILE, 128), 1) // 32
    mean = jnp.zeros((TILE, 1), F32)
    square = jnp.zeros((TILE, 1), F32)
    for j in range(RING):
        total = jnp.zeros((TILE, 128), F32)
        for i in range(RING):
            k = RING * i + j
            total = total + tail[k * TILE : (k + 1) * TILE, :].astype(F32)
        at = 32 * ((j + 1) % RING)
        mean = mean + jnp.sum(total[:, at : at + 3], axis=1, keepdims=True)
        square = square + jnp.sum(total[:, at + 3 : at + 6], axis=1, keepdims=True)
    mean = mean * (1.0 / MERGED)
    rstd = lax.rsqrt(square * (1.0 / MERGED) - mean * mean + 1e-05)
    acc[...] = jnp.zeros_like(acc)

    def step(i, carry):
        for j in (0, 1):
            x_copy(2 * i + j).wait()
            w_copy(2 * i + j).wait()
        here = pl.ds(pl.multiple_of(i * deep, deep), deep)
        v = x[:, here].astype(F32)
        normed = (v - mean) * rstd * pair(0, i) + pair(1, i)
        acc[...] += jnp.dot(normed.astype(BF), w[here, :], preferred_element_type=F32)
        return carry

    lax.fori_loop(0, N_HID // 2, step, 0)
    lefts.wait()
    blocks = []
    for i in range(RING):
        v = jnp.zeros((TILE, 128), F32)
        for j in range(RING):
            k = RING * i + j
            v = jnp.where(quarter == j, tail[k * TILE : (k + 1) * TILE, :].astype(F32), v)
        blocks.append(((v - mean) * rstd * left_ref[0, i] + left_ref[1, i]).astype(BF))
    rest = jnp.concatenate(blocks, axis=1)
    y = acc[...] + pb_ref[...] + jnp.dot(
        rest, wl[...].reshape(N_HID * 32, FEAT), preferred_element_type=F32
    )
    y = 0.5 * y * (1.0 + lax.erf(y * math.sqrt(0.5)))
    o_ref[...] = y.astype(BF)


def project(gathered, weight, gain, bias, out_bias):
    both = jnp.stack([gain, bias]).astype(F32).reshape(2, N_HID, MFEAT)
    return pl.pallas_call(
        project_kernel,
        out_shape=jax.ShapeDtypeStruct((TILE, FEAT), BF),
        in_specs=[pl.BlockSpec(memory_space=pl.ANY)] * 2 + [vmem()] * 3,
        out_specs=vmem(),
        scratch_shapes=[
            VM((N_HID * TILE, 128), BF),
            VM((TILE, N_HID * MAIN), BF),
            VM((N_HID * MAIN, FEAT), BF),
            VM((N_HID, 32, FEAT), BF),
            VM((TILE, FEAT), F32),
            pltpu.SemaphoreType.DMA((2,)),
            pltpu.SemaphoreType.DMA((N_HID,)),
            pltpu.SemaphoreType.DMA((N_HID,)),
        ],
        compiler_params=params(30),
        cost_estimate=pl.CostEstimate(
            flops=2 * TILE * MERGED * FEAT, bytes_accessed=17 << 20, transcendentals=0
        ),
        name="project",
    )(
        in_hbm(gathered),
        in_hbm(weight.reshape(N_HID, MFEAT, FEAT)),
        both[:, :, :MAIN],
        both[:, :, MAIN:].reshape(2, RING, 1, 128),
        out_bias,
    )


def turn(v, cos, sin):
    return v * cos + pltpu.roll(v, HEAD_DIM // 2, 1) * sin


def qkv(arrays, where, weight, cos, sin, sources, name):
    half = arrays[0].shape[0] // RING
    rows = 2 * half
    n = len(arrays)
    deep = 4 * FEAT
    cols = FEAT + HEAD_DIM

    def kernel(src_ref, *refs):
        ins = refs[:n]
        w_hbm, cos_ref, sin_ref, q_ref, kv_ref, xs, w, acc, sq, sem = refs[n:]

        def copy(k):
            there = pl.ds(pl.multiple_of(src_ref[k] * FEAT, FEAT), FEAT)
            here = pl.ds(k * FEAT, FEAT)
            return pltpu.make_async_copy(w_hbm.at[there, :], w.at[here, :], sem.at[k])

        for k in range(N_HID):
            copy(k).start()
        for k in range(N_HID):
            block = jnp.concatenate([ins[a][row : row + half, :] for a, row in where[k]], axis=0)
            xs[:, k * FEAT : (k + 1) * FEAT] = block
        acc[...] = jnp.zeros_like(acc)
        sq[...] = jnp.zeros_like(sq)

        def step(i, carry):
            for j in range(4):
                copy(4 * i + j).wait()
            here = pl.ds(pl.multiple_of(i * deep, deep), deep)
            acc[...] += jnp.dot(xs[:, here], w[here, :], preferred_element_type=F32)
            v = xs[:, here].astype(F32)
            v = v * v
            sq[...] += sum(v[:, c : c + 128] for c in range(0, deep, 128))
            return carry

        lax.fori_loop(0, RING, step, 0)
        scale = lax.rsqrt(jnp.sum(sq[...], axis=1, keepdims=True) * (1.0 / D) + 1e-05)
        for h in range(FEAT // HEAD_DIM):
            part = acc[:, h * HEAD_DIM : (h + 1) * HEAD_DIM] * scale
            q_ref[:, h * HEAD_DIM : (h + 1) * HEAD_DIM] = turn(
                part, cos_ref[...], sin_ref[...]
            ).astype(BF)
        kv_ref[...] = (acc[:, FEAT:] * scale).astype(BF)

    return pl.pallas_call(
        kernel,
        out_shape=(
            jax.ShapeDtypeStruct((rows, FEAT), BF),
            jax.ShapeDtypeStruct((rows, HEAD_DIM), BF),
        ),
        in_specs=[pl.BlockSpec(memory_space=pltpu.SMEM)]
        + [vmem() for _ in arrays]
        + [pl.BlockSpec(memory_space=pl.ANY), vmem(), vmem()],
        out_specs=(vmem(), vmem()),
        scratch_shapes=[
            VM((rows, D), BF),
            VM((D, cols), BF),
            VM((rows, cols), F32),
            VM((rows, HEAD_DIM), F32),
            pltpu.SemaphoreType.DMA((N_HID,)),
        ],
        compiler_params=params(20),
        cost_estimate=pl.CostEstimate(
            flops=2 * rows * D * cols, bytes_accessed=12 << 20, transcendentals=0
        ),
        name=name,
    )(sources, *arrays, in_hbm(weight), cos, sin)


def attend_kernel(
    low_ref, qt, qi, ot, pt, oi, pi, cos_ref, sin_ref, row_ref, col_ref, o_ref, qs, keys, vals
):
    upper = low_ref[0] == 0
    lane = lax.broadcasted_iota(jnp.int32, (LIVE, HEAD_DIM), 1)
    own = jnp.concatenate([ot[...], oi[...]], axis=0).astype(F32)
    other = jnp.concatenate([pt[...], pi[...]], axis=0).astype(F32)
    low = jnp.where(upper, other, own)
    high = jnp.where(upper, own, other)
    key = jnp.where(lane < 64, low, pltpu.roll(high, 64, 1))
    val = jnp.where(lane < 64, pltpu.roll(low, 64, 1), high)
    keys[...] = turn(key, cos_ref[...], sin_ref[...]).astype(BF)
    vals[...] = val.astype(BF)
    qs[:TEXT] = qt[...]
    qs[TEXT:] = qi[...]
    code = col_ref[...]

    def block(i, carry):
        rows = pl.ds(pl.multiple_of(i * 128, 128), 128)
        mine = row_ref[rows, :]
        start = jnp.where(mine >= 1024, 1024, 0)
        live = jnp.logical_and(code <= mine, code >= start)
        for h in range(FEAT // HEAD_DIM):
            cols = slice(h * HEAD_DIM, (h + 1) * HEAD_DIM)
            s = lax.dot_general(
                qs[rows, cols], keys[...], (((1,), (1,)), ((), ())), preferred_element_type=F32
            ) * (1.0 / math.sqrt(HEAD_DIM))
            s = jnp.where(live, s, -jnp.inf)
            w = jnp.exp(s - jnp.max(s, axis=1, keepdims=True))
            total = jnp.sum(w, axis=1, keepdims=True)
            mixed = jnp.dot(w.astype(BF), vals[...], preferred_element_type=F32)
            o_ref[rows, cols] = (mixed / total).astype(BF)
        return carry

    lax.fori_loop(0, LIVE // 128, block, 0)


def attend(low, qt, qi, ot, pt, oi, pi, cos, sin, code):
    return pl.pallas_call(
        attend_kernel,
        out_shape=jax.ShapeDtypeStruct((LIVE, FEAT), BF),
        in_specs=[pl.BlockSpec(memory_space=pltpu.SMEM)] + [vmem()] * 10,
        out_specs=vmem(),
        scratch_shapes=[VM((LIVE, FEAT), BF), VM((LIVE, HEAD_DIM), BF), VM((LIVE, HEAD_DIM), BF)],
        compiler_params=params(24),
        cost_estimate=pl.CostEstimate(flops=1 << 30, bytes_accessed=2 << 20, transcendentals=0),
        name="attend",
    )(low, qt, qi, ot, pt, oi, pi, cos, sin, code[:, None], code[None, :])


def finish_kernel(
    text_ref, tile_ref, a_hbm, w_hbm, slot_ref, o_ref, a, w, acc, sums, a_sem, w_sem
):
    two = 2 * FEAT

    def a_copy(k):
        here = pl.ds(pl.multiple_of(k * FEAT, FEAT), FEAT)
        return pltpu.make_async_copy(a_hbm.at[pl.ds(k * LIVE, LIVE), :], a.at[:, here], a_sem.at[k])

    def w_copy(k):
        here = pl.ds(k * FEAT, FEAT)
        return pltpu.make_async_copy(w_hbm.at[here, :], w.at[here, :], w_sem.at[k])

    for k in range(N_HID):
        a_copy(k).start()
        w_copy(k).start()
    acc[...] = jnp.zeros_like(acc)

    def step(i, carry):
        for j in (0, 1):
            a_copy(2 * i + j).wait()
            w_copy(2 * i + j).wait()
        here = pl.ds(pl.multiple_of(i * two, two), two)
        acc[...] += jnp.dot(a[:, here], w[here, :], preferred_element_type=F32)
        return carry

    lax.fori_loop(0, N_HID // 2, step, 0)
    sums[...] = acc[...].astype(BF)

    def one(r, carry):
        row = slot_ref[r]
        pick = (lax.broadcasted_iota(jnp.int32, (LEN_MAX, LIVE), 1) == row).astype(BF)
        moved = jnp.dot(pick, sums[...], preferred_element_type=F32)
        image = jnp.dot(pick[:, TEXT:], tile_ref[...], preferred_element_type=F32)
        base = jnp.where(row >= TEXT, image, text_ref[r].astype(F32))
        o_ref[r] = (base + moved).astype(BF)
        return carry

    lax.fori_loop(0, REQ_GRP, one, 0)


def finish(text, tile, heads, weight, slots):
    return pl.pallas_call(
        finish_kernel,
        out_shape=jax.ShapeDtypeStruct((REQ_GRP, LEN_MAX, FEAT), BF),
        in_specs=[vmem()] * 2 + [pl.BlockSpec(memory_space=pl.ANY)] * 2 + [vmem()],
        out_specs=vmem(),
        scratch_shapes=[
            VM((LIVE, D), BF),
            VM((D, FEAT), BF),
            VM((LIVE, FEAT), F32),
            VM((LIVE, FEAT), BF),
            pltpu.SemaphoreType.DMA((N_HID,)),
            pltpu.SemaphoreType.DMA((N_HID,)),
        ],
        compiler_params=params(32),
        cost_estimate=pl.CostEstimate(
            flops=2 * LIVE * FEAT * D, bytes_accessed=14 << 20, transcendentals=0
        ),
        name="finish",
    )(text, tile, in_hbm(heads), in_hbm(weight), slots)


def shards(
    merged,
    ln_gain,
    ln_bias,
    proj_weight,
    proj_bias,
    text_embed,
    attn_gain,
    query_weight,
    key_weight,
    value_weight,
    out_weight,
    final_gain,
    head_weight,
    lengths,
    tile_request,
    insert_pos,
):
    hid = lax.axis_index("hid")
    me = lax.axis_index("req")
    owners = tile_request // REQ_GRP
    tiles = jnp.arange(N_REQ, dtype=jnp.int32)
    tile_order = jnp.sum(
        jnp.where(owners[None, :] == tiles[:, None], tiles[None, :], 0), axis=1
    ).astype(jnp.int32)
    mine = owners == me
    local_req = jnp.sum(jnp.where(mine, tile_request % REQ_GRP, 0))
    start = jnp.sum(jnp.where(mine, insert_pos, 0))
    len_a = lengths[0]
    first = local_req * len_a + start

    n = jnp.arange(LIVE, dtype=jnp.int32)
    packed = jnp.where(n < TEXT, jnp.where(n < first, n, n + TILE), n - TEXT + first)
    second = packed >= len_a
    pos = packed - jnp.where(second, len_a, 0)
    code = pos + jnp.where(second, 1024, 0)
    flat = pos + jnp.where(second, LEN_MAX, 0)
    slot = jnp.arange(LEN_MAX, dtype=jnp.int32)
    at = jnp.stack([slot, slot + len_a])
    in_tile = jnp.logical_and(at >= first, at < first + TILE)
    row_of = jnp.where(in_tile, at - first + TEXT, jnp.where(at < first, at, at - TILE))
    row_of = jnp.where(slot[None, :] < lengths[:, None], row_of, -1)

    half_dim = HEAD_DIM // 2
    inv_freq = jnp.exp(
        jnp.arange(half_dim, dtype=F32) * (-2.0 * math.log(1000000.0) / HEAD_DIM)
    )
    angles = pos.astype(F32)[:, None] * inv_freq[None, :]
    cosine, sine = jnp.cos(angles), jnp.sin(angles)
    cos = jnp.concatenate([cosine, cosine], axis=1)
    sin = jnp.concatenate([-sine, sine], axis=1)

    x, z = hid // RING, hid % RING
    rel = jnp.arange(N_HID, dtype=jnp.int32)
    sources = ((x + rel // RING) % RING) * RING + (z + rel % RING) % RING

    gathered = lax.all_gather(pack(merged, tile_order, (hid % RING)[None]), "hid", axis=0, tiled=True)

    pick = (flat[:TEXT, None] == jnp.arange(REQ_GRP * LEN_MAX)[None, :]).astype(BF)
    text_rows = jnp.dot(
        pick, text_embed.reshape(REQ_GRP * LEN_MAX, FEAT), preferred_element_type=F32
    ).astype(BF)
    weight = (
        jnp.concatenate([query_weight, key_weight, value_weight], axis=1).astype(F32)
        * attn_gain.astype(F32)[:, None]
    ).astype(BF)
    partner = [(i, i ^ 1) for i in range(N_HID)]
    text_blocks, text_where = gather_far(gather_near(text_rows))
    q_text, kv_text = qkv(
        text_blocks, text_where, weight, cos[:TEXT], sin[:TEXT], sources, "qkv_text"
    )
    gathered, q_text, kv_text = lax.optimization_barrier((gathered, q_text, kv_text))
    projected = project(
        gathered,
        proj_weight,
        ln_gain,
        ln_bias,
        proj_bias[None, :],
    )
    tile = lax.all_to_all(
        projected.reshape(N_REQ, TILE // N_REQ, FEAT), "req", split_axis=0, concat_axis=0, tiled=True
    ).reshape(TILE, FEAT)
    other_text = lax.ppermute(kv_text, "hid", partner)
    strip = FEAT // N_REQ
    piece = lax.dynamic_slice_in_dim(out_weight, me * strip, strip, axis=0)
    piece = piece.reshape(strip, N_HID, FEAT).transpose(1, 0, 2)
    piece = lax.all_to_all(piece, "hid", split_axis=0, concat_axis=0, tiled=True)
    piece, tile = lax.optimization_barrier((piece, tile))
    tile_blocks, tile_where = gather_far(gather_near(tile))
    columns = lax.all_gather(piece, "req", axis=1, tiled=True).reshape(D, FEAT)
    q_tile, kv_tile = qkv(
        tile_blocks, tile_where, weight, cos[TEXT:], sin[TEXT:], sources, "qkv_tile"
    )
    other_tile = lax.ppermute(kv_tile, "hid", partner)

    low = (hid % 2 == 0).astype(jnp.int32)[None]
    attended = attend(
        low, q_text, q_tile, kv_text, other_text, kv_tile, other_tile, cos, sin, code
    )
    heads = lax.all_gather(attended, "hid", axis=0, tiled=True)
    hidden = finish(text_embed, tile, heads, columns, row_of[:, :, None])

    last = jnp.sum(jnp.where(slot[None, :] == lengths[:, None] - 1, row_of, 0), axis=1)
    pick_last = (last[:, None] == n[None, :]).astype(BF)
    rows_last = jnp.dot(pick_last, attended, preferred_element_type=F32).astype(BF)
    term = jnp.dot(rows_last, out_weight, preferred_element_type=F32)
    base = jnp.dot(pick_last[:, :TEXT], text_rows, preferred_element_type=F32) + jnp.dot(
        pick_last[:, TEXT:], tile, preferred_element_type=F32
    )
    spot = lax.broadcasted_iota(jnp.int32, (1, N_HID, 1), 1) == hid
    term = term + jnp.where(spot, base[:, None, :], 0.0).reshape(REQ_GRP, D)
    term = over_line(term, along_z)
    full_width = over_line(term, along_x).astype(BF)
    all_last = lax.all_gather(full_width, "req", axis=0, tiled=True)
    last_values = all_last.astype(F32)
    last_squares = jnp.sum(last_values * last_values, axis=1)
    final_norm = jnp.sqrt(last_squares)
    final_scaled = (
        last_values * lax.rsqrt(last_squares / D + 1e-05)[:, None] * final_gain.astype(F32)
    ).astype(BF)
    logits = lax.dot_general(
        final_scaled, head_weight, (((1,), (1,)), ((), ())), preferred_element_type=F32
    )
    top = jnp.max(logits, axis=1)
    for move in (along_z, along_x):
        here, below, above, far_top = line_of(top, move)
        top = jnp.maximum(jnp.maximum(here, below), jnp.maximum(above, far_top))
    logit_max = lax.pmax(top, "req")
    return (hidden, final_norm, logit_max)


def solution(mesh):
    return jax.shard_map(
        shards,
        mesh=mesh,
        in_specs=(
            P(None, "req", "hid"),
            P(),
            P(),
            P(None, "hid"),
            P("hid"),
            P("req", None, "hid"),
            P(),
            P(None, "hid"),
            P(None, "hid"),
            P(None, "hid"),
            P("hid", None),
            P(),
            P(("req", "hid"), None),
            P("req"),
            P(),
            P(),
        ),
        out_specs=(P("req", None, "hid"), P(), P()),
        check_vma=False,
    )
```

```python
import math

import jax
import jax.numpy as jnp
from jax import lax
from jax.experimental import pallas as pl
from jax.experimental.pallas import tpu as pltpu
from jax.sharding import PartitionSpec as P

HEAD_DIM = 128
D = 6144
MERGED = 12800
REQ_GRP = 2
LEN_MAX = 480
LIVE = 640
TILE = 256
TEXT = LIVE - TILE
N_HID = 16
N_REQ = 8
RING = 4
FEAT = D // N_HID
MFEAT = MERGED // N_HID
MAIN = 768
MPAD = 896
BF = jnp.bfloat16
F32 = jnp.float32
VM = pltpu.VMEM


def vmem():
    return pl.BlockSpec(memory_space=pltpu.VMEM)


def params(mib):
    return pltpu.CompilerParams(vmem_limit_bytes=mib << 20)


def shift(block, dx, dz):
    route = []
    for i in range(N_HID):
        x, z = divmod(i, RING)
        route.append((((x + dx) % RING) * RING + (z + dz) % RING, i))
    return lax.ppermute(block, "hid", route)


def line_of(block, move):
    return [block, move(block, -1), move(block, 1), move(block, 2)]


def along_x(b, d):
    return shift(b, d, 0)


def along_z(b, d):
    return shift(b, 0, d)


def join(*blocks):
    total = blocks[0].astype(F32)
    for b in blocks[1:]:
        total = total + b.astype(F32)
    return total


def over_line(block, move):
    own, below, above, far = line_of(block, move)
    return (own + far) + (below + above)


def axes_of(first):
    return (along_z, along_x) if first == 0 else (along_x, along_z)


def gather_near(shard):
    half = shard.shape[0] // 2
    near = []
    for first in (0, 1):
        inner, outer = axes_of(first)
        own = lax.slice_in_dim(shard, first * half, (first + 1) * half, axis=0)
        group = jnp.concatenate(line_of(own, inner), axis=0)
        near.append((group, outer(group, -1), outer(group, 1)))
    return near


def gather_far(near):
    arrays, tables = [], []
    for first in (0, 1):
        _, outer = axes_of(first)
        group, minus, plus = near[first]
        half = group.shape[0] // RING
        far_a = outer(lax.slice_in_dim(minus, 0, 2 * half, axis=0), -1)
        far_b = outer(lax.slice_in_dim(plus, 2 * half, 4 * half, axis=0), 1)
        offs = [0, -1, 1, 2]
        table = {}
        for array, out, part in (
            (group, 0, offs),
            (minus, -1, offs),
            (plus, 1, offs),
            (far_a, 2, offs[:2]),
            (far_b, 2, offs[2:]),
        ):
            arrays.append(array)
            for j, d in enumerate(part):
                rel = (out % RING, d % RING) if first == 0 else (d % RING, out % RING)
                table[rel] = (len(arrays) - 1, j * half)
        tables.append(table)
    order = [(dx, dz) for dx in range(RING) for dz in range(RING)]
    return arrays, [(tables[0][r], tables[1][r]) for r in order]


def in_hbm(x):
    return pltpu.with_memory_space_constraint(x, pltpu.HBM)


def pack_kernel(order_ref, place_ref, x_ref, o_ref, tail):
    def step(g, carry):
        rows = x_ref[order_ref[g]]
        v = rows.astype(F32)
        here = pl.ds(pl.multiple_of(g * 32, 32), 32)
        lane = lax.broadcasted_iota(jnp.int32, (32, 128), 1)
        block = jnp.zeros((32, 128), F32)
        j = 32
        for s in (jnp.sum(v, axis=1, keepdims=True), jnp.sum(v * v, axis=1, keepdims=True)):
            for _ in range(3):
                part = s.astype(BF).astype(F32)
                block = jnp.where(lane == j, part, block)
                s = s - part
                j += 1
        o_ref[here, 0:MAIN] = rows[:, 0:MAIN]
        tail[here, :] = block
        tail[here, 0:32] = v[:, MAIN:MFEAT]
        return carry

    lax.fori_loop(0, N_REQ, step, 0)
    o_ref[:, MAIN:MPAD] = pltpu.roll(tail[...], place_ref[0] * 32, 1).astype(BF)


def pack(merged, tile_order, place):
    return pl.pallas_call(
        pack_kernel,
        out_shape=jax.ShapeDtypeStruct((TILE, MPAD), BF),
        in_specs=[pl.BlockSpec(memory_space=pltpu.SMEM)] * 2 + [vmem()],
        out_specs=vmem(),
        scratch_shapes=[VM((TILE, 128), F32)],
        compiler_params=params(16),
        name="pack",
    )(tile_order, place, merged)


def project_kernel(
    x_hbm, w_hbm, gb_ref, left_ref, pb_ref, o_ref, tail, x, w, wl, acc, sem, x_sem, w_sem
):
    deep = 2 * MAIN
    tails = pltpu.make_async_copy(x_hbm.at[:, pl.ds(MAIN, 128)], tail, sem.at[0])
    lefts = pltpu.make_async_copy(w_hbm.at[:, pl.ds(MAIN, 32), :], wl, sem.at[1])

    def x_copy(k):
        here = pl.ds(pl.multiple_of(k * MAIN, MAIN), MAIN)
        there = x_hbm.at[pl.ds(k * TILE, TILE), pl.ds(0, MAIN)]
        return pltpu.make_async_copy(there, x.at[:, here], x_sem.at[k])

    def pair(part, i):
        return jnp.concatenate([gb_ref[part, pl.ds(2 * i + j, 1), :] for j in (0, 1)], axis=1)

    def w_copy(k):
        here = pl.ds(k * MAIN, MAIN)
        return pltpu.make_async_copy(w_hbm.at[k, pl.ds(0, MAIN), :], w.at[here, :], w_sem.at[k])

    tails.start()
    for k in range(N_HID):
        x_copy(k).start()
        w_copy(k).start()
    lefts.start()
    tails.wait()
    quarter = lax.broadcasted_iota(jnp.int32, (TILE, 128), 1) // 32
    mean = jnp.zeros((TILE, 1), F32)
    square = jnp.zeros((TILE, 1), F32)
    for j in range(RING):
        total = jnp.zeros((TILE, 128), F32)
        for i in range(RING):
            k = RING * i + j
            total = total + tail[k * TILE : (k + 1) * TILE, :].astype(F32)
        at = 32 * ((j + 1) % RING)
        mean = mean + jnp.sum(total[:, at : at + 3], axis=1, keepdims=True)
        square = square + jnp.sum(total[:, at + 3 : at + 6], axis=1, keepdims=True)
    mean = mean * (1.0 / MERGED)
    rstd = lax.rsqrt(square * (1.0 / MERGED) - mean * mean + 1e-05)
    acc[...] = jnp.zeros_like(acc)

    def step(i, carry):
        for j in (0, 1):
            x_copy(2 * i + j).wait()
            w_copy(2 * i + j).wait()
        here = pl.ds(pl.multiple_of(i * deep, deep), deep)
        v = x[:, here].astype(F32)
        normed = (v - mean) * rstd * pair(0, i) + pair(1, i)
        acc[...] += jnp.dot(normed.astype(BF), w[here, :], preferred_element_type=F32)
        return carry

    lax.fori_loop(0, N_HID // 2, step, 0)
    lefts.wait()
    blocks = []
    for i in range(RING):
        v = jnp.zeros((TILE, 128), F32)
        for j in range(RING):
            k = RING * i + j
            v = jnp.where(quarter == j, tail[k * TILE : (k + 1) * TILE, :].astype(F32), v)
        blocks.append(((v - mean) * rstd * left_ref[0, i] + left_ref[1, i]).astype(BF))
    rest = jnp.concatenate(blocks, axis=1)
    y = acc[...] + pb_ref[...] + jnp.dot(
        rest, wl[...].reshape(N_HID * 32, FEAT), preferred_element_type=F32
    )
    y = 0.5 * y * (1.0 + lax.erf(y * math.sqrt(0.5)))
    o_ref[...] = y.astype(BF)


def project(gathered, weight, gain, bias, out_bias):
    both = jnp.stack([gain, bias]).astype(F32).reshape(2, N_HID, MFEAT)
    return pl.pallas_call(
        project_kernel,
        out_shape=jax.ShapeDtypeStruct((TILE, FEAT), BF),
        in_specs=[pl.BlockSpec(memory_space=pl.ANY)] * 2 + [vmem()] * 3,
        out_specs=vmem(),
        scratch_shapes=[
            VM((N_HID * TILE, 128), BF),
            VM((TILE, N_HID * MAIN), BF),
            VM((N_HID * MAIN, FEAT), BF),
            VM((N_HID, 32, FEAT), BF),
            VM((TILE, FEAT), F32),
            pltpu.SemaphoreType.DMA((2,)),
            pltpu.SemaphoreType.DMA((N_HID,)),
            pltpu.SemaphoreType.DMA((N_HID,)),
        ],
        compiler_params=params(30),
        cost_estimate=pl.CostEstimate(
            flops=2 * TILE * MERGED * FEAT, bytes_accessed=17 << 20, transcendentals=0
        ),
        name="project",
    )(
        in_hbm(gathered),
        in_hbm(weight.reshape(N_HID, MFEAT, FEAT)),
        both[:, :, :MAIN],
        both[:, :, MAIN:].reshape(2, RING, 1, 128),
        out_bias,
    )


def turn(v, cos, sin):
    return v * cos + pltpu.roll(v, HEAD_DIM // 2, 1) * sin


def qkv(arrays, where, weight, cos, sin, sources, name):
    half = arrays[0].shape[0] // RING
    rows = 2 * half
    n = len(arrays)
    deep = 4 * FEAT
    cols = FEAT + HEAD_DIM

    def kernel(src_ref, *refs):
        ins = refs[:n]
        w_hbm, cos_ref, sin_ref, q_ref, kv_ref, xs, w, acc, sem = refs[n:]

        def copy(k):
            there = pl.ds(pl.multiple_of(src_ref[k] * FEAT, FEAT), FEAT)
            here = pl.ds(k * FEAT, FEAT)
            return pltpu.make_async_copy(w_hbm.at[there, :], w.at[here, :], sem.at[k])

        for k in range(N_HID):
            copy(k).start()
        square = jnp.zeros((rows, HEAD_DIM), F32)
        for k in range(N_HID):
            block = jnp.concatenate([ins[a][row : row + half, :] for a, row in where[k]], axis=0)
            xs[:, k * FEAT : (k + 1) * FEAT] = block
            v = block.astype(F32)
            v = v * v
            square = square + (v[:, 0:128] + v[:, 128:256] + v[:, 256:384])
        acc[...] = jnp.zeros_like(acc)

        def step(i, carry):
            for j in range(4):
                copy(4 * i + j).wait()
            here = pl.ds(pl.multiple_of(i * deep, deep), deep)
            acc[...] += jnp.dot(xs[:, here], w[here, :], preferred_element_type=F32)
            return carry

        lax.fori_loop(0, RING, step, 0)
        scale = lax.rsqrt(jnp.sum(square, axis=1, keepdims=True) * (1.0 / D) + 1e-05)
        for h in range(FEAT // HEAD_DIM):
            part = acc[:, h * HEAD_DIM : (h + 1) * HEAD_DIM] * scale
            q_ref[:, h * HEAD_DIM : (h + 1) * HEAD_DIM] = turn(
                part, cos_ref[...], sin_ref[...]
            ).astype(BF)
        kv_ref[...] = (acc[:, FEAT:] * scale).astype(BF)

    return pl.pallas_call(
        kernel,
        out_shape=(
            jax.ShapeDtypeStruct((rows, FEAT), BF),
            jax.ShapeDtypeStruct((rows, HEAD_DIM), BF),
        ),
        in_specs=[pl.BlockSpec(memory_space=pltpu.SMEM)]
        + [vmem() for _ in arrays]
        + [pl.BlockSpec(memory_space=pl.ANY), vmem(), vmem()],
        out_specs=(vmem(), vmem()),
        scratch_shapes=[
            VM((rows, D), BF),
            VM((D, cols), BF),
            VM((rows, cols), F32),
            pltpu.SemaphoreType.DMA((N_HID,)),
        ],
        compiler_params=params(20),
        cost_estimate=pl.CostEstimate(
            flops=2 * rows * D * cols, bytes_accessed=12 << 20, transcendentals=0
        ),
        name=name,
    )(sources, *arrays, in_hbm(weight), cos, sin)


def attend_kernel(
    low_ref, qt, qi, ot, pt, oi, pi, cos_ref, sin_ref, row_ref, col_ref, o_ref, qs, keys, vals
):
    upper = low_ref[0] == 0
    lane = lax.broadcasted_iota(jnp.int32, (LIVE, HEAD_DIM), 1)
    own = jnp.concatenate([ot[...], oi[...]], axis=0).astype(F32)
    other = jnp.concatenate([pt[...], pi[...]], axis=0).astype(F32)
    low = jnp.where(upper, other, own)
    high = jnp.where(upper, own, other)
    key = jnp.where(lane < 64, low, pltpu.roll(high, 64, 1))
    val = jnp.where(lane < 64, pltpu.roll(low, 64, 1), high)
    keys[...] = turn(key, cos_ref[...], sin_ref[...]).astype(BF)
    vals[...] = val.astype(BF)
    qs[:TEXT] = qt[...]
    qs[TEXT:] = qi[...]
    code = col_ref[...]

    def block(i, carry):
        rows = pl.ds(pl.multiple_of(i * 128, 128), 128)
        mine = row_ref[rows, :]
        start = jnp.where(mine >= 1024, 1024, 0)
        live = jnp.logical_and(code <= mine, code >= start)
        for h in range(FEAT // HEAD_DIM):
            cols = slice(h * HEAD_DIM, (h + 1) * HEAD_DIM)
            s = lax.dot_general(
                qs[rows, cols], keys[...], (((1,), (1,)), ((), ())), preferred_element_type=F32
            ) * (1.0 / math.sqrt(HEAD_DIM))
            s = jnp.where(live, s, -jnp.inf)
            w = jnp.exp(s - jnp.max(s, axis=1, keepdims=True))
            total = jnp.sum(w, axis=1, keepdims=True)
            mixed = jnp.dot(w.astype(BF), vals[...], preferred_element_type=F32)
            o_ref[rows, cols] = (mixed / total).astype(BF)
        return carry

    lax.fori_loop(0, LIVE // 128, block, 0)


def attend(low, qt, qi, ot, pt, oi, pi, cos, sin, code):
    return pl.pallas_call(
        attend_kernel,
        out_shape=jax.ShapeDtypeStruct((LIVE, FEAT), BF),
        in_specs=[pl.BlockSpec(memory_space=pltpu.SMEM)] + [vmem()] * 10,
        out_specs=vmem(),
        scratch_shapes=[VM((LIVE, FEAT), BF), VM((LIVE, HEAD_DIM), BF), VM((LIVE, HEAD_DIM), BF)],
        compiler_params=params(24),
        cost_estimate=pl.CostEstimate(flops=1 << 30, bytes_accessed=2 << 20, transcendentals=0),
        name="attend",
    )(low, qt, qi, ot, pt, oi, pi, cos, sin, code[:, None], code[None, :])


def finish_kernel(
    text_ref, tile_ref, a_hbm, w_hbm, slot_ref, o_ref, a, w, acc, sums, a_sem, w_sem
):
    two = 2 * FEAT

    def a_copy(k):
        here = pl.ds(pl.multiple_of(k * FEAT, FEAT), FEAT)
        return pltpu.make_async_copy(a_hbm.at[pl.ds(pl.multiple_of(k * LIVE, LIVE), LIVE), :], a.at[:, here], a_sem.at[k])

    def w_copy(k, r):
        return pltpu.make_async_copy(w_hbm.at[r, k], w.at[k, r], w_sem.at[k, r])

    def begin(k, carry):
        a_copy(k).start()
        for r in range(N_REQ):
            w_copy(k, r).start()
        return carry

    lax.fori_loop(0, N_HID, begin, 0)
    acc[...] = jnp.zeros_like(acc)

    def step(i, carry):
        for j in (0, 1):
            a_copy(2 * i + j).wait()
            for r in range(N_REQ):
                w_copy(2 * i + j, r).wait()
        here = pl.ds(pl.multiple_of(i * two, two), two)
        block = w[pl.ds(2 * i, 2)].reshape(two, FEAT)
        acc[...] += jnp.dot(a[:, here], block, preferred_element_type=F32)
        return carry

    lax.fori_loop(0, N_HID // 2, step, 0)
    sums[...] = acc[...].astype(BF)

    def one(r, carry):
        row = slot_ref[r]
        pick = (lax.broadcasted_iota(jnp.int32, (LEN_MAX, LIVE), 1) == row).astype(BF)
        moved = jnp.dot(pick, sums[...], preferred_element_type=F32)
        image = jnp.dot(pick[:, TEXT:], tile_ref[...], preferred_element_type=F32)
        base = jnp.where(row >= TEXT, image, text_ref[r].astype(F32))
        o_ref[r] = (base + moved).astype(BF)
        return carry

    lax.fori_loop(0, REQ_GRP, one, 0)


def finish(text, tile, heads, weight, slots):
    return pl.pallas_call(
        finish_kernel,
        out_shape=jax.ShapeDtypeStruct((REQ_GRP, LEN_MAX, FEAT), BF),
        in_specs=[vmem()] * 2 + [pl.BlockSpec(memory_space=pl.ANY)] * 2 + [vmem()],
        out_specs=vmem(),
        scratch_shapes=[
            VM((LIVE, D), BF),
            VM((N_HID, N_REQ, FEAT // N_REQ, FEAT), BF),
            VM((LIVE, FEAT), F32),
            VM((LIVE, FEAT), BF),
            pltpu.SemaphoreType.DMA((N_HID,)),
            pltpu.SemaphoreType.DMA((N_HID, N_REQ)),
        ],
        compiler_params=params(32),
        cost_estimate=pl.CostEstimate(
            flops=2 * LIVE * FEAT * D, bytes_accessed=14 << 20, transcendentals=0
        ),
        name="finish",
    )(text, tile, in_hbm(heads), in_hbm(weight), slots)


def shards(
    merged,
    ln_gain,
    ln_bias,
    proj_weight,
    proj_bias,
    text_embed,
    attn_gain,
    query_weight,
    key_weight,
    value_weight,
    out_weight,
    final_gain,
    head_weight,
    lengths,
    tile_request,
    insert_pos,
):
    hid = lax.axis_index("hid")
    me = lax.axis_index("req")
    owners = tile_request // REQ_GRP
    tiles = jnp.arange(N_REQ, dtype=jnp.int32)
    tile_order = jnp.sum(
        jnp.where(owners[None, :] == tiles[:, None], tiles[None, :], 0), axis=1
    ).astype(jnp.int32)
    mine = owners == me
    local_req = jnp.sum(jnp.where(mine, tile_request % REQ_GRP, 0))
    start = jnp.sum(jnp.where(mine, insert_pos, 0))
    len_a = lengths[0]
    first = local_req * len_a + start

    n = jnp.arange(LIVE, dtype=jnp.int32)
    packed = jnp.where(n < TEXT, jnp.where(n < first, n, n + TILE), n - TEXT + first)
    second = packed >= len_a
    pos = packed - jnp.where(second, len_a, 0)
    code = pos + jnp.where(second, 1024, 0)
    flat = pos + jnp.where(second, LEN_MAX, 0)
    slot = jnp.arange(LEN_MAX, dtype=jnp.int32)
    at = jnp.stack([slot, slot + len_a])
    in_tile = jnp.logical_and(at >= first, at < first + TILE)
    row_of = jnp.where(in_tile, at - first + TEXT, jnp.where(at < first, at, at - TILE))
    row_of = jnp.where(slot[None, :] < lengths[:, None], row_of, -1)

    half_dim = HEAD_DIM // 2
    inv_freq = jnp.exp(
        jnp.arange(half_dim, dtype=F32) * (-2.0 * math.log(1000000.0) / HEAD_DIM)
    )
    angles = pos.astype(F32)[:, None] * inv_freq[None, :]
    cosine, sine = jnp.cos(angles), jnp.sin(angles)
    cos = jnp.concatenate([cosine, cosine], axis=1)
    sin = jnp.concatenate([-sine, sine], axis=1)

    x, z = hid // RING, hid % RING
    rel = jnp.arange(N_HID, dtype=jnp.int32)
    sources = ((x + rel // RING) % RING) * RING + (z + rel % RING) % RING

    gathered = lax.all_gather(pack(merged, tile_order, (hid % RING)[None]), "hid", axis=0, tiled=True)

    pick = (flat[:TEXT, None] == jnp.arange(REQ_GRP * LEN_MAX)[None, :]).astype(BF)
    text_rows = jnp.dot(
        pick, text_embed.reshape(REQ_GRP * LEN_MAX, FEAT), preferred_element_type=F32
    ).astype(BF)
    weight = (
        jnp.concatenate([query_weight, key_weight, value_weight], axis=1).astype(F32)
        * attn_gain.astype(F32)[:, None]
    ).astype(BF)
    partner = [(i, i ^ 1) for i in range(N_HID)]
    text_blocks, text_where = gather_far(gather_near(text_rows))
    strip = FEAT // N_REQ
    piece = lax.dynamic_slice_in_dim(out_weight, me * strip, strip, axis=0)
    piece = piece.reshape(strip, N_HID, FEAT).transpose(1, 0, 2)
    piece, *text_blocks[3:5] = lax.optimization_barrier((piece, *text_blocks[3:5]))
    piece = lax.all_to_all(piece, "hid", split_axis=0, concat_axis=0, tiled=True)
    q_text, kv_text = qkv(
        text_blocks, text_where, weight, cos[:TEXT], sin[:TEXT], sources, "qkv_text"
    )
    gathered, q_text, kv_text = lax.optimization_barrier((gathered, q_text, kv_text))
    projected = project(
        gathered,
        proj_weight,
        ln_gain,
        ln_bias,
        proj_bias[None, :],
    )
    tile = lax.all_to_all(
        projected.reshape(N_REQ, TILE // N_REQ, FEAT), "req", split_axis=0, concat_axis=0, tiled=True
    ).reshape(TILE, FEAT)
    other_text = lax.ppermute(kv_text, "hid", partner)
    piece, tile = lax.optimization_barrier((piece, tile))
    tile_blocks, tile_where = gather_far(gather_near(tile))
    columns = lax.all_gather(piece, "req", axis=0, tiled=False)
    q_tile, kv_tile = qkv(
        tile_blocks, tile_where, weight, cos[TEXT:], sin[TEXT:], sources, "qkv_tile"
    )
    other_tile = lax.ppermute(kv_tile, "hid", partner)

    low = (hid % 2 == 0).astype(jnp.int32)[None]
    attended = attend(
        low, q_text, q_tile, kv_text, other_text, kv_tile, other_tile, cos, sin, code
    )
    heads = lax.all_gather(attended, "hid", axis=0, tiled=True)
    hidden = finish(text_embed, tile, heads, columns, row_of[:, :, None])

    last = jnp.sum(jnp.where(slot[None, :] == lengths[:, None] - 1, row_of, 0), axis=1)
    pick_last = (last[:, None] == n[None, :]).astype(BF)
    rows_last = jnp.dot(pick_last, attended, preferred_element_type=F32).astype(BF)
    term = jnp.dot(rows_last, out_weight, preferred_element_type=F32)
    base = jnp.dot(pick_last[:, :TEXT], text_rows, preferred_element_type=F32) + jnp.dot(
        pick_last[:, TEXT:], tile, preferred_element_type=F32
    )
    spot = lax.broadcasted_iota(jnp.int32, (1, N_HID, 1), 1) == hid
    term = term + jnp.where(spot, base[:, None, :], 0.0).reshape(REQ_GRP, D)
    term = over_line(term, along_z)
    full_width = over_line(term, along_x).astype(BF)
    all_last = lax.all_gather(full_width, "req", axis=0, tiled=True)
    last_values = all_last.astype(F32)
    last_squares = jnp.sum(last_values * last_values, axis=1)
    final_norm = jnp.sqrt(last_squares)
    final_scaled = (
        last_values * lax.rsqrt(last_squares / D + 1e-05)[:, None] * final_gain.astype(F32)
    ).astype(BF)
    logits = lax.dot_general(
        final_scaled, head_weight, (((1,), (1,)), ((), ())), preferred_element_type=F32
    )
    top = jnp.max(logits, axis=1)
    for move in (along_z, along_x):
        here, below, above, far_top = line_of(top, move)
        top = jnp.maximum(jnp.maximum(here, below), jnp.maximum(above, far_top))
    logit_max = lax.pmax(top, "req")
    return (hidden, final_norm, logit_max)


def solution(mesh):
    return jax.shard_map(
        shards,
        mesh=mesh,
        in_specs=(
            P(None, "req", "hid"),
            P(),
            P(),
            P(None, "hid"),
            P("hid"),
            P("req", None, "hid"),
            P(),
            P(None, "hid"),
            P(None, "hid"),
            P(None, "hid"),
            P("hid", None),
            P(),
            P(("req", "hid"), None),
            P("req"),
            P(),
            P(),
        ),
        out_specs=(P("req", None, "hid"), P(), P()),
        check_vma=False,
    )
```

```python
import math

import jax
import jax.numpy as jnp
from jax import lax
from jax.experimental import pallas as pl
from jax.experimental.pallas import tpu as pltpu
from jax.sharding import PartitionSpec as P

HEAD_DIM = 128
D = 6144
MERGED = 12800
REQ_GRP = 2
LEN_MAX = 480
LIVE = 640
TILE = 256
TEXT = LIVE - TILE
N_HID = 16
N_REQ = 8
RING = 4
FEAT = D // N_HID
MFEAT = MERGED // N_HID
MAIN = 768
MPAD = 896
BF = jnp.bfloat16
F32 = jnp.float32
VM = pltpu.VMEM


def vmem():
    return pl.BlockSpec(memory_space=pltpu.VMEM)


def params(mib):
    return pltpu.CompilerParams(vmem_limit_bytes=mib << 20)


def shift(block, dx, dz):
    route = []
    for i in range(N_HID):
        x, z = divmod(i, RING)
        route.append((((x + dx) % RING) * RING + (z + dz) % RING, i))
    return lax.ppermute(block, "hid", route)


def line_of(block, move):
    return [block, move(block, -1), move(block, 1), move(block, 2)]


def along_x(b, d):
    return shift(b, d, 0)


def along_z(b, d):
    return shift(b, 0, d)


def join(*blocks):
    total = blocks[0].astype(F32)
    for b in blocks[1:]:
        total = total + b.astype(F32)
    return total


def over_line(block, move):
    own, below, above, far = line_of(block, move)
    return (own + far) + (below + above)


def axes_of(first):
    return (along_z, along_x) if first == 0 else (along_x, along_z)


def gather_near(shard):
    half = shard.shape[0] // 2
    near = []
    for first in (0, 1):
        inner, outer = axes_of(first)
        own = lax.slice_in_dim(shard, first * half, (first + 1) * half, axis=0)
        group = jnp.concatenate(line_of(own, inner), axis=0)
        near.append((group, outer(group, -1), outer(group, 1)))
    return near


def gather_far(near):
    arrays, tables = [], []
    for first in (0, 1):
        _, outer = axes_of(first)
        group, minus, plus = near[first]
        half = group.shape[0] // RING
        far_a = outer(lax.slice_in_dim(minus, 0, 2 * half, axis=0), -1)
        far_b = outer(lax.slice_in_dim(plus, 2 * half, 4 * half, axis=0), 1)
        offs = [0, -1, 1, 2]
        table = {}
        for array, out, part in (
            (group, 0, offs),
            (minus, -1, offs),
            (plus, 1, offs),
            (far_a, 2, offs[:2]),
            (far_b, 2, offs[2:]),
        ):
            arrays.append(array)
            for j, d in enumerate(part):
                rel = (out % RING, d % RING) if first == 0 else (d % RING, out % RING)
                table[rel] = (len(arrays) - 1, j * half)
        tables.append(table)
    order = [(dx, dz) for dx in range(RING) for dz in range(RING)]
    return arrays, [(tables[0][r], tables[1][r]) for r in order]


def in_hbm(x):
    return pltpu.with_memory_space_constraint(x, pltpu.HBM)


def pack_kernel(order_ref, place_ref, x_ref, o_ref, tail):
    def step(g, carry):
        rows = x_ref[order_ref[g]]
        v = rows.astype(F32)
        here = pl.ds(pl.multiple_of(g * 32, 32), 32)
        lane = lax.broadcasted_iota(jnp.int32, (32, 128), 1)
        block = jnp.zeros((32, 128), F32)
        j = 32
        for s in (jnp.sum(v, axis=1, keepdims=True), jnp.sum(v * v, axis=1, keepdims=True)):
            for _ in range(3):
                part = s.astype(BF).astype(F32)
                block = jnp.where(lane == j, part, block)
                s = s - part
                j += 1
        o_ref[here, 0:MAIN] = rows[:, 0:MAIN]
        tail[here, :] = block
        tail[here, 0:32] = v[:, MAIN:MFEAT]
        return carry

    lax.fori_loop(0, N_REQ, step, 0, unroll=True)
    o_ref[:, MAIN:MPAD] = pltpu.roll(tail[...], place_ref[0] * 32, 1).astype(BF)


def pack(merged, tile_order, place):
    return pl.pallas_call(
        pack_kernel,
        out_shape=jax.ShapeDtypeStruct((TILE, MPAD), BF),
        in_specs=[pl.BlockSpec(memory_space=pltpu.SMEM)] * 2 + [vmem()],
        out_specs=vmem(),
        scratch_shapes=[VM((TILE, 128), F32)],
        compiler_params=params(16),
        name="pack",
    )(tile_order, place, merged)


def project_kernel(
    x_hbm, w_hbm, gb_ref, left_ref, pb_ref, o_ref, tail, x, w, wl, acc, sem, x_sem, w_sem
):
    deep = 2 * MAIN
    tails = pltpu.make_async_copy(x_hbm.at[:, pl.ds(MAIN, 128)], tail, sem.at[0])
    lefts = pltpu.make_async_copy(w_hbm.at[:, pl.ds(MAIN, 32), :], wl, sem.at[1])

    def x_copy(k):
        here = pl.ds(pl.multiple_of(k * MAIN, MAIN), MAIN)
        there = x_hbm.at[pl.ds(k * TILE, TILE), pl.ds(0, MAIN)]
        return pltpu.make_async_copy(there, x.at[:, here], x_sem.at[k])

    def pair(part, i):
        return jnp.concatenate([gb_ref[part, pl.ds(2 * i + j, 1), :] for j in (0, 1)], axis=1)

    def w_copy(k):
        here = pl.ds(k * MAIN, MAIN)
        return pltpu.make_async_copy(w_hbm.at[k, pl.ds(0, MAIN), :], w.at[here, :], w_sem.at[k])

    tails.start()
    for k in range(N_HID):
        x_copy(k).start()
        w_copy(k).start()
    lefts.start()
    tails.wait()
    quarter = lax.broadcasted_iota(jnp.int32, (TILE, 128), 1) // 32
    mean = jnp.zeros((TILE, 1), F32)
    square = jnp.zeros((TILE, 1), F32)
    for j in range(RING):
        total = jnp.zeros((TILE, 128), F32)
        for i in range(RING):
            k = RING * i + j
            total = total + tail[k * TILE : (k + 1) * TILE, :].astype(F32)
        at = 32 * ((j + 1) % RING)
        mean = mean + jnp.sum(total[:, at : at + 3], axis=1, keepdims=True)
        square = square + jnp.sum(total[:, at + 3 : at + 6], axis=1, keepdims=True)
    mean = mean * (1.0 / MERGED)
    rstd = lax.rsqrt(square * (1.0 / MERGED) - mean * mean + 1e-05)
    acc[...] = jnp.zeros_like(acc)

    def step(i, carry):
        for j in (0, 1):
            x_copy(2 * i + j).wait()
            w_copy(2 * i + j).wait()
        here = pl.ds(pl.multiple_of(i * deep, deep), deep)
        v = x[:, here].astype(F32)
        normed = (v - mean) * rstd * pair(0, i) + pair(1, i)
        acc[...] += jnp.dot(normed.astype(BF), w[here, :], preferred_element_type=F32)
        return carry

    lax.fori_loop(0, N_HID // 2, step, 0)
    lefts.wait()
    blocks = []
    for i in range(RING):
        v = jnp.zeros((TILE, 128), F32)
        for j in range(RING):
            k = RING * i + j
            v = jnp.where(quarter == j, tail[k * TILE : (k + 1) * TILE, :].astype(F32), v)
        blocks.append(((v - mean) * rstd * left_ref[0, i] + left_ref[1, i]).astype(BF))
    rest = jnp.concatenate(blocks, axis=1)
    y = acc[...] + pb_ref[...] + jnp.dot(
        rest, wl[...].reshape(N_HID * 32, FEAT), preferred_element_type=F32
    )
    y = 0.5 * y * (1.0 + lax.erf(y * math.sqrt(0.5)))
    o_ref[...] = y.astype(BF)


def project(gathered, weight, gain, bias, out_bias):
    both = jnp.stack([gain, bias]).astype(F32).reshape(2, N_HID, MFEAT)
    return pl.pallas_call(
        project_kernel,
        out_shape=jax.ShapeDtypeStruct((TILE, FEAT), BF),
        in_specs=[pl.BlockSpec(memory_space=pl.ANY)] * 2 + [vmem()] * 3,
        out_specs=vmem(),
        scratch_shapes=[
            VM((N_HID * TILE, 128), BF),
            VM((TILE, N_HID * MAIN), BF),
            VM((N_HID * MAIN, FEAT), BF),
            VM((N_HID, 32, FEAT), BF),
            VM((TILE, FEAT), F32),
            pltpu.SemaphoreType.DMA((2,)),
            pltpu.SemaphoreType.DMA((N_HID,)),
            pltpu.SemaphoreType.DMA((N_HID,)),
        ],
        compiler_params=params(30),
        cost_estimate=pl.CostEstimate(
            flops=2 * TILE * MERGED * FEAT, bytes_accessed=17 << 20, transcendentals=0
        ),
        name="project",
    )(
        in_hbm(gathered),
        in_hbm(weight.reshape(N_HID, MFEAT, FEAT)),
        both[:, :, :MAIN],
        both[:, :, MAIN:].reshape(2, RING, 1, 128),
        out_bias,
    )


def turn(v, cos, sin):
    return v * cos + pltpu.roll(v, HEAD_DIM // 2, 1) * sin


def qkv(arrays, where, weight, cos, sin, sources, name):
    half = arrays[0].shape[0] // RING
    rows = 2 * half
    n = len(arrays)
    deep = 4 * FEAT
    cols = FEAT + HEAD_DIM

    def kernel(src_ref, *refs):
        ins = refs[:n]
        w_hbm, cos_ref, sin_ref, q_ref, kv_ref, xs, w, acc, sem = refs[n:]

        def copy(k):
            there = pl.ds(pl.multiple_of(src_ref[k] * FEAT, FEAT), FEAT)
            here = pl.ds(k * FEAT, FEAT)
            return pltpu.make_async_copy(w_hbm.at[there, :], w.at[here, :], sem.at[k])

        for k in range(N_HID):
            copy(k).start()
        square = jnp.zeros((rows, HEAD_DIM), F32)
        for k in range(N_HID):
            block = jnp.concatenate([ins[a][row : row + half, :] for a, row in where[k]], axis=0)
            xs[:, k * FEAT : (k + 1) * FEAT] = block
            v = block.astype(F32)
            v = v * v
            square = square + (v[:, 0:128] + v[:, 128:256] + v[:, 256:384])
        acc[...] = jnp.zeros_like(acc)

        def step(i, carry):
            for j in range(4):
                copy(4 * i + j).wait()
            here = pl.ds(pl.multiple_of(i * deep, deep), deep)
            acc[...] += jnp.dot(xs[:, here], w[here, :], preferred_element_type=F32)
            return carry

        lax.fori_loop(0, RING, step, 0)
        scale = lax.rsqrt(jnp.sum(square, axis=1, keepdims=True) * (1.0 / D) + 1e-05)
        for h in range(FEAT // HEAD_DIM):
            part = acc[:, h * HEAD_DIM : (h + 1) * HEAD_DIM] * scale
            q_ref[:, h * HEAD_DIM : (h + 1) * HEAD_DIM] = turn(
                part, cos_ref[...], sin_ref[...]
            ).astype(BF)
        kv_ref[...] = (acc[:, FEAT:] * scale).astype(BF)

    return pl.pallas_call(
        kernel,
        out_shape=(
            jax.ShapeDtypeStruct((rows, FEAT), BF),
            jax.ShapeDtypeStruct((rows, HEAD_DIM), BF),
        ),
        in_specs=[pl.BlockSpec(memory_space=pltpu.SMEM)]
        + [vmem() for _ in arrays]
        + [pl.BlockSpec(memory_space=pl.ANY), vmem(), vmem()],
        out_specs=(vmem(), vmem()),
        scratch_shapes=[
            VM((rows, D), BF),
            VM((D, cols), BF),
            VM((rows, cols), F32),
            pltpu.SemaphoreType.DMA((N_HID,)),
        ],
        compiler_params=params(20),
        cost_estimate=pl.CostEstimate(
            flops=2 * rows * D * cols, bytes_accessed=12 << 20, transcendentals=0
        ),
        name=name,
    )(sources, *arrays, in_hbm(weight), cos, sin)


def attend_kernel(
    low_ref, qt, qi, ot, pt, oi, pi, cos_ref, sin_ref, row_ref, col_ref, o_ref, qs, keys, vals
):
    upper = low_ref[0] == 0
    lane = lax.broadcasted_iota(jnp.int32, (LIVE, HEAD_DIM), 1)
    own = jnp.concatenate([ot[...], oi[...]], axis=0).astype(F32)
    other = jnp.concatenate([pt[...], pi[...]], axis=0).astype(F32)
    low = jnp.where(upper, other, own)
    high = jnp.where(upper, own, other)
    key = jnp.where(lane < 64, low, pltpu.roll(high, 64, 1))
    val = jnp.where(lane < 64, pltpu.roll(low, 64, 1), high)
    keys[...] = turn(key, cos_ref[...], sin_ref[...]).astype(BF)
    vals[...] = val.astype(BF)
    qs[:TEXT] = qt[...]
    qs[TEXT:] = qi[...]
    code = col_ref[...]

    def block(i, carry):
        rows = pl.ds(pl.multiple_of(i * 128, 128), 128)
        mine = row_ref[rows, :]
        start = jnp.where(mine >= 1024, 1024, 0)
        live = jnp.logical_and(code <= mine, code >= start)
        for h in range(FEAT // HEAD_DIM):
            cols = slice(h * HEAD_DIM, (h + 1) * HEAD_DIM)
            s = lax.dot_general(
                qs[rows, cols], keys[...], (((1,), (1,)), ((), ())), preferred_element_type=F32
            ) * (1.0 / math.sqrt(HEAD_DIM))
            s = jnp.where(live, s, -jnp.inf)
            w = jnp.exp(s - jnp.max(s, axis=1, keepdims=True))
            total = jnp.sum(w, axis=1, keepdims=True)
            mixed = jnp.dot(w.astype(BF), vals[...], preferred_element_type=F32)
            o_ref[rows, cols] = (mixed / total).astype(BF)
        return carry

    lax.fori_loop(0, LIVE // 128, block, 0)


def attend(low, qt, qi, ot, pt, oi, pi, cos, sin, code):
    return pl.pallas_call(
        attend_kernel,
        out_shape=jax.ShapeDtypeStruct((LIVE, FEAT), BF),
        in_specs=[pl.BlockSpec(memory_space=pltpu.SMEM)] + [vmem()] * 10,
        out_specs=vmem(),
        scratch_shapes=[VM((LIVE, FEAT), BF), VM((LIVE, HEAD_DIM), BF), VM((LIVE, HEAD_DIM), BF)],
        compiler_params=params(24),
        cost_estimate=pl.CostEstimate(flops=1 << 30, bytes_accessed=2 << 20, transcendentals=0),
        name="attend",
    )(low, qt, qi, ot, pt, oi, pi, cos, sin, code[:, None], code[None, :])


def finish_kernel(
    text_ref, tile_ref, a_hbm, w_hbm, slot_ref, o_ref, a, w, acc, sums, a_sem, w_sem
):
    two = 2 * FEAT

    def a_copy(k):
        here = pl.ds(pl.multiple_of(k * FEAT, FEAT), FEAT)
        return pltpu.make_async_copy(a_hbm.at[pl.ds(pl.multiple_of(k * LIVE, LIVE), LIVE), :], a.at[:, here], a_sem.at[k])

    def w_copy(k, r):
        return pltpu.make_async_copy(w_hbm.at[r, k], w.at[k, r], w_sem.at[k, r])

    def begin(k, carry):
        a_copy(k).start()
        for r in range(N_REQ):
            w_copy(k, r).start()
        return carry

    lax.fori_loop(0, N_HID, begin, 0)
    acc[...] = jnp.zeros_like(acc)

    def step(i, carry):
        for j in (0, 1):
            a_copy(2 * i + j).wait()
            for r in range(N_REQ):
                w_copy(2 * i + j, r).wait()
        here = pl.ds(pl.multiple_of(i * two, two), two)
        block = w[pl.ds(2 * i, 2)].reshape(two, FEAT)
        acc[...] += jnp.dot(a[:, here], block, preferred_element_type=F32)
        return carry

    lax.fori_loop(0, N_HID // 2, step, 0)
    sums[...] = acc[...].astype(BF)

    def one(r, carry):
        row = slot_ref[r]
        pick = (lax.broadcasted_iota(jnp.int32, (LEN_MAX, LIVE), 1) == row).astype(BF)
        moved = jnp.dot(pick, sums[...], preferred_element_type=F32)
        image = jnp.dot(pick[:, TEXT:], tile_ref[...], preferred_element_type=F32)
        base = jnp.where(row >= TEXT, image, text_ref[r].astype(F32))
        o_ref[r] = (base + moved).astype(BF)
        return carry

    lax.fori_loop(0, REQ_GRP, one, 0)


def finish(text, tile, heads, weight, slots):
    return pl.pallas_call(
        finish_kernel,
        out_shape=jax.ShapeDtypeStruct((REQ_GRP, LEN_MAX, FEAT), BF),
        in_specs=[vmem()] * 2 + [pl.BlockSpec(memory_space=pl.ANY)] * 2 + [vmem()],
        out_specs=vmem(),
        scratch_shapes=[
            VM((LIVE, D), BF),
            VM((N_HID, N_REQ, FEAT // N_REQ, FEAT), BF),
            VM((LIVE, FEAT), F32),
            VM((LIVE, FEAT), BF),
            pltpu.SemaphoreType.DMA((N_HID,)),
            pltpu.SemaphoreType.DMA((N_HID, N_REQ)),
        ],
        compiler_params=params(32),
        cost_estimate=pl.CostEstimate(
            flops=2 * LIVE * FEAT * D, bytes_accessed=14 << 20, transcendentals=0
        ),
        name="finish",
    )(text, tile, in_hbm(heads), in_hbm(weight), slots)


def shards(
    merged,
    ln_gain,
    ln_bias,
    proj_weight,
    proj_bias,
    text_embed,
    attn_gain,
    query_weight,
    key_weight,
    value_weight,
    out_weight,
    final_gain,
    head_weight,
    lengths,
    tile_request,
    insert_pos,
):
    hid = lax.axis_index("hid")
    me = lax.axis_index("req")
    owners = tile_request // REQ_GRP
    tiles = jnp.arange(N_REQ, dtype=jnp.int32)
    tile_order = jnp.sum(
        jnp.where(owners[None, :] == tiles[:, None], tiles[None, :], 0), axis=1
    ).astype(jnp.int32)
    mine = owners == me
    local_req = jnp.sum(jnp.where(mine, tile_request % REQ_GRP, 0))
    start = jnp.sum(jnp.where(mine, insert_pos, 0))
    len_a = lengths[0]
    first = local_req * len_a + start

    n = jnp.arange(LIVE, dtype=jnp.int32)
    packed = jnp.where(n < TEXT, jnp.where(n < first, n, n + TILE), n - TEXT + first)
    second = packed >= len_a
    pos = packed - jnp.where(second, len_a, 0)
    code = pos + jnp.where(second, 1024, 0)
    flat = pos + jnp.where(second, LEN_MAX, 0)
    slot = jnp.arange(LEN_MAX, dtype=jnp.int32)
    at = jnp.stack([slot, slot + len_a])
    in_tile = jnp.logical_and(at >= first, at < first + TILE)
    row_of = jnp.where(in_tile, at - first + TEXT, jnp.where(at < first, at, at - TILE))
    row_of = jnp.where(slot[None, :] < lengths[:, None], row_of, -1)

    half_dim = HEAD_DIM // 2
    inv_freq = jnp.exp(
        jnp.arange(half_dim, dtype=F32) * (-2.0 * math.log(1000000.0) / HEAD_DIM)
    )
    angles = pos.astype(F32)[:, None] * inv_freq[None, :]
    cosine, sine = jnp.cos(angles), jnp.sin(angles)
    cos = jnp.concatenate([cosine, cosine], axis=1)
    sin = jnp.concatenate([-sine, sine], axis=1)

    x, z = hid // RING, hid % RING
    rel = jnp.arange(N_HID, dtype=jnp.int32)
    sources = ((x + rel // RING) % RING) * RING + (z + rel % RING) % RING

    gathered = lax.all_gather(pack(merged, tile_order, (hid % RING)[None]), "hid", axis=0, tiled=True)

    pick = (flat[:TEXT, None] == jnp.arange(REQ_GRP * LEN_MAX)[None, :]).astype(BF)
    text_rows = jnp.dot(
        pick, text_embed.reshape(REQ_GRP * LEN_MAX, FEAT), preferred_element_type=F32
    ).astype(BF)
    weight = (
        jnp.concatenate([query_weight, key_weight, value_weight], axis=1).astype(F32)
        * attn_gain.astype(F32)[:, None]
    ).astype(BF)
    partner = [(i, i ^ 1) for i in range(N_HID)]
    text_blocks, text_where = gather_far(gather_near(text_rows))
    strip = FEAT // N_REQ
    piece = lax.dynamic_slice_in_dim(out_weight, me * strip, strip, axis=0)
    piece = piece.reshape(strip, N_HID, FEAT).transpose(1, 0, 2)
    q_text, kv_text = qkv(
        text_blocks, text_where, weight, cos[:TEXT], sin[:TEXT], sources, "qkv_text"
    )
    gathered, piece, q_text, kv_text = lax.optimization_barrier((gathered, piece, q_text, kv_text))
    piece = lax.all_to_all(piece, "hid", split_axis=0, concat_axis=0, tiled=True)
    projected = project(
        gathered,
        proj_weight,
        ln_gain,
        ln_bias,
        proj_bias[None, :],
    )
    projected, piece = lax.optimization_barrier((projected, piece))
    tile = lax.all_to_all(
        projected.reshape(N_REQ, TILE // N_REQ, FEAT), "req", split_axis=0, concat_axis=0, tiled=True
    ).reshape(TILE, FEAT)
    other_text = lax.ppermute(kv_text, "hid", partner)
    piece, tile = lax.optimization_barrier((piece, tile))
    tile_blocks, tile_where = gather_far(gather_near(tile))
    columns = lax.all_gather(piece, "req", axis=0, tiled=False)
    q_tile, kv_tile = qkv(
        tile_blocks, tile_where, weight, cos[TEXT:], sin[TEXT:], sources, "qkv_tile"
    )
    other_tile = lax.ppermute(kv_tile, "hid", partner)

    low = (hid % 2 == 0).astype(jnp.int32)[None]
    attended = attend(
        low, q_text, q_tile, kv_text, other_text, kv_tile, other_tile, cos, sin, code
    )
    heads = lax.all_gather(attended, "hid", axis=0, tiled=True)
    hidden = finish(text_embed, tile, heads, columns, row_of[:, :, None])

    last = jnp.sum(jnp.where(slot[None, :] == lengths[:, None] - 1, row_of, 0), axis=1)
    pick_last = (last[:, None] == n[None, :]).astype(BF)
    rows_last = jnp.dot(pick_last, attended, preferred_element_type=F32).astype(BF)
    term = jnp.dot(rows_last, out_weight, preferred_element_type=F32)
    base = jnp.dot(pick_last[:, :TEXT], text_rows, preferred_element_type=F32) + jnp.dot(
        pick_last[:, TEXT:], tile, preferred_element_type=F32
    )
    spot = lax.broadcasted_iota(jnp.int32, (1, N_HID, 1), 1) == hid
    term = term + jnp.where(spot, base[:, None, :], 0.0).reshape(REQ_GRP, D)
    term = over_line(term, along_z)
    full_width = over_line(term, along_x).astype(BF)
    all_last = lax.all_gather(full_width, "req", axis=0, tiled=True)
    last_values = all_last.astype(F32)
    last_squares = jnp.sum(last_values * last_values, axis=1)
    final_norm = jnp.sqrt(last_squares)
    final_scaled = (
        last_values * lax.rsqrt(last_squares / D + 1e-05)[:, None] * final_gain.astype(F32)
    ).astype(BF)
    logits = lax.dot_general(
        final_scaled, head_weight, (((1,), (1,)), ((), ())), preferred_element_type=F32
    )
    top = jnp.max(logits, axis=1)
    for move in (along_z, along_x):
        here, below, above, far_top = line_of(top, move)
        top = jnp.maximum(jnp.maximum(here, below), jnp.maximum(above, far_top))
    logit_max = lax.pmax(top, "req")
    return (hidden, final_norm, logit_max)


def solution(mesh):
    return jax.shard_map(
        shards,
        mesh=mesh,
        in_specs=(
            P(None, "req", "hid"),
            P(),
            P(),
            P(None, "hid"),
            P("hid"),
            P("req", None, "hid"),
            P(),
            P(None, "hid"),
            P(None, "hid"),
            P(None, "hid"),
            P("hid", None),
            P(),
            P(("req", "hid"), None),
            P("req"),
            P(),
            P(),
        ),
        out_specs=(P("req", None, "hid"), P(), P()),
        check_vma=False,
    )
```

```python
import math

import jax
import jax.numpy as jnp
from jax import lax
from jax.experimental import pallas as pl
from jax.experimental.pallas import tpu as pltpu
from jax.sharding import PartitionSpec as P

HEAD_DIM = 128
D = 6144
MERGED = 12800
REQ_GRP = 2
LEN_MAX = 480
LIVE = 640
TILE = 256
TEXT = LIVE - TILE
N_HID = 16
N_REQ = 8
RING = 4
FEAT = D // N_HID
MFEAT = MERGED // N_HID
MAIN = 768
MPAD = 896
BF = jnp.bfloat16
F32 = jnp.float32
VM = pltpu.VMEM


def vmem():
    return pl.BlockSpec(memory_space=pltpu.VMEM)


def params(mib):
    return pltpu.CompilerParams(vmem_limit_bytes=mib << 20)


def shift(block, dx, dz):
    route = []
    for i in range(N_HID):
        x, z = divmod(i, RING)
        route.append((((x + dx) % RING) * RING + (z + dz) % RING, i))
    return lax.ppermute(block, "hid", route)


def line_of(block, move):
    return [block, move(block, -1), move(block, 1), move(block, 2)]


def along_x(b, d):
    return shift(b, d, 0)


def along_z(b, d):
    return shift(b, 0, d)


def join(*blocks):
    total = blocks[0].astype(F32)
    for b in blocks[1:]:
        total = total + b.astype(F32)
    return total


def over_line(block, move):
    own, below, above, far = line_of(block, move)
    return (own + far) + (below + above)


def axes_of(first):
    return (along_z, along_x) if first == 0 else (along_x, along_z)


def gather_near(shard):
    half = shard.shape[0] // 2
    near = []
    for first in (0, 1):
        inner, outer = axes_of(first)
        own = lax.slice_in_dim(shard, first * half, (first + 1) * half, axis=0)
        group = jnp.concatenate(line_of(own, inner), axis=0)
        near.append((group, outer(group, -1), outer(group, 1)))
    return near


def gather_far(near):
    arrays, tables = [], []
    for first in (0, 1):
        _, outer = axes_of(first)
        group, minus, plus = near[first]
        half = group.shape[0] // RING
        far_a = outer(lax.slice_in_dim(minus, 0, 2 * half, axis=0), -1)
        far_b = outer(lax.slice_in_dim(plus, 2 * half, 4 * half, axis=0), 1)
        offs = [0, -1, 1, 2]
        table = {}
        for array, out, part in (
            (group, 0, offs),
            (minus, -1, offs),
            (plus, 1, offs),
            (far_a, 2, offs[:2]),
            (far_b, 2, offs[2:]),
        ):
            arrays.append(array)
            for j, d in enumerate(part):
                rel = (out % RING, d % RING) if first == 0 else (d % RING, out % RING)
                table[rel] = (len(arrays) - 1, j * half)
        tables.append(table)
    order = [(dx, dz) for dx in range(RING) for dz in range(RING)]
    return arrays, [(tables[0][r], tables[1][r]) for r in order]


def in_hbm(x):
    return pltpu.with_memory_space_constraint(x, pltpu.HBM)


def pack_kernel(order_ref, place_ref, x_ref, o_ref, tail):
    def step(g, carry):
        rows = x_ref[order_ref[g]]
        v = rows.astype(F32)
        here = pl.ds(pl.multiple_of(g * 32, 32), 32)
        lane = lax.broadcasted_iota(jnp.int32, (32, 128), 1)
        block = jnp.zeros((32, 128), F32)
        j = 32
        for s in (jnp.sum(v, axis=1, keepdims=True), jnp.sum(v * v, axis=1, keepdims=True)):
            for _ in range(3):
                part = s.astype(BF).astype(F32)
                block = jnp.where(lane == j, part, block)
                s = s - part
                j += 1
        o_ref[here, 0:MAIN] = rows[:, 0:MAIN]
        tail[here, :] = block
        tail[here, 0:32] = v[:, MAIN:MFEAT]
        return carry

    lax.fori_loop(0, N_REQ, step, 0, unroll=True)
    o_ref[:, MAIN:MPAD] = pltpu.roll(tail[...], place_ref[0] * 32, 1).astype(BF)


def pack(merged, tile_order, place):
    return pl.pallas_call(
        pack_kernel,
        out_shape=jax.ShapeDtypeStruct((TILE, MPAD), BF),
        in_specs=[pl.BlockSpec(memory_space=pltpu.SMEM)] * 2 + [vmem()],
        out_specs=vmem(),
        scratch_shapes=[VM((TILE, 128), F32)],
        compiler_params=params(16),
        name="pack",
    )(tile_order, place, merged)


def cut_kernel(row_ref, w_hbm, o_hbm, sem):
    strip = FEAT // N_REQ
    rows = pl.ds(pl.multiple_of(row_ref[0], strip), strip)
    copies = [
        pltpu.make_async_copy(w_hbm.at[rows, pl.ds(k * FEAT, FEAT)], o_hbm.at[k], sem.at[k])
        for k in range(N_HID)
    ]
    for c in copies:
        c.start()
    for c in copies:
        c.wait()


def cut(weight, row):
    return pl.pallas_call(
        cut_kernel,
        out_shape=jax.ShapeDtypeStruct((N_HID, FEAT // N_REQ, FEAT), BF),
        in_specs=[pl.BlockSpec(memory_space=pltpu.SMEM), pl.BlockSpec(memory_space=pl.ANY)],
        out_specs=pl.BlockSpec(memory_space=pl.ANY),
        scratch_shapes=[pltpu.SemaphoreType.DMA((N_HID,))],
        name="cut",
    )(row, in_hbm(weight))


def project_kernel(
    x_hbm, w_hbm, gb_ref, left_ref, pb_ref, o_ref, tail, x, w, wl, acc, sem, x_sem, w_sem
):
    deep = 2 * MAIN
    tails = pltpu.make_async_copy(x_hbm.at[:, pl.ds(MAIN, 128)], tail, sem.at[0])
    lefts = pltpu.make_async_copy(w_hbm.at[:, pl.ds(MAIN, 32), :], wl, sem.at[1])

    def x_copy(k):
        here = pl.ds(pl.multiple_of(k * MAIN, MAIN), MAIN)
        there = x_hbm.at[pl.ds(k * TILE, TILE), pl.ds(0, MAIN)]
        return pltpu.make_async_copy(there, x.at[:, here], x_sem.at[k])

    def pair(part, i):
        return jnp.concatenate([gb_ref[part, pl.ds(2 * i + j, 1), :] for j in (0, 1)], axis=1)

    def w_copy(k):
        here = pl.ds(k * MAIN, MAIN)
        return pltpu.make_async_copy(w_hbm.at[k, pl.ds(0, MAIN), :], w.at[here, :], w_sem.at[k])

    tails.start()
    for k in range(N_HID):
        x_copy(k).start()
        w_copy(k).start()
    lefts.start()
    tails.wait()
    quarter = lax.broadcasted_iota(jnp.int32, (TILE, 128), 1) // 32
    mean = jnp.zeros((TILE, 1), F32)
    square = jnp.zeros((TILE, 1), F32)
    for j in range(RING):
        total = jnp.zeros((TILE, 128), F32)
        for i in range(RING):
            k = RING * i + j
            total = total + tail[k * TILE : (k + 1) * TILE, :].astype(F32)
        at = 32 * ((j + 1) % RING)
        mean = mean + jnp.sum(total[:, at : at + 3], axis=1, keepdims=True)
        square = square + jnp.sum(total[:, at + 3 : at + 6], axis=1, keepdims=True)
    mean = mean * (1.0 / MERGED)
    rstd = lax.rsqrt(square * (1.0 / MERGED) - mean * mean + 1e-05)
    acc[...] = jnp.zeros_like(acc)

    def step(i, carry):
        for j in (0, 1):
            x_copy(2 * i + j).wait()
            w_copy(2 * i + j).wait()
        here = pl.ds(pl.multiple_of(i * deep, deep), deep)
        v = x[:, here].astype(F32)
        normed = (v - mean) * rstd * pair(0, i) + pair(1, i)
        acc[...] += jnp.dot(normed.astype(BF), w[here, :], preferred_element_type=F32)
        return carry

    lax.fori_loop(0, N_HID // 2, step, 0)
    lefts.wait()
    blocks = []
    for i in range(RING):
        v = jnp.zeros((TILE, 128), F32)
        for j in range(RING):
            k = RING * i + j
            v = jnp.where(quarter == j, tail[k * TILE : (k + 1) * TILE, :].astype(F32), v)
        blocks.append(((v - mean) * rstd * left_ref[0, i] + left_ref[1, i]).astype(BF))
    rest = jnp.concatenate(blocks, axis=1)
    y = acc[...] + pb_ref[...] + jnp.dot(
        rest, wl[...].reshape(N_HID * 32, FEAT), preferred_element_type=F32
    )
    y = 0.5 * y * (1.0 + lax.erf(y * math.sqrt(0.5)))
    o_ref[...] = y.astype(BF)


def gain_and_bias(gain, bias):
    both = jnp.stack([gain, bias]).astype(F32).reshape(2, N_HID, MFEAT)
    return both[:, :, :MAIN], both[:, :, MAIN:].reshape(2, RING, 1, 128)


def project(gathered, weight, both, left, out_bias):
    return pl.pallas_call(
        project_kernel,
        out_shape=jax.ShapeDtypeStruct((TILE, FEAT), BF),
        in_specs=[pl.BlockSpec(memory_space=pl.ANY)] * 2 + [vmem()] * 3,
        out_specs=vmem(),
        scratch_shapes=[
            VM((N_HID * TILE, 128), BF),
            VM((TILE, N_HID * MAIN), BF),
            VM((N_HID * MAIN, FEAT), BF),
            VM((N_HID, 32, FEAT), BF),
            VM((TILE, FEAT), F32),
            pltpu.SemaphoreType.DMA((2,)),
            pltpu.SemaphoreType.DMA((N_HID,)),
            pltpu.SemaphoreType.DMA((N_HID,)),
        ],
        compiler_params=params(30),
        cost_estimate=pl.CostEstimate(
            flops=2 * TILE * MERGED * FEAT, bytes_accessed=17 << 20, transcendentals=0
        ),
        name="project",
    )(
        in_hbm(gathered),
        in_hbm(weight.reshape(N_HID, MFEAT, FEAT)),
        both,
        left,
        out_bias,
    )


def turn(v, cos, sin):
    return v * cos + pltpu.roll(v, HEAD_DIM // 2, 1) * sin


def qkv(arrays, where, weight, cos, sin, sources, name):
    half = arrays[0].shape[0] // RING
    rows = 2 * half
    n = len(arrays)
    deep = 4 * FEAT
    cols = FEAT + HEAD_DIM

    def kernel(src_ref, *refs):
        ins = refs[:n]
        w_hbm, cos_ref, sin_ref, q_ref, kv_ref, xs, w, acc, sem = refs[n:]

        def copy(k):
            there = pl.ds(pl.multiple_of(src_ref[k] * FEAT, FEAT), FEAT)
            here = pl.ds(k * FEAT, FEAT)
            return pltpu.make_async_copy(w_hbm.at[there, :], w.at[here, :], sem.at[k])

        for k in range(N_HID):
            copy(k).start()
        square = jnp.zeros((rows, HEAD_DIM), F32)
        for k in range(N_HID):
            block = jnp.concatenate([ins[a][row : row + half, :] for a, row in where[k]], axis=0)
            xs[:, k * FEAT : (k + 1) * FEAT] = block
            v = block.astype(F32)
            v = v * v
            square = square + (v[:, 0:128] + v[:, 128:256] + v[:, 256:384])
        acc[...] = jnp.zeros_like(acc)

        def step(i, carry):
            for j in range(4):
                copy(4 * i + j).wait()
            here = pl.ds(pl.multiple_of(i * deep, deep), deep)
            acc[...] += jnp.dot(xs[:, here], w[here, :], preferred_element_type=F32)
            return carry

        lax.fori_loop(0, RING, step, 0)
        scale = lax.rsqrt(jnp.sum(square, axis=1, keepdims=True) * (1.0 / D) + 1e-05)
        for h in range(FEAT // HEAD_DIM):
            part = acc[:, h * HEAD_DIM : (h + 1) * HEAD_DIM] * scale
            q_ref[:, h * HEAD_DIM : (h + 1) * HEAD_DIM] = turn(
                part, cos_ref[...], sin_ref[...]
            ).astype(BF)
        kv_ref[...] = (acc[:, FEAT:] * scale).astype(BF)

    return pl.pallas_call(
        kernel,
        out_shape=(
            jax.ShapeDtypeStruct((rows, FEAT), BF),
            jax.ShapeDtypeStruct((rows, HEAD_DIM), BF),
        ),
        in_specs=[pl.BlockSpec(memory_space=pltpu.SMEM)]
        + [vmem() for _ in arrays]
        + [pl.BlockSpec(memory_space=pl.ANY), vmem(), vmem()],
        out_specs=(vmem(), vmem()),
        scratch_shapes=[
            VM((rows, D), BF),
            VM((D, cols), BF),
            VM((rows, cols), F32),
            pltpu.SemaphoreType.DMA((N_HID,)),
        ],
        compiler_params=params(20),
        cost_estimate=pl.CostEstimate(
            flops=2 * rows * D * cols, bytes_accessed=12 << 20, transcendentals=0
        ),
        name=name,
    )(sources, *arrays, in_hbm(weight), cos, sin)


def attend_kernel(
    low_ref, qt, qi, ot, pt, oi, pi, cos_ref, sin_ref, row_ref, col_ref, o_ref, qs, keys, vals
):
    upper = low_ref[0] == 0
    lane = lax.broadcasted_iota(jnp.int32, (LIVE, HEAD_DIM), 1)
    own = jnp.concatenate([ot[...], oi[...]], axis=0).astype(F32)
    other = jnp.concatenate([pt[...], pi[...]], axis=0).astype(F32)
    low = jnp.where(upper, other, own)
    high = jnp.where(upper, own, other)
    key = jnp.where(lane < 64, low, pltpu.roll(high, 64, 1))
    val = jnp.where(lane < 64, pltpu.roll(low, 64, 1), high)
    keys[...] = turn(key, cos_ref[...], sin_ref[...]).astype(BF)
    vals[...] = val.astype(BF)
    qs[:TEXT] = qt[...]
    qs[TEXT:] = qi[...]
    code = col_ref[...]

    def block(i, carry):
        rows = pl.ds(pl.multiple_of(i * 128, 128), 128)
        mine = row_ref[rows, :]
        start = jnp.where(mine >= 1024, 1024, 0)
        live = jnp.logical_and(code <= mine, code >= start)
        for h in range(FEAT // HEAD_DIM):
            cols = slice(h * HEAD_DIM, (h + 1) * HEAD_DIM)
            s = lax.dot_general(
                qs[rows, cols], keys[...], (((1,), (1,)), ((), ())), preferred_element_type=F32
            ) * (1.0 / math.sqrt(HEAD_DIM))
            s = jnp.where(live, s, -jnp.inf)
            w = jnp.exp(s - jnp.max(s, axis=1, keepdims=True))
            total = jnp.sum(w, axis=1, keepdims=True)
            mixed = jnp.dot(w.astype(BF), vals[...], preferred_element_type=F32)
            o_ref[rows, cols] = (mixed / total).astype(BF)
        return carry

    lax.fori_loop(0, LIVE // 128, block, 0)


def attend(low, qt, qi, ot, pt, oi, pi, cos, sin, code):
    return pl.pallas_call(
        attend_kernel,
        out_shape=jax.ShapeDtypeStruct((LIVE, FEAT), BF),
        in_specs=[pl.BlockSpec(memory_space=pltpu.SMEM)] + [vmem()] * 10,
        out_specs=vmem(),
        scratch_shapes=[VM((LIVE, FEAT), BF), VM((LIVE, HEAD_DIM), BF), VM((LIVE, HEAD_DIM), BF)],
        compiler_params=params(24),
        cost_estimate=pl.CostEstimate(flops=1 << 30, bytes_accessed=2 << 20, transcendentals=0),
        name="attend",
    )(low, qt, qi, ot, pt, oi, pi, cos, sin, code[:, None], code[None, :])


def finish_kernel(
    text_ref, tile_ref, a_hbm, w_hbm, slot_ref, o_ref, a, w, acc, sums, a_sem, w_sem
):
    two = 2 * FEAT

    def a_copy(k):
        here = pl.ds(pl.multiple_of(k * FEAT, FEAT), FEAT)
        return pltpu.make_async_copy(a_hbm.at[pl.ds(pl.multiple_of(k * LIVE, LIVE), LIVE), :], a.at[:, here], a_sem.at[k])

    def w_copy(k, r):
        return pltpu.make_async_copy(w_hbm.at[r, k], w.at[k, r], w_sem.at[k, r])

    def begin(k, carry):
        a_copy(k).start()
        for r in range(N_REQ):
            w_copy(k, r).start()
        return carry

    lax.fori_loop(0, N_HID, begin, 0)
    acc[...] = jnp.zeros_like(acc)

    def step(i, carry):
        for j in (0, 1):
            a_copy(2 * i + j).wait()
            for r in range(N_REQ):
                w_copy(2 * i + j, r).wait()
        here = pl.ds(pl.multiple_of(i * two, two), two)
        block = w[pl.ds(2 * i, 2)].reshape(two, FEAT)
        acc[...] += jnp.dot(a[:, here], block, preferred_element_type=F32)
        return carry

    lax.fori_loop(0, N_HID // 2, step, 0)
    sums[...] = acc[...].astype(BF)

    def one(r, carry):
        row = slot_ref[r]
        pick = (lax.broadcasted_iota(jnp.int32, (LEN_MAX, LIVE), 1) == row).astype(BF)
        moved = jnp.dot(pick, sums[...], preferred_element_type=F32)
        image = jnp.dot(pick[:, TEXT:], tile_ref[...], preferred_element_type=F32)
        base = jnp.where(row >= TEXT, image, text_ref[r].astype(F32))
        o_ref[r] = (base + moved).astype(BF)
        return carry

    lax.fori_loop(0, REQ_GRP, one, 0)


def finish(text, tile, heads, weight, slots):
    return pl.pallas_call(
        finish_kernel,
        out_shape=jax.ShapeDtypeStruct((REQ_GRP, LEN_MAX, FEAT), BF),
        in_specs=[vmem()] * 2 + [pl.BlockSpec(memory_space=pl.ANY)] * 2 + [vmem()],
        out_specs=vmem(),
        scratch_shapes=[
            VM((LIVE, D), BF),
            VM((N_HID, N_REQ, FEAT // N_REQ, FEAT), BF),
            VM((LIVE, FEAT), F32),
            VM((LIVE, FEAT), BF),
            pltpu.SemaphoreType.DMA((N_HID,)),
            pltpu.SemaphoreType.DMA((N_HID, N_REQ)),
        ],
        compiler_params=params(32),
        cost_estimate=pl.CostEstimate(
            flops=2 * LIVE * FEAT * D, bytes_accessed=14 << 20, transcendentals=0
        ),
        name="finish",
    )(text, tile, in_hbm(heads), in_hbm(weight), slots)


def shards(
    merged,
    ln_gain,
    ln_bias,
    proj_weight,
    proj_bias,
    text_embed,
    attn_gain,
    query_weight,
    key_weight,
    value_weight,
    out_weight,
    final_gain,
    head_weight,
    lengths,
    tile_request,
    insert_pos,
):
    hid = lax.axis_index("hid")
    me = lax.axis_index("req")
    owners = tile_request // REQ_GRP
    tiles = jnp.arange(N_REQ, dtype=jnp.int32)
    tile_order = jnp.sum(
        jnp.where(owners[None, :] == tiles[:, None], tiles[None, :], 0), axis=1
    ).astype(jnp.int32)
    mine = owners == me
    local_req = jnp.sum(jnp.where(mine, tile_request % REQ_GRP, 0))
    start = jnp.sum(jnp.where(mine, insert_pos, 0))
    len_a = lengths[0]
    first = local_req * len_a + start

    n = jnp.arange(LIVE, dtype=jnp.int32)
    packed = jnp.where(n < TEXT, jnp.where(n < first, n, n + TILE), n - TEXT + first)
    second = packed >= len_a
    pos = packed - jnp.where(second, len_a, 0)
    code = pos + jnp.where(second, 1024, 0)
    flat = pos + jnp.where(second, LEN_MAX, 0)
    slot = jnp.arange(LEN_MAX, dtype=jnp.int32)
    at = jnp.stack([slot, slot + len_a])
    in_tile = jnp.logical_and(at >= first, at < first + TILE)
    row_of = jnp.where(in_tile, at - first + TEXT, jnp.where(at < first, at, at - TILE))
    row_of = jnp.where(slot[None, :] < lengths[:, None], row_of, -1)

    half_dim = HEAD_DIM // 2
    inv_freq = jnp.exp(
        jnp.arange(half_dim, dtype=F32) * (-2.0 * math.log(1000000.0) / HEAD_DIM)
    )
    angles = pos.astype(F32)[:, None] * inv_freq[None, :]
    cosine, sine = jnp.cos(angles), jnp.sin(angles)
    cos = jnp.concatenate([cosine, cosine], axis=1)
    sin = jnp.concatenate([-sine, sine], axis=1)

    x, z = hid // RING, hid % RING
    rel = jnp.arange(N_HID, dtype=jnp.int32)
    sources = ((x + rel // RING) % RING) * RING + (z + rel % RING) % RING

    gathered = lax.all_gather(pack(merged, tile_order, (hid % RING)[None]), "hid", axis=0, tiled=True)

    pick = (flat[:TEXT, None] == jnp.arange(REQ_GRP * LEN_MAX)[None, :]).astype(BF)
    text_rows = jnp.dot(
        pick, text_embed.reshape(REQ_GRP * LEN_MAX, FEAT), preferred_element_type=F32
    ).astype(BF)
    weight = (
        jnp.concatenate([query_weight, key_weight, value_weight], axis=1).astype(F32)
        * attn_gain.astype(F32)[:, None]
    ).astype(BF)
    partner = [(i, i ^ 1) for i in range(N_HID)]
    text_blocks, text_where = gather_far(gather_near(text_rows))
    strip = FEAT // N_REQ
    piece = cut(out_weight, (me * strip)[None].astype(jnp.int32))
    both, left = gain_and_bias(ln_gain, ln_bias)
    both, left, *text_blocks[8:] = lax.optimization_barrier((both, left, *text_blocks[8:]))
    q_text, kv_text = qkv(
        text_blocks, text_where, weight, cos[:TEXT], sin[:TEXT], sources, "qkv_text"
    )
    piece, q_text = lax.optimization_barrier((piece, q_text))
    gathered, q_text, kv_text = lax.optimization_barrier((gathered, q_text, kv_text))
    piece = lax.all_to_all(piece, "hid", split_axis=0, concat_axis=0, tiled=True)
    projected = project(
        gathered,
        proj_weight,
        both,
        left,
        proj_bias[None, :],
    )
    projected, piece = lax.optimization_barrier((projected, piece))
    tile = lax.all_to_all(
        projected.reshape(N_REQ, TILE // N_REQ, FEAT), "req", split_axis=0, concat_axis=0, tiled=True
    ).reshape(TILE, FEAT)
    other_text = lax.ppermute(kv_text, "hid", partner)
    piece, tile = lax.optimization_barrier((piece, tile))
    tile_blocks, tile_where = gather_far(gather_near(tile))
    columns = lax.all_gather(piece, "req", axis=0, tiled=False)
    q_tile, kv_tile = qkv(
        tile_blocks, tile_where, weight, cos[TEXT:], sin[TEXT:], sources, "qkv_tile"
    )
    other_tile = lax.ppermute(kv_tile, "hid", partner)

    low = (hid % 2 == 0).astype(jnp.int32)[None]
    attended = attend(
        low, q_text, q_tile, kv_text, other_text, kv_tile, other_tile, cos, sin, code
    )
    heads = lax.all_gather(attended, "hid", axis=0, tiled=True)
    hidden = finish(text_embed, tile, heads, columns, row_of[:, :, None])

    last = jnp.sum(jnp.where(slot[None, :] == lengths[:, None] - 1, row_of, 0), axis=1)
    pick_last = (last[:, None] == n[None, :]).astype(BF)
    rows_last = jnp.dot(pick_last, attended, preferred_element_type=F32).astype(BF)
    term = jnp.dot(rows_last, out_weight, preferred_element_type=F32)
    base = jnp.dot(pick_last[:, :TEXT], text_rows, preferred_element_type=F32) + jnp.dot(
        pick_last[:, TEXT:], tile, preferred_element_type=F32
    )
    spot = lax.broadcasted_iota(jnp.int32, (1, N_HID, 1), 1) == hid
    term = term + jnp.where(spot, base[:, None, :], 0.0).reshape(REQ_GRP, D)
    term = over_line(term, along_z)
    full_width = over_line(term, along_x).astype(BF)
    all_last = lax.all_gather(full_width, "req", axis=0, tiled=True)
    last_values = all_last.astype(F32)
    last_squares = jnp.sum(last_values * last_values, axis=1)
    final_norm = jnp.sqrt(last_squares)
    final_scaled = (
        last_values * lax.rsqrt(last_squares / D + 1e-05)[:, None] * final_gain.astype(F32)
    ).astype(BF)
    logits = lax.dot_general(
        final_scaled, head_weight, (((1,), (1,)), ((), ())), preferred_element_type=F32
    )
    top = jnp.max(logits, axis=1)
    for move in (along_z, along_x):
        here, below, above, far_top = line_of(top, move)
        top = jnp.maximum(jnp.maximum(here, below), jnp.maximum(above, far_top))
    logit_max = lax.pmax(top, "req")
    return (hidden, final_norm, logit_max)


def solution(mesh):
    return jax.shard_map(
        shards,
        mesh=mesh,
        in_specs=(
            P(None, "req", "hid"),
            P(),
            P(),
            P(None, "hid"),
            P("hid"),
            P("req", None, "hid"),
            P(),
            P(None, "hid"),
            P(None, "hid"),
            P(None, "hid"),
            P("hid", None),
            P(),
            P(("req", "hid"), None),
            P("req"),
            P(),
            P(),
        ),
        out_specs=(P("req", None, "hid"), P(), P()),
        check_vma=False,
    )
```

```python
import math

import jax
import jax.numpy as jnp
from jax import lax
from jax.experimental import pallas as pl
from jax.experimental.pallas import tpu as pltpu
from jax.sharding import PartitionSpec as P

HEAD_DIM = 128
D = 6144
MERGED = 12800
REQ_GRP = 2
LEN_MAX = 480
LIVE = 640
TILE = 256
TEXT = LIVE - TILE
N_HID = 16
N_REQ = 8
RING = 4
FEAT = D // N_HID
MFEAT = MERGED // N_HID
MAIN = 768
MPAD = 896
BF = jnp.bfloat16
F32 = jnp.float32
VM = pltpu.VMEM


def vmem():
    return pl.BlockSpec(memory_space=pltpu.VMEM)


def params(mib):
    return pltpu.CompilerParams(vmem_limit_bytes=mib << 20)


def shift(block, dx, dz):
    route = []
    for i in range(N_HID):
        x, z = divmod(i, RING)
        route.append((((x + dx) % RING) * RING + (z + dz) % RING, i))
    return lax.ppermute(block, "hid", route)


def line_of(block, move):
    return [block, move(block, -1), move(block, 1), move(block, 2)]


def along_x(b, d):
    return shift(b, d, 0)


def along_z(b, d):
    return shift(b, 0, d)


def join(*blocks):
    total = blocks[0].astype(F32)
    for b in blocks[1:]:
        total = total + b.astype(F32)
    return total


def over_line(block, move):
    own, below, above, far = line_of(block, move)
    return (own + far) + (below + above)


def axes_of(first):
    return (along_z, along_x) if first == 0 else (along_x, along_z)


def gather_near(shard):
    half = shard.shape[0] // 2
    near = []
    for first in (0, 1):
        inner, outer = axes_of(first)
        own = lax.slice_in_dim(shard, first * half, (first + 1) * half, axis=0)
        group = jnp.concatenate(line_of(own, inner), axis=0)
        near.append((group, outer(group, -1), outer(group, 1)))
    return near


def gather_far(near):
    arrays, tables = [], []
    for first in (0, 1):
        _, outer = axes_of(first)
        group, minus, plus = near[first]
        half = group.shape[0] // RING
        far_a = outer(lax.slice_in_dim(minus, 0, 2 * half, axis=0), -1)
        far_b = outer(lax.slice_in_dim(plus, 2 * half, 4 * half, axis=0), 1)
        offs = [0, -1, 1, 2]
        table = {}
        for array, out, part in (
            (group, 0, offs),
            (minus, -1, offs),
            (plus, 1, offs),
            (far_a, 2, offs[:2]),
            (far_b, 2, offs[2:]),
        ):
            arrays.append(array)
            for j, d in enumerate(part):
                rel = (out % RING, d % RING) if first == 0 else (d % RING, out % RING)
                table[rel] = (len(arrays) - 1, j * half)
        tables.append(table)
    order = [(dx, dz) for dx in range(RING) for dz in range(RING)]
    return arrays, [(tables[0][r], tables[1][r]) for r in order]


def in_hbm(x):
    return pltpu.with_memory_space_constraint(x, pltpu.HBM)


def pack_kernel(order_ref, place_ref, x_ref, o_ref, tail):
    def step(g, carry):
        rows = x_ref[order_ref[g]]
        v = rows.astype(F32)
        here = pl.ds(pl.multiple_of(g * 32, 32), 32)
        lane = lax.broadcasted_iota(jnp.int32, (32, 128), 1)
        block = jnp.zeros((32, 128), F32)
        j = 32
        for s in (jnp.sum(v, axis=1, keepdims=True), jnp.sum(v * v, axis=1, keepdims=True)):
            for _ in range(3):
                part = s.astype(BF).astype(F32)
                block = jnp.where(lane == j, part, block)
                s = s - part
                j += 1
        o_ref[here, 0:MAIN] = rows[:, 0:MAIN]
        tail[here, :] = block
        tail[here, 0:32] = v[:, MAIN:MFEAT]
        return carry

    lax.fori_loop(0, N_REQ, step, 0, unroll=True)
    o_ref[:, MAIN:MPAD] = pltpu.roll(tail[...], place_ref[0] * 32, 1).astype(BF)


def pack(merged, tile_order, place):
    return pl.pallas_call(
        pack_kernel,
        out_shape=jax.ShapeDtypeStruct((TILE, MPAD), BF),
        in_specs=[pl.BlockSpec(memory_space=pltpu.SMEM)] * 2 + [vmem()],
        out_specs=vmem(),
        scratch_shapes=[VM((TILE, 128), F32)],
        compiler_params=params(16),
        name="pack",
    )(tile_order, place, merged)


def cut_kernel(row_ref, w_hbm, o_ref, sem):
    strip = FEAT // N_REQ
    rows = pl.ds(pl.multiple_of(row_ref[0], strip), strip)
    copies = [
        pltpu.make_async_copy(w_hbm.at[rows, pl.ds(k * FEAT, FEAT)], o_ref.at[k], sem.at[k])
        for k in range(N_HID)
    ]
    for c in copies:
        c.start()
    for c in copies:
        c.wait()


def cut(weight, row):
    return pl.pallas_call(
        cut_kernel,
        out_shape=jax.ShapeDtypeStruct((N_HID, FEAT // N_REQ, FEAT), BF),
        in_specs=[pl.BlockSpec(memory_space=pltpu.SMEM), pl.BlockSpec(memory_space=pl.ANY)],
        out_specs=vmem(),
        scratch_shapes=[pltpu.SemaphoreType.DMA((N_HID,))],
        name="cut",
    )(row, in_hbm(weight))


def project_kernel(
    x_hbm, w_hbm, gb_ref, left_ref, pb_ref, o_ref, tail, x, w, wl, acc, sem, x_sem, w_sem
):
    deep = 2 * MAIN
    tails = pltpu.make_async_copy(x_hbm.at[:, pl.ds(MAIN, 128)], tail, sem.at[0])
    lefts = pltpu.make_async_copy(w_hbm.at[:, pl.ds(MAIN, 32), :], wl, sem.at[1])

    def x_copy(k):
        here = pl.ds(pl.multiple_of(k * MAIN, MAIN), MAIN)
        there = x_hbm.at[pl.ds(k * TILE, TILE), pl.ds(0, MAIN)]
        return pltpu.make_async_copy(there, x.at[:, here], x_sem.at[k])

    def pair(part, i):
        return jnp.concatenate([gb_ref[part, pl.ds(2 * i + j, 1), :] for j in (0, 1)], axis=1)

    def w_copy(k):
        here = pl.ds(k * MAIN, MAIN)
        return pltpu.make_async_copy(w_hbm.at[k, pl.ds(0, MAIN), :], w.at[here, :], w_sem.at[k])

    tails.start()
    for k in range(N_HID):
        x_copy(k).start()
        w_copy(k).start()
    lefts.start()
    tails.wait()
    quarter = lax.broadcasted_iota(jnp.int32, (TILE, 128), 1) // 32
    mean = jnp.zeros((TILE, 1), F32)
    square = jnp.zeros((TILE, 1), F32)
    for j in range(RING):
        total = jnp.zeros((TILE, 128), F32)
        for i in range(RING):
            k = RING * i + j
            total = total + tail[k * TILE : (k + 1) * TILE, :].astype(F32)
        at = 32 * ((j + 1) % RING)
        mean = mean + jnp.sum(total[:, at : at + 3], axis=1, keepdims=True)
        square = square + jnp.sum(total[:, at + 3 : at + 6], axis=1, keepdims=True)
    mean = mean * (1.0 / MERGED)
    rstd = lax.rsqrt(square * (1.0 / MERGED) - mean * mean + 1e-05)
    acc[...] = jnp.zeros_like(acc)

    def step(i, carry):
        for j in (0, 1):
            x_copy(2 * i + j).wait()
            w_copy(2 * i + j).wait()
        here = pl.ds(pl.multiple_of(i * deep, deep), deep)
        v = x[:, here].astype(F32)
        normed = (v - mean) * rstd * pair(0, i) + pair(1, i)
        acc[...] += jnp.dot(normed.astype(BF), w[here, :], preferred_element_type=F32)
        return carry

    lax.fori_loop(0, N_HID // 2, step, 0)
    lefts.wait()
    blocks = []
    for i in range(RING):
        v = jnp.zeros((TILE, 128), F32)
        for j in range(RING):
            k = RING * i + j
            v = jnp.where(quarter == j, tail[k * TILE : (k + 1) * TILE, :].astype(F32), v)
        blocks.append(((v - mean) * rstd * left_ref[0, i] + left_ref[1, i]).astype(BF))
    rest = jnp.concatenate(blocks, axis=1)
    y = acc[...] + pb_ref[...] + jnp.dot(
        rest, wl[...].reshape(N_HID * 32, FEAT), preferred_element_type=F32
    )
    y = 0.5 * y * (1.0 + lax.erf(y * math.sqrt(0.5)))
    o_ref[...] = y.astype(BF)


def gain_and_bias(gain, bias):
    both = jnp.stack([gain, bias]).astype(F32).reshape(2, N_HID, MFEAT)
    return both[:, :, :MAIN], both[:, :, MAIN:].reshape(2, RING, 1, 128)


def project(gathered, weight, both, left, out_bias):
    return pl.pallas_call(
        project_kernel,
        out_shape=jax.ShapeDtypeStruct((TILE, FEAT), BF),
        in_specs=[pl.BlockSpec(memory_space=pl.ANY)] * 2 + [vmem()] * 3,
        out_specs=vmem(),
        scratch_shapes=[
            VM((N_HID * TILE, 128), BF),
            VM((TILE, N_HID * MAIN), BF),
            VM((N_HID * MAIN, FEAT), BF),
            VM((N_HID, 32, FEAT), BF),
            VM((TILE, FEAT), F32),
            pltpu.SemaphoreType.DMA((2,)),
            pltpu.SemaphoreType.DMA((N_HID,)),
            pltpu.SemaphoreType.DMA((N_HID,)),
        ],
        compiler_params=params(30),
        cost_estimate=pl.CostEstimate(
            flops=2 * TILE * MERGED * FEAT, bytes_accessed=17 << 20, transcendentals=0
        ),
        name="project",
    )(
        in_hbm(gathered),
        in_hbm(weight.reshape(N_HID, MFEAT, FEAT)),
        both,
        left,
        out_bias,
    )


def turn(v, cos, sin):
    return v * cos + pltpu.roll(v, HEAD_DIM // 2, 1) * sin


def qkv(arrays, where, weight, cos, sin, sources, name):
    half = arrays[0].shape[0] // RING
    rows = 2 * half
    n = len(arrays)
    deep = 4 * FEAT
    cols = FEAT + HEAD_DIM

    def kernel(src_ref, *refs):
        ins = refs[:n]
        w_hbm, cos_ref, sin_ref, q_ref, kv_ref, xs, w, acc, sem = refs[n:]

        def copy(k):
            there = pl.ds(pl.multiple_of(src_ref[k] * FEAT, FEAT), FEAT)
            here = pl.ds(k * FEAT, FEAT)
            return pltpu.make_async_copy(w_hbm.at[there, :], w.at[here, :], sem.at[k])

        for k in range(N_HID):
            copy(k).start()
        square = jnp.zeros((rows, HEAD_DIM), F32)
        for k in range(N_HID):
            block = jnp.concatenate([ins[a][row : row + half, :] for a, row in where[k]], axis=0)
            xs[:, k * FEAT : (k + 1) * FEAT] = block
            v = block.astype(F32)
            v = v * v
            square = square + (v[:, 0:128] + v[:, 128:256] + v[:, 256:384])
        acc[...] = jnp.zeros_like(acc)

        def step(i, carry):
            for j in range(4):
                copy(4 * i + j).wait()
            here = pl.ds(pl.multiple_of(i * deep, deep), deep)
            acc[...] += jnp.dot(xs[:, here], w[here, :], preferred_element_type=F32)
            return carry

        lax.fori_loop(0, RING, step, 0)
        scale = lax.rsqrt(jnp.sum(square, axis=1, keepdims=True) * (1.0 / D) + 1e-05)
        for h in range(FEAT // HEAD_DIM):
            part = acc[:, h * HEAD_DIM : (h + 1) * HEAD_DIM] * scale
            q_ref[:, h * HEAD_DIM : (h + 1) * HEAD_DIM] = turn(
                part, cos_ref[...], sin_ref[...]
            ).astype(BF)
        kv_ref[...] = (acc[:, FEAT:] * scale).astype(BF)

    return pl.pallas_call(
        kernel,
        out_shape=(
            jax.ShapeDtypeStruct((rows, FEAT), BF),
            jax.ShapeDtypeStruct((rows, HEAD_DIM), BF),
        ),
        in_specs=[pl.BlockSpec(memory_space=pltpu.SMEM)]
        + [vmem() for _ in arrays]
        + [pl.BlockSpec(memory_space=pl.ANY), vmem(), vmem()],
        out_specs=(vmem(), vmem()),
        scratch_shapes=[
            VM((rows, D), BF),
            VM((D, cols), BF),
            VM((rows, cols), F32),
            pltpu.SemaphoreType.DMA((N_HID,)),
        ],
        compiler_params=params(20),
        cost_estimate=pl.CostEstimate(
            flops=2 * rows * D * cols, bytes_accessed=12 << 20, transcendentals=0
        ),
        name=name,
    )(sources, *arrays, in_hbm(weight), cos, sin)


def attend_kernel(
    low_ref, qt, qi, ot, pt, oi, pi, cos_ref, sin_ref, row_ref, col_ref, o_ref, qs, keys, vals
):
    upper = low_ref[0] == 0
    lane = lax.broadcasted_iota(jnp.int32, (LIVE, HEAD_DIM), 1)
    own = jnp.concatenate([ot[...], oi[...]], axis=0).astype(F32)
    other = jnp.concatenate([pt[...], pi[...]], axis=0).astype(F32)
    low = jnp.where(upper, other, own)
    high = jnp.where(upper, own, other)
    key = jnp.where(lane < 64, low, pltpu.roll(high, 64, 1))
    val = jnp.where(lane < 64, pltpu.roll(low, 64, 1), high)
    keys[...] = turn(key, cos_ref[...], sin_ref[...]).astype(BF)
    vals[...] = val.astype(BF)
    qs[:TEXT] = qt[...]
    qs[TEXT:] = qi[...]
    code = col_ref[...]

    def block(i, carry):
        rows = pl.ds(pl.multiple_of(i * 128, 128), 128)
        mine = row_ref[rows, :]
        start = jnp.where(mine >= 1024, 1024, 0)
        live = jnp.logical_and(code <= mine, code >= start)
        for h in range(FEAT // HEAD_DIM):
            cols = slice(h * HEAD_DIM, (h + 1) * HEAD_DIM)
            s = lax.dot_general(
                qs[rows, cols], keys[...], (((1,), (1,)), ((), ())), preferred_element_type=F32
            ) * (1.0 / math.sqrt(HEAD_DIM))
            s = jnp.where(live, s, -jnp.inf)
            w = jnp.exp(s - jnp.max(s, axis=1, keepdims=True))
            total = jnp.sum(w, axis=1, keepdims=True)
            mixed = jnp.dot(w.astype(BF), vals[...], preferred_element_type=F32)
            o_ref[rows, cols] = (mixed / total).astype(BF)
        return carry

    lax.fori_loop(0, LIVE // 128, block, 0)


def attend(low, qt, qi, ot, pt, oi, pi, cos, sin, code):
    return pl.pallas_call(
        attend_kernel,
        out_shape=jax.ShapeDtypeStruct((LIVE, FEAT), BF),
        in_specs=[pl.BlockSpec(memory_space=pltpu.SMEM)] + [vmem()] * 10,
        out_specs=vmem(),
        scratch_shapes=[VM((LIVE, FEAT), BF), VM((LIVE, HEAD_DIM), BF), VM((LIVE, HEAD_DIM), BF)],
        compiler_params=params(24),
        cost_estimate=pl.CostEstimate(flops=1 << 30, bytes_accessed=2 << 20, transcendentals=0),
        name="attend",
    )(low, qt, qi, ot, pt, oi, pi, cos, sin, code[:, None], code[None, :])


def finish_kernel(
    text_ref, tile_ref, a_hbm, w_hbm, slot_ref, o_ref, a, w, acc, sums, a_sem, w_sem
):
    two = 2 * FEAT

    def a_copy(k):
        here = pl.ds(pl.multiple_of(k * FEAT, FEAT), FEAT)
        return pltpu.make_async_copy(a_hbm.at[pl.ds(pl.multiple_of(k * LIVE, LIVE), LIVE), :], a.at[:, here], a_sem.at[k])

    def w_copy(k, r):
        return pltpu.make_async_copy(w_hbm.at[r, k], w.at[k, r], w_sem.at[k, r])

    def begin(k, carry):
        a_copy(k).start()
        for r in range(N_REQ):
            w_copy(k, r).start()
        return carry

    lax.fori_loop(0, N_HID, begin, 0)
    acc[...] = jnp.zeros_like(acc)

    def step(i, carry):
        for j in (0, 1):
            a_copy(2 * i + j).wait()
            for r in range(N_REQ):
                w_copy(2 * i + j, r).wait()
        here = pl.ds(pl.multiple_of(i * two, two), two)
        block = w[pl.ds(2 * i, 2)].reshape(two, FEAT)
        acc[...] += jnp.dot(a[:, here], block, preferred_element_type=F32)
        return carry

    lax.fori_loop(0, N_HID // 2, step, 0)
    sums[...] = acc[...].astype(BF)

    def one(r, carry):
        row = slot_ref[r]
        pick = (lax.broadcasted_iota(jnp.int32, (LEN_MAX, LIVE), 1) == row).astype(BF)
        moved = jnp.dot(pick, sums[...], preferred_element_type=F32)
        image = jnp.dot(pick[:, TEXT:], tile_ref[...], preferred_element_type=F32)
        base = jnp.where(row >= TEXT, image, text_ref[r].astype(F32))
        o_ref[r] = (base + moved).astype(BF)
        return carry

    lax.fori_loop(0, REQ_GRP, one, 0)


def finish(text, tile, heads, weight, slots):
    return pl.pallas_call(
        finish_kernel,
        out_shape=jax.ShapeDtypeStruct((REQ_GRP, LEN_MAX, FEAT), BF),
        in_specs=[vmem()] * 2 + [pl.BlockSpec(memory_space=pl.ANY)] * 2 + [vmem()],
        out_specs=vmem(),
        scratch_shapes=[
            VM((LIVE, D), BF),
            VM((N_HID, N_REQ, FEAT // N_REQ, FEAT), BF),
            VM((LIVE, FEAT), F32),
            VM((LIVE, FEAT), BF),
            pltpu.SemaphoreType.DMA((N_HID,)),
            pltpu.SemaphoreType.DMA((N_HID, N_REQ)),
        ],
        compiler_params=params(32),
        cost_estimate=pl.CostEstimate(
            flops=2 * LIVE * FEAT * D, bytes_accessed=14 << 20, transcendentals=0
        ),
        name="finish",
    )(text, tile, in_hbm(heads), in_hbm(weight), slots)


def shards(
    merged,
    ln_gain,
    ln_bias,
    proj_weight,
    proj_bias,
    text_embed,
    attn_gain,
    query_weight,
    key_weight,
    value_weight,
    out_weight,
    final_gain,
    head_weight,
    lengths,
    tile_request,
    insert_pos,
):
    hid = lax.axis_index("hid")
    me = lax.axis_index("req")
    owners = tile_request // REQ_GRP
    tiles = jnp.arange(N_REQ, dtype=jnp.int32)
    tile_order = jnp.sum(
        jnp.where(owners[None, :] == tiles[:, None], tiles[None, :], 0), axis=1
    ).astype(jnp.int32)
    mine = owners == me
    local_req = jnp.sum(jnp.where(mine, tile_request % REQ_GRP, 0))
    start = jnp.sum(jnp.where(mine, insert_pos, 0))
    len_a = lengths[0]
    first = local_req * len_a + start

    n = jnp.arange(LIVE, dtype=jnp.int32)
    packed = jnp.where(n < TEXT, jnp.where(n < first, n, n + TILE), n - TEXT + first)
    second = packed >= len_a
    pos = packed - jnp.where(second, len_a, 0)
    code = pos + jnp.where(second, 1024, 0)
    flat = pos + jnp.where(second, LEN_MAX, 0)
    slot = jnp.arange(LEN_MAX, dtype=jnp.int32)
    at = jnp.stack([slot, slot + len_a])
    in_tile = jnp.logical_and(at >= first, at < first + TILE)
    row_of = jnp.where(in_tile, at - first + TEXT, jnp.where(at < first, at, at - TILE))
    row_of = jnp.where(slot[None, :] < lengths[:, None], row_of, -1)

    half_dim = HEAD_DIM // 2
    inv_freq = jnp.exp(
        jnp.arange(half_dim, dtype=F32) * (-2.0 * math.log(1000000.0) / HEAD_DIM)
    )
    angles = pos.astype(F32)[:, None] * inv_freq[None, :]
    cosine, sine = jnp.cos(angles), jnp.sin(angles)
    cos = jnp.concatenate([cosine, cosine], axis=1)
    sin = jnp.concatenate([-sine, sine], axis=1)

    x, z = hid // RING, hid % RING
    rel = jnp.arange(N_HID, dtype=jnp.int32)
    sources = ((x + rel // RING) % RING) * RING + (z + rel % RING) % RING

    gathered = lax.all_gather(pack(merged, tile_order, (hid % RING)[None]), "hid", axis=0, tiled=True)

    pick = (flat[:TEXT, None] == jnp.arange(REQ_GRP * LEN_MAX)[None, :]).astype(BF)
    text_rows = jnp.dot(
        pick, text_embed.reshape(REQ_GRP * LEN_MAX, FEAT), preferred_element_type=F32
    ).astype(BF)
    weight = (
        jnp.concatenate([query_weight, key_weight, value_weight], axis=1).astype(F32)
        * attn_gain.astype(F32)[:, None]
    ).astype(BF)
    partner = [(i, i ^ 1) for i in range(N_HID)]
    text_blocks, text_where = gather_far(gather_near(text_rows))
    strip = FEAT // N_REQ
    piece = cut(out_weight, (me * strip)[None].astype(jnp.int32))
    both, left = gain_and_bias(ln_gain, ln_bias)
    both, left, *text_blocks[8:] = lax.optimization_barrier((both, left, *text_blocks[8:]))
    q_text, kv_text = qkv(
        text_blocks, text_where, weight, cos[:TEXT], sin[:TEXT], sources, "qkv_text"
    )
    piece, q_text = lax.optimization_barrier((piece, q_text))
    gathered, q_text, kv_text = lax.optimization_barrier((gathered, q_text, kv_text))
    piece = lax.all_to_all(piece, "hid", split_axis=0, concat_axis=0, tiled=True)
    projected = project(
        gathered,
        proj_weight,
        both,
        left,
        proj_bias[None, :],
    )
    projected, piece = lax.optimization_barrier((projected, piece))
    tile = lax.all_to_all(
        projected.reshape(N_REQ, TILE // N_REQ, FEAT), "req", split_axis=0, concat_axis=0, tiled=True
    ).reshape(TILE, FEAT)
    other_text = lax.ppermute(kv_text, "hid", partner)
    piece, tile = lax.optimization_barrier((piece, tile))
    tile_blocks, tile_where = gather_far(gather_near(tile))
    columns = lax.all_gather(piece, "req", axis=0, tiled=False)
    q_tile, kv_tile = qkv(
        tile_blocks, tile_where, weight, cos[TEXT:], sin[TEXT:], sources, "qkv_tile"
    )
    other_tile = lax.ppermute(kv_tile, "hid", partner)

    low = (hid % 2 == 0).astype(jnp.int32)[None]
    attended = attend(
        low, q_text, q_tile, kv_text, other_text, kv_tile, other_tile, cos, sin, code
    )
    heads = lax.all_gather(attended, "hid", axis=0, tiled=True)
    hidden = finish(text_embed, tile, heads, columns, row_of[:, :, None])

    last = jnp.sum(jnp.where(slot[None, :] == lengths[:, None] - 1, row_of, 0), axis=1)
    pick_last = (last[:, None] == n[None, :]).astype(BF)
    rows_last = jnp.dot(pick_last, attended, preferred_element_type=F32).astype(BF)
    term = jnp.dot(rows_last, out_weight, preferred_element_type=F32)
    base = jnp.dot(pick_last[:, :TEXT], text_rows, preferred_element_type=F32) + jnp.dot(
        pick_last[:, TEXT:], tile, preferred_element_type=F32
    )
    spot = lax.broadcasted_iota(jnp.int32, (1, N_HID, 1), 1) == hid
    term = term + jnp.where(spot, base[:, None, :], 0.0).reshape(REQ_GRP, D)
    term = over_line(term, along_z)
    full_width = over_line(term, along_x).astype(BF)
    all_last = lax.all_gather(full_width, "req", axis=0, tiled=True)
    last_values = all_last.astype(F32)
    last_squares = jnp.sum(last_values * last_values, axis=1)
    final_norm = jnp.sqrt(last_squares)
    final_scaled = (
        last_values * lax.rsqrt(last_squares / D + 1e-05)[:, None] * final_gain.astype(F32)
    ).astype(BF)
    logits = lax.dot_general(
        final_scaled, head_weight, (((1,), (1,)), ((), ())), preferred_element_type=F32
    )
    top = jnp.max(logits, axis=1)
    for move in (along_z, along_x):
        here, below, above, far_top = line_of(top, move)
        top = jnp.maximum(jnp.maximum(here, below), jnp.maximum(above, far_top))
    logit_max = lax.pmax(top, "req")
    return (hidden, final_norm, logit_max)


def solution(mesh):
    return jax.shard_map(
        shards,
        mesh=mesh,
        in_specs=(
            P(None, "req", "hid"),
            P(),
            P(),
            P(None, "hid"),
            P("hid"),
            P("req", None, "hid"),
            P(),
            P(None, "hid"),
            P(None, "hid"),
            P(None, "hid"),
            P("hid", None),
            P(),
            P(("req", "hid"), None),
            P("req"),
            P(),
            P(),
        ),
        out_specs=(P("req", None, "hid"), P(), P()),
        check_vma=False,
    )
```
